32 devices in a mesh: gx: 2 (over core), gy: 4 (over y, x), gz: 4 (over z).
Axes of the slice: x: 2, y: 2, z: 4, core: 2. Of those that a mesh axis runs over, the one named last changes fastest.
Arguments:
- offsets: float32 [3, 8, 16, 512], P(None, 'gx', 'gy', 'gz'), may hold values from 0 to 1, as said below
- charges: float32 [8, 16, 512], P('gx', 'gy', 'gz'), may hold values from -0.3 to 0.3
- up_inverse: float32 [64, 64], replicated, may hold values from -0.75 to 0.75
- translations: bfloat16 [316, 4096], replicated, may hold values from -0.0546875 to 0.0546875
- down_inverse: float32 [64, 64], replicated, may hold values from -0.75 to 0.75
Outputs:
- potential: float32 [8, 16, 512], P('gx', 'gy', 'gz')
The draws below stay inside these ranges and needn't reach their ends.
Inputs may be any that keep to these rules, and one draw needn't show every extreme that they name: `offsets`: each leaf box is cut into a regular lattice of 32 equal cells; the box's 32 bodies lie in distinct cells, each at least 0.15 of a cell's side away from its cell's faces.
All inputs are finite; a program needn't handle non-finite values.
Results may differ from the reference program's by a relative error of at most 0.0028.
Values may be sent and summed in bfloat16 or wider, within the bound.
No kernel may reach another device: no remote copies, remote signals or barrier semaphores. Data moves between devices by JAX's collectives and lax.ppermute only.
A program may use at most 128 MiB of HBM per device.

```python
import math
import jax
import jax.numpy as jnp
import numpy as np
from jax import lax

BODIES = 32
EQ = 64
OFFSETS = 316
NX = 8
NY = 16
NZ = 16


def draw_offsets(key, part):
    log_count = BODIES.bit_length() - 1
    side_x = 2 ** ((log_count + 2) // 3)
    side_y = 2 ** ((log_count + 1) // 3)
    side_z = 2 ** (log_count // 3)
    key_order = jax.random.fold_in(key, 11)
    key_jitter = jax.random.fold_in(key, 12)
    box_shape = (NX, NY, NZ, BODIES)
    scores = jax.random.randint(key_order, box_shape, 0, 1 << 20, dtype=jnp.int32) * BODIES
    scores = scores + lax.broadcasted_iota(jnp.int32, box_shape, 3)
    ranked = jnp.argsort(scores, axis=-1).astype(jnp.int32)
    cell_x = (ranked // (side_y * side_z)).astype(jnp.float32)
    cell_y = (ranked // side_z % side_y).astype(jnp.float32)
    cell_z = (ranked % side_z).astype(jnp.float32)
    jitter = jax.random.uniform(key_jitter, (3,) + box_shape, jnp.float32)
    interior = 0.15 + 0.7 * jitter
    placed = jnp.stack([(cell_x + interior[0]) / side_x, (cell_y + interior[1]) / side_y, (cell_z + interior[2]) / side_z])
    return placed.reshape(3, NX, NY, NZ * BODIES)


def block_levels(key, extent, pieces, low, largest):
    gain, own = 1.0, jax.random.fold_in(key, 6)
    for position, blocks in pieces:
        draws = jnp.exp(jax.random.uniform(jax.random.fold_in(own, position), (blocks,), jnp.float32, low / len(pieces), largest / len(pieces)))
        gain = gain * jnp.repeat(draws, extent[position] // blocks).reshape([-1 if axis == position else 1 for axis in range(len(extent))])
    return gain


def scatter_about(rng, shape, scale, bound, pieces=(), kind=jnp.bfloat16):
    values = jax.random.normal(rng, shape, jnp.float32) * scale
    if len(pieces) > 0:
        values = block_levels(rng, shape, pieces, -0.22, 0.18) * values
    return jnp.clip(values, min=-bound, max=bound).astype(kind)


def setup_inputs(seed: int = 0) -> dict:
    key_list = jax.random.split(jax.random.key(seed), 6)
    return {
        "offsets": draw_offsets(jax.random.fold_in(key_list[5], 71), 0),
        "charges": scatter_about(key_list[1], (NX, NY, NZ * BODIES), 0.05, 0.3, ((0, 2), (1, 4), (2, 4)), jnp.float32),
        "up_inverse": scatter_about(key_list[2], (EQ, EQ), EQ ** -0.5, 0.75, (), jnp.float32),
        "translations": scatter_about(key_list[3], (OFFSETS, EQ * EQ), (189 * EQ) ** -0.5, 0.0546875),
        "down_inverse": scatter_about(key_list[4], (EQ, EQ), EQ ** -0.5, 0.75, (), jnp.float32),
    }


RADIUS = 0.9

def sphere_points(num_points):
    number = jnp.arange(num_points).astype(jnp.float32)
    height = 1.0 - (2.0 * number + 1.0) / num_points
    across = jnp.sqrt(1.0 - height * height)
    turned = number * (math.pi * (3.0 - math.sqrt(5.0)))
    return (across * jnp.cos(turned), across * jnp.sin(turned), height)

def green(delta_x, delta_y, delta_z):
    square = delta_x * delta_x + delta_y * delta_y + delta_z * delta_z
    inside = square > 0.0
    return jnp.where(inside, lax.rsqrt(jnp.where(inside, square, 1.0)), 0.0)

def table_rows(zero_row):
    listing = []
    counter = 0
    for along_x in range(-3, 4):
        for along_y in range(-3, 4):
            for along_z in range(-3, 4):
                if max(abs(along_x), abs(along_y), abs(along_z)) >= 2:
                    listing.append(counter)
                    counter += 1
                else:
                    listing.append(zero_row)
    return np.array(listing, dtype=np.int32)

def full_table(translations, points):
    padded = jnp.concatenate([translations, jnp.zeros((1, translations.shape[1]), translations.dtype)], axis=0)
    picked = jnp.take(padded, jnp.asarray(table_rows(translations.shape[0])), axis=0)
    return picked.reshape(7, 7, 7, points, points)

def unfold(source_array, along_axis, parents):
    middle = lax.slice_in_dim(source_array, 1, 1 + 2 * (parents + 2), axis=along_axis)
    old_shape = middle.shape
    paired = middle.reshape(old_shape[:along_axis] + (parents + 2, 2) + old_shape[along_axis + 1:])
    windows = [lax.slice_in_dim(paired, offset, offset + parents, axis=along_axis) for offset in range(3)]
    stacked = jnp.stack(windows, axis=along_axis + 1)
    return stacked.reshape(old_shape[:along_axis] + (parents, 6) + old_shape[along_axis + 1:])

def translate(extended, operators, parents_x, parents_y, parents_z, points):
    unfolded = unfold(unfold(unfold(extended, 0, parents_x), 2, parents_y), 4, parents_z)
    flat_rows = unfolded.transpose(0, 2, 4, 1, 3, 5, 6).reshape(parents_x * parents_y * parents_z, 216 * points)
    results = []
    for class_x in range(2):
        for class_y in range(2):
            for class_z in range(2):
                slab_table = operators[1 - class_x:7 - class_x, 1 - class_y:7 - class_y, 1 - class_z:7 - class_z]
                slab_table = slab_table.reshape(216 * points, points)
                results.append(jnp.dot(flat_rows, slab_table, preferred_element_type=jnp.float32))
    joined = jnp.stack(results).reshape(2, 2, 2, parents_x, parents_y, parents_z, points)
    return joined.transpose(3, 0, 4, 1, 5, 2, 6).reshape(2 * parents_x, 2 * parents_y, 2 * parents_z, points)

def place_bodies(offsets, start_x, start_y, start_z):
    leaves_x, leaves_y = (offsets.shape[1], offsets.shape[2])
    leaves_z = offsets.shape[3] // BODIES
    scaled = offsets.reshape(3, leaves_x, leaves_y, leaves_z, BODIES)
    box_shape = (leaves_x, leaves_y, leaves_z)
    corner_x = (lax.broadcasted_iota(jnp.int32, box_shape, 0) + start_x).astype(jnp.float32)
    corner_y = (lax.broadcasted_iota(jnp.int32, box_shape, 1) + start_y).astype(jnp.float32)
    corner_z = (lax.broadcasted_iota(jnp.int32, box_shape, 2) + start_z).astype(jnp.float32)
    body_x = corner_x[..., None] + scaled[0]
    body_y = corner_y[..., None] + scaled[1]
    body_z = corner_z[..., None] + scaled[2]
    return (body_x, body_y, body_z, corner_x + 0.5, corner_y + 0.5, corner_z + 0.5)

def upward_check(body_x, body_y, body_z, weights, centre_x, centre_y, centre_z, sphere):
    point_x = centre_x[..., None] + RADIUS * sphere[0]
    point_y = centre_y[..., None] + RADIUS * sphere[1]
    point_z = centre_z[..., None] + RADIUS * sphere[2]
    kernel = green(point_x[..., :, None] - body_x[..., None, :], point_y[..., :, None] - body_y[..., None, :], point_z[..., :, None] - body_z[..., None, :])
    return lax.optimization_barrier(jnp.sum(kernel * weights[..., None, :], axis=-1))

def evaluate_far(body_x, body_y, body_z, density, centre_x, centre_y, centre_z, sphere):
    point_x = centre_x[..., None] + RADIUS * sphere[0]
    point_y = centre_y[..., None] + RADIUS * sphere[1]
    point_z = centre_z[..., None] + RADIUS * sphere[2]
    kernel = green(body_x[..., :, None] - point_x[..., None, :], body_y[..., :, None] - point_y[..., None, :], body_z[..., :, None] - point_z[..., None, :])
    return lax.optimization_barrier(jnp.sum(kernel * density[..., None, :], axis=-1))

def pair_sum(target_x, target_y, target_z, source_x, source_y, source_z, source_q):
    kernel = green(target_x[..., :, None] - source_x[..., None, :], target_y[..., :, None] - source_y[..., None, :], target_z[..., :, None] - source_z[..., None, :])
    return lax.optimization_barrier(jnp.sum(kernel * source_q[..., None, :], axis=-1))

def reference(offsets, charges, up_inverse, translations, down_inverse):
    body_x, body_y, body_z, centre_x, centre_y, centre_z = place_bodies(offsets, 0, 0, 0)
    weights = charges.reshape(NX, NY, NZ, BODIES)
    sphere = sphere_points(EQ)
    planes = jnp.arange(NX, dtype=jnp.int32)

    def plane_of(member, plane_index):
        return lax.dynamic_slice_in_dim(member, plane_index, 1, 0)
    padded = [jnp.pad(member, ((1, 1), (1, 1), (1, 1), (0, 0))) for member in (body_x, body_y, body_z, weights)]

    def near_plane(plane_index):
        targets = [plane_of(member, plane_index) for member in (body_x, body_y, body_z)]
        result = jnp.zeros((1, NY, NZ, BODIES), jnp.float32)
        for shift_x in range(3):
            for shift_y in range(3):
                for shift_z in range(3):
                    sources = [plane_of(member, plane_index + shift_x)[:, shift_y:shift_y + NY, shift_z:shift_z + NZ] for member in padded]
                    result = result + pair_sum(targets[0], targets[1], targets[2], sources[0], sources[1], sources[2], sources[3])
        return result[0]
    near_part = lax.map(near_plane, planes)

    def check_plane(plane_index):
        return upward_check(plane_of(body_x, plane_index), plane_of(body_y, plane_index), plane_of(body_z, plane_index), plane_of(weights, plane_index), plane_of(centre_x, plane_index), plane_of(centre_y, plane_index), plane_of(centre_z, plane_index), sphere)[0]
    up_check = lax.map(check_plane, planes)
    up_density = jnp.dot(up_check.reshape(NX * NY * NZ, EQ), up_inverse, precision=lax.Precision.HIGHEST, preferred_element_type=jnp.float32).astype(jnp.bfloat16).reshape(NX, NY, NZ, EQ)
    operators = full_table(translations, EQ)
    padded_density = jnp.pad(up_density, ((3, 3), (3, 3), (3, 3), (0, 0)))

    def parent_slab(parent_index):
        slab_piece = lax.dynamic_slice_in_dim(padded_density, 2 * parent_index, 8, 0)
        return translate(slab_piece, operators, 1, NY // 2, NZ // 2, EQ)
    down_check = lax.map(parent_slab, jnp.arange(NX // 2, dtype=jnp.int32)).reshape(NX, NY, NZ, EQ)
    down_density = jnp.dot(down_check.reshape(NX * NY * NZ, EQ), down_inverse, precision=lax.Precision.HIGHEST, preferred_element_type=jnp.float32).reshape(NX, NY, NZ, EQ)

    def far_plane(plane_index):
        return evaluate_far(plane_of(body_x, plane_index), plane_of(body_y, plane_index), plane_of(body_z, plane_index), plane_of(down_density, plane_index), plane_of(centre_x, plane_index), plane_of(centre_y, plane_index), plane_of(centre_z, plane_index), sphere)[0]
    far_part = lax.map(far_plane, planes)
    return (near_part + far_part).reshape(NX, NY, NZ * BODIES)
```

```python
import functools
import math

import jax
import jax.numpy as jnp
import numpy as np
from jax import lax
from jax.experimental import pallas as pl
from jax.experimental.pallas import tpu as pltpu
from jax.sharding import PartitionSpec as P

BODIES = 32
RADIUS = 0.9
REACH = 3
SPAN = 2 * REACH + 1
F32 = jnp.float32
BF16 = jnp.bfloat16
NT = (((1,), (1,)), ((), ()))


def surface(points):
    number = np.arange(points).astype(np.float32)
    height = np.float32(1.0) - (np.float32(2.0) * number + np.float32(1.0)) / np.float32(points)
    across = np.sqrt(np.float32(1.0) - height * height)
    turned = number * np.float32(math.pi * (3.0 - math.sqrt(5.0)))
    columns = np.zeros((points, 128), np.float32)
    columns[:, 0] = RADIUS * across * np.cos(turned)
    columns[:, 1] = RADIUS * across * np.sin(turned)
    columns[:, 2] = RADIUS * height
    return columns


def numbering():
    table, count = {}, 0
    for ox in range(-REACH, REACH + 1):
        for oy in range(-REACH, REACH + 1):
            for oz in range(-REACH, REACH + 1):
                if max(abs(ox), abs(oy), abs(oz)) >= 2:
                    table[ox, oy, oz] = count
                    count += 1
    return table


def split(value):
    high = value.astype(BF16)
    return high, (value - high.astype(F32)).astype(BF16)


def surface_green(sphere, offs_ref, x, y):
    rows = [offs_ref[c, x, pl.ds(y, 1), :] - 0.5 for c in range(3)]
    square = None
    for c in range(3):
        delta = sphere[:, c : c + 1] - rows[c]
        square = delta * delta if square is None else square + delta * delta
    return lax.rsqrt(square)


def upward_kernel(offs_ref, q_ref, sphere_ref, uinv_ref, shuffle_ref, u_ref, check_ref, wide_ref):
    _, lx, ly, lanes = offs_ref.shape
    lz = lanes // BODIES
    points = uinv_ref.shape[0]
    sphere = sphere_ref[...]
    segment = (
        lax.broadcasted_iota(jnp.int32, (8, lanes), 1) // BODIES
        == lax.broadcasted_iota(jnp.int32, (8, lanes), 0)
    ).astype(BF16)
    wide_ref[...] = jnp.zeros_like(wide_ref)
    wide_ref[:points, :points] = uinv_ref[...]
    wide_ref[points:, points:] = uinv_ref[...]
    for x in range(lx):
        for pair in range(ly // 2):
            parts = [
                surface_green(sphere, offs_ref, x, 2 * pair + par) * q_ref[x, pl.ds(2 * pair + par, 1), :]
                for par in range(2)
            ]
            high, low = split(jnp.concatenate(parts, axis=0))
            sums = lax.dot_general(segment, high, NT, preferred_element_type=F32)
            sums = sums + lax.dot_general(segment, low, NT, preferred_element_type=F32)
            check_ref[pl.ds((x * (ly // 2) + pair) * lz, lz), :] = sums[:lz]
    density = jnp.dot(
        check_ref[...], wide_ref[...], precision=lax.Precision.HIGHEST, preferred_element_type=F32
    ).astype(BF16)
    u_ref[...] = jnp.dot(density, shuffle_ref[...], preferred_element_type=F32)


def table_kernel(t_ref, w_ref, rows_ref):
    count, width = t_ref.shape
    groups = width // 128
    stride = rows_ref.shape[0] // groups
    points = math.isqrt(width)
    half = points // 2
    order = numbering()
    for a in range(groups):
        rows_ref[pl.ds(a * stride, count), :] = t_ref[:, a * 128 : (a + 1) * 128].astype(F32)
    left = lax.broadcasted_iota(jnp.int32, (groups, 128), 1) < points
    zero = jnp.zeros((groups, 128), F32)
    for ox in range(SPAN):
        for oy in range(SPAN):
            for k in range((SPAN + 1) // 2):
                loaded = []
                for oz in (2 * k, 2 * k + 1):
                    at = order.get((ox - REACH, oy - REACH, oz - REACH))
                    loaded.append(zero if at is None else rows_ref[pl.ds(at, groups, stride=stride), :])
                one, two = loaded
                even = jnp.where(left, one, pltpu.roll(two, points, 1))
                odd = jnp.where(left, pltpu.roll(one, points, 1), two)
                at = slice(k * 128, (k + 1) * 128)
                w_ref[ox, pl.ds(oy * points, half), at] = even.astype(BF16)
                w_ref[ox, pl.ds(oy * points + half, half), at] = odd.astype(BF16)


def final_kernel(
    offs_ref, u_ref, w_ref, dinv_ref, sphere_ref, body_ref, out_ref, left_ref, acc_ref, dense_ref, win_ref, sum_ref
):
    _, lx, ly, lanes = offs_ref.shape
    lz = lanes // BODIES
    points = dinv_ref.shape[0]
    ext_x, pairs, ext_z, _ = u_ref.shape
    half = ly // 2
    block = half * ext_z
    width = (SPAN - 1) * points
    for x in range(ext_x):
        for j in range(SPAN // 2):
            left_ref[pl.ds(x * block, block), j * 128 : (j + 1) * 128] = (
                u_ref[x, j : j + half].reshape(block, 128).astype(BF16)
            )
    wide = jnp.concatenate([dinv_ref[...]] * 2, axis=0)
    expand = (
        lax.broadcasted_iota(jnp.int32, (lx * half * lz, lx * half * lanes), 1) // BODIES
        == lax.broadcasted_iota(jnp.int32, (lx * half * lz, lx * half * lanes), 0)
    ).astype(BF16)
    lane = lax.broadcasted_iota(jnp.int32, (lz, 128), 1)
    level = lax.broadcasted_iota(jnp.int32, (lz, 128), 0)
    for cy in range(2):
        total = [None] * lx
        for ox in range(-REACH, REACH + 1):
            chosen = [b for b in range(lx) if not (ox == -REACH and b % 2 == 0) and not (ox == REACH and b % 2 == 1)]
            parts = [left_ref[pl.ds((b + ox + 2) * block, block), :] for b in chosen]
            lhs = jnp.concatenate(parts, axis=0)
            rhs = w_ref[ox + REACH, pl.ds((1 - cy) * points, width), :]
            got = jnp.dot(lhs, rhs, preferred_element_type=F32)
            for n, b in enumerate(chosen):
                piece = got[n * block : (n + 1) * block]
                total[b] = piece if total[b] is None else total[b] + piece
        for b in range(lx):
            for p in range(half):
                acc_ref[b * half + p, pl.ds(8, ext_z), :] = total[b][p * ext_z : (p + 1) * ext_z]
        for g in range(lx * half):
            folded = None
            for k in range((SPAN + 1) // 2):
                shown = []
                for oz in (2 * k - REACH, 2 * k + 1 - REACH):
                    if oz > REACH:
                        shown.append(jnp.zeros((lz, 128), F32))
                        continue
                    got = acc_ref[g, pl.ds(8 + oz + 2, lz), k * 128 : (k + 1) * 128]
                    if oz == -REACH:
                        got = jnp.where(level % 2 == 1, got, 0.0)
                    if oz == REACH:
                        got = jnp.where(level % 2 == 0, got, 0.0)
                    shown.append(got)
                both = jnp.where(lane < points, shown[0], shown[1])
                folded = both if folded is None else folded + both
            sum_ref[pl.ds(g * lz, lz), :] = folded
        dense = jnp.dot(sum_ref[...], wide, precision=lax.Precision.HIGHEST, preferred_element_type=F32)
        high, low = split(dense.T)
        spread = jnp.dot(high, expand, preferred_element_type=F32)
        spread = spread + jnp.dot(low, expand, preferred_element_type=F32)
        for g in range(lx * half):
            dense_ref[g, cy] = spread[:, g * lanes : (g + 1) * lanes]

    rows = (lx + 2) * (ly + 2)
    place = lax.broadcasted_iota(jnp.int32, (rows, 128), 0)
    spot = lax.broadcasted_iota(jnp.int32, (rows, 128), 1) // BODIES
    base = [place // (ly + 2) - 1, place % (ly + 2) - 1, None]
    for w in range(2):
        for c in range(3):
            at = base[c] if c < 2 else spot - 1 + 2 * w
            win_ref[w * 3 + c] = body_ref[w, c] + at.astype(F32)
        for s in range(2):
            fit = (spot >= s) & (spot < s + 3)
            win_ref[6 + w * 2 + s] = jnp.where(fit, body_ref[w, 3], 0.0)

    sphere = sphere_ref[...]
    ones = jnp.ones((8, 128), BF16)

    def plane(x, carry):
        lead = lax.broadcasted_iota(jnp.int32, (ly, lanes), 0)
        spots = lax.broadcasted_iota(jnp.int32, (ly, lanes), 1) // BODIES
        places = [offs_ref[0, x] + x.astype(F32), offs_ref[1, x] + lead.astype(F32), offs_ref[2, x] + spots.astype(F32)]
        turned = jnp.concatenate(places + [places[0]] * (4 - 3), axis=0).T
        for y in range(ly):
            gathered = []
            for z in range(lz):
                w, s = z // 2, z % 2
                target = [turned[z * BODIES : (z + 1) * BODIES, c * ly + y : c * ly + y + 1] for c in range(3)]
                total = None
                for dx in range(3):
                    for dy in range(3):
                        r = (x + dx) * (ly + 2) + y + dy
                        square = None
                        for c in range(3):
                            delta = target[c] - win_ref[w * 3 + c, pl.ds(r, 1), :]
                            square = delta * delta if square is None else square + delta * delta
                        inverse = lax.rsqrt(square)
                        if dx == 1 and dy == 1:
                            inverse = jnp.where(square > 0.0, inverse, 0.0)
                        term = inverse * win_ref[6 + w * 2 + s, pl.ds(r, 1), :]
                        total = term if total is None else total + term
                gathered.append(total)
            high, low = split(jnp.concatenate(gathered, axis=0))
            near = lax.dot_general(ones, high, NT, preferred_element_type=F32)
            near = near + lax.dot_general(ones, low, NT, preferred_element_type=F32)
            kernel = surface_green(sphere, offs_ref, x, y)
            far = jnp.sum(kernel * dense_ref[x * half + y // 2, y % 2], axis=0, keepdims=True)
            out_ref[x, pl.ds(y, 1), :] = near[:1] + far
        return carry

    lax.fori_loop(0, lx, plane, 0)


def swap(low, high, axis):
    count = lax.axis_size(axis)
    even = lax.axis_index(axis) % 2 == 0
    first = [(i, i + 1) for i in range(0, count - 1, 2)]
    second = [(i, i + 1) for i in range(1, count - 1, 2)]

    def both(pairs):
        return [pair for i, j in pairs for pair in ((i, j), (j, i))]

    one = lax.ppermute(jnp.where(even, high, low), axis, both(first))
    if not second:
        two = jnp.zeros_like(one)
    else:
        two = lax.ppermute(jnp.where(even, low, high), axis, both(second))
    return jnp.where(even, two, one), jnp.where(even, one, two)


def vmem():
    return pl.BlockSpec(memory_space=pltpu.VMEM)


def per_device(offsets, charges, up_inverse, translations, down_inverse):
    points = up_inverse.shape[0]
    _, lx, ly, lanes = offsets.shape
    lz = lanes // BODIES
    half = ly // 2
    sphere = jnp.asarray(surface(points))
    source = np.concatenate([np.arange(0, points, 2), np.arange(1, points, 2)])
    shuffle = np.zeros((2 * points, 2 * points), np.float32)
    for par in range(2):
        shuffle[par * points + source, par * points + np.arange(points)] = 1.0
    density = pl.pallas_call(
        upward_kernel,
        out_shape=jax.ShapeDtypeStruct((lx * half * lz, 2 * points), F32),
        in_specs=[vmem()] * 5,
        out_specs=vmem(),
        scratch_shapes=[pltpu.VMEM((lx * half * lz, 2 * points), F32), pltpu.VMEM((2 * points, 2 * points), F32)],
        name="upward",
    )(offsets, charges, sphere, up_inverse, jnp.asarray(shuffle, BF16))
    count, width = translations.shape
    stride = (count + 7) // 8 * 8
    weights = pl.pallas_call(
        table_kernel,
        out_shape=jax.ShapeDtypeStruct((SPAN, SPAN * points, (SPAN + 1) * points), BF16),
        in_specs=[vmem()],
        out_specs=vmem(),
        scratch_shapes=[pltpu.VMEM((width // 128 * stride, 128), F32)],
        compiler_params=pltpu.CompilerParams(vmem_limit_bytes=20 << 20),
        name="table",
    )(translations)

    dense = density.reshape(lx, half, lz, 2 * points)
    body = jnp.concatenate([offsets, charges[None]], axis=0)

    def pack(one, two):
        return jnp.concatenate([one.reshape(-1, 128), two.reshape(-1, 128)], axis=0)

    def unpack(packet, one, two):
        cut = math.prod(one) // 128
        return packet[:cut].reshape(one), packet[cut:].reshape(two)

    size = (lx, 1, lz, 2 * points), (4, lx, 1, lanes)
    below, above = swap(pack(dense[:, :1], body[:, :, :1]), pack(dense[:, -1:], body[:, :, -1:]), "gy")
    below, above = unpack(below, *size), unpack(above, *size)
    dense = jnp.concatenate([below[0], dense, above[0]], axis=1)
    body = jnp.concatenate([below[1], body, above[1]], axis=2)
    size = (lx, half + 2, 2, 2 * points), (4, lx, ly + 2, BODIES)
    below, above = swap(
        pack(dense[:, :, :2], body[..., :BODIES]), pack(dense[:, :, -2:], body[..., -BODIES:]), "gz"
    )
    below, above = unpack(below, *size), unpack(above, *size)
    dense = jnp.concatenate([below[0], dense, above[0]], axis=2)
    body = jnp.concatenate([below[1], body, above[1]], axis=3)
    size = (2, half + 2, lz + 4, 2 * points), (4, 1, ly + 2, lanes + 2 * BODIES)
    below, above = swap(pack(dense[:2], body[:, :1]), pack(dense[-2:], body[:, -1:]), "gx")
    below, above = unpack(below, *size), unpack(above, *size)
    dense = jnp.concatenate([below[0], dense, above[0]], axis=0)
    body = jnp.concatenate([below[1], body, above[1]], axis=1)
    rows = (lx + 2) * (ly + 2)
    body = jnp.stack([body[..., :lanes], body[..., 2 * BODIES :]]).reshape(2, 4, rows, lanes)

    ext = (lx + 4) * half * (lz + 4)
    return pl.pallas_call(
        final_kernel,
        out_shape=jax.ShapeDtypeStruct((lx, ly, lanes), F32),
        in_specs=[vmem()] * 6,
        out_specs=vmem(),
        scratch_shapes=[
            pltpu.VMEM((ext, 6 * points), BF16),
            pltpu.VMEM((lx * half, 8 + lz + 4 + 8, (SPAN + 1) * points), F32),
            pltpu.VMEM((lx * half, 2, points, lanes), F32),
            pltpu.VMEM((10, rows, lanes), F32),
            pltpu.VMEM((lx * half * lz, 2 * points), F32),
        ],
        compiler_params=pltpu.CompilerParams(vmem_limit_bytes=30 << 20),
        name="final",
    )(offsets, dense, weights, down_inverse, sphere, body)


def solution(mesh):
    in_specs = (P(None, "gx", "gy", "gz"), P("gx", "gy", "gz"), P(), P(), P())
    out_specs = P("gx", "gy", "gz")
    return jax.shard_map(
        per_device, mesh=mesh, in_specs=in_specs, out_specs=out_specs, check_vma=False
    )
```

```python
import functools
import math

import jax
import jax.numpy as jnp
import numpy as np
from jax import lax
from jax.experimental import pallas as pl
from jax.experimental.pallas import tpu as pltpu
from jax.sharding import PartitionSpec as P

BODIES = 32
RADIUS = 0.9
REACH = 3
SPAN = 2 * REACH + 1
F32 = jnp.float32
BF16 = jnp.bfloat16
NT = (((1,), (1,)), ((), ()))


def surface(points):
    number = np.arange(points).astype(np.float32)
    height = np.float32(1.0) - (np.float32(2.0) * number + np.float32(1.0)) / np.float32(points)
    across = np.sqrt(np.float32(1.0) - height * height)
    turned = number * np.float32(math.pi * (3.0 - math.sqrt(5.0)))
    columns = np.zeros((points, 128), np.float32)
    columns[:, 0] = RADIUS * across * np.cos(turned)
    columns[:, 1] = RADIUS * across * np.sin(turned)
    columns[:, 2] = RADIUS * height
    return columns


def numbering():
    table, count = {}, 0
    for ox in range(-REACH, REACH + 1):
        for oy in range(-REACH, REACH + 1):
            for oz in range(-REACH, REACH + 1):
                if max(abs(ox), abs(oy), abs(oz)) >= 2:
                    table[ox, oy, oz] = count
                    count += 1
    return table


def split(value):
    high = value.astype(BF16)
    return high, (value - high.astype(F32)).astype(BF16)


def surface_green(sphere, offs_ref, x, y):
    rows = [offs_ref[c, x, pl.ds(y, 1), :] - 0.5 for c in range(3)]
    square = None
    for c in range(3):
        delta = sphere[:, c : c + 1] - rows[c]
        square = delta * delta if square is None else square + delta * delta
    return lax.rsqrt(square)


def select(even, one, two):
    return jnp.where(even, one, two), jnp.where(even, two, one)


def put(refs, at, even, low, high):
    refs[0][at, :] = jnp.where(even, high, low)
    for ref in refs[1:]:
        ref[at, :] = jnp.where(even, low, high)


def get(refs, even):
    one = refs[0][...]
    return select(even, one, refs[1][...] if len(refs) > 1 else jnp.zeros_like(one))


def upward_kernel(offs_hbm, q_hbm, sphere_hbm, uinv_hbm, u_ref, *rest):
    *packets, offs_ref, q_ref, sphere_ref, uinv_ref, check_ref, wide_ref, sems = rest
    copies = [
        pltpu.make_async_copy(source, target, sems.at[n])
        for n, (source, target) in enumerate(
            ((offs_hbm, offs_ref), (q_hbm, q_ref), (sphere_hbm, sphere_ref), (uinv_hbm, uinv_ref))
        )
    ]
    for copy in copies:
        copy.start()
    _, lx, ly, lanes = offs_ref.shape
    lz = lanes // BODIES
    half = ly // 2
    points = uinv_ref.shape[0]
    even = lax.axis_index("gy") % 2 == 0
    segment = (
        lax.broadcasted_iota(jnp.int32, (8, lanes), 1) // BODIES
        == lax.broadcasted_iota(jnp.int32, (8, lanes), 0)
    ).astype(BF16)
    wide_ref[...] = jnp.zeros_like(wide_ref)
    column = lax.broadcasted_iota(jnp.int32, (2 * points, 2 * points), 1)
    within = column % points
    wanted = column - within + jnp.where(within < points // 2, 2 * within, 2 * within - points + 1)
    shuffle = (lax.broadcasted_iota(jnp.int32, (2 * points, 2 * points), 0) == wanted).astype(BF16)
    for copy in copies[:3]:
        copy.wait()
    sphere = sphere_ref[...]
    for c in range(4):
        for x in range(lx):
            low, high = [
                offs_ref[c, x, pl.ds(y, 1), :] if c < 3 else q_ref[x, pl.ds(y, 1), :] for y in (0, ly - 1)
            ]
            put(packets, pl.ds(lx * lz + c * lx + x, 1), even, low, high)
    for x in range(lx):
        for pair in range(half):
            parts = [
                surface_green(sphere, offs_ref, x, 2 * pair + par) * q_ref[x, pl.ds(2 * pair + par, 1), :]
                for par in range(2)
            ]
            high, low = split(jnp.concatenate(parts, axis=0))
            sums = lax.dot_general(segment, high, NT, preferred_element_type=F32)
            sums = sums + lax.dot_general(segment, low, NT, preferred_element_type=F32)
            check_ref[pl.ds((x * half + pair) * lz, lz), :] = sums[:lz]
    copies[3].wait()
    wide_ref[:points, :points] = uinv_ref[...]
    wide_ref[points:, points:] = uinv_ref[...]
    density = jnp.dot(
        check_ref[...], wide_ref[...], precision=lax.Precision.HIGHEST, preferred_element_type=F32
    ).astype(BF16)
    u_ref[...] = jnp.dot(density, shuffle, preferred_element_type=F32)
    for x in range(lx):
        low = u_ref[pl.ds(x * half * lz, lz), :]
        high = u_ref[pl.ds((x * half + half - 1) * lz, lz), :]
        put(packets, pl.ds(x * lz, lz), even, low, high)


def table_kernel(t_ref, after_ref, w_ref, rows_ref):
    count, width = t_ref.shape
    groups = width // 128
    stride = rows_ref.shape[0] // groups
    points = math.isqrt(width)
    half = points // 2
    order = numbering()
    for a in range(groups):
        rows_ref[pl.ds(a * stride, count), :] = t_ref[:, a * 128 : (a + 1) * 128].astype(F32)
    left = lax.broadcasted_iota(jnp.int32, (groups, 128), 1) < points
    zero = jnp.zeros((groups, 128), F32)
    for ox in range(SPAN):
        for oy in range(SPAN):
            for k in range((SPAN + 1) // 2):
                loaded = []
                for oz in (2 * k, 2 * k + 1):
                    at = order.get((ox - REACH, oy - REACH, oz - REACH))
                    loaded.append(zero if at is None else rows_ref[pl.ds(at, groups, stride=stride), :])
                one, two = loaded
                even = jnp.where(left, one, pltpu.roll(two, points, 1))
                odd = jnp.where(left, pltpu.roll(one, points, 1), two)
                at = slice(k * 128, (k + 1) * 128)
                w_ref[ox, pl.ds(oy * points, half), at] = even.astype(BF16)
                w_ref[ox, pl.ds(oy * points + half, half), at] = odd.astype(BF16)


def zpack_kernel(count, offs_ref, q_ref, u_ref, *rest):
    received, (d_ref, r_ref, *packets) = rest[:count], rest[count:]
    _, lx, ly, lanes = offs_ref.shape
    lz = lanes // BODIES
    half = ly // 2
    wide = ly + 2
    above, below = get(received, lax.axis_index("gy") % 2 == 0)
    even = lax.axis_index("gz") % 2 == 0
    for x in range(lx):
        at = x * (half + 2) * lz
        d_ref[pl.ds(at, lz), :] = below[x * lz : (x + 1) * lz]
        d_ref[pl.ds(at + lz, half * lz), :] = u_ref[pl.ds(x * half * lz, half * lz), :]
        d_ref[pl.ds(at + (half + 1) * lz, lz), :] = above[x * lz : (x + 1) * lz]
        for c in range(4):
            row = lx * lz + c * lx + x
            r_ref[c, pl.ds(x * wide, 1), :] = below[row : row + 1]
            r_ref[c, pl.ds(x * wide + 1, ly), :] = offs_ref[c, x] if c < 3 else q_ref[x]
            r_ref[c, pl.ds(x * wide + ly + 1, 1), :] = above[row : row + 1]
    for g in range(lx * (half + 2)):
        put(packets, pl.ds(g * 2, 2), even, d_ref[pl.ds(g * lz, 2), :], d_ref[pl.ds(g * lz + lz - 2, 2), :])
    spot = lax.broadcasted_iota(jnp.int32, (lx, lanes), 1) // BODIES
    base = lx * (half + 2) * 2
    for c in range(4):
        rows = [r_ref[c, pl.ds(j, lx, stride=wide), :] for j in range(wide)]
        for pack in range(half):
            low = high = None
            for j in range(4):
                row = rows[2 * pack + j]
                first = pltpu.roll(row, j * BODIES, 1) if j else row
                last = pltpu.roll(row, (j + 1) % 4 * BODIES, 1) if (j + 1) % 4 else row
                low = first if low is None else jnp.where(spot == j, first, low)
                high = last if high is None else jnp.where(spot == j, last, high)
            put(packets, pl.ds(base + (c * half + pack) * lx, lx), even, low, high)


def xpack_kernel(count, d_ref, r_ref, *rest):
    received, (e_ref, zl_ref, zh_ref, *packets) = rest[:count], rest[count:]
    groups = e_ref.shape[0]
    lx = zl_ref.shape[1] // 2
    pairs = groups // lx
    half = pairs - 2
    wide = 2 * half + 2
    lz = d_ref.shape[0] // groups
    above, below = get(received, lax.axis_index("gz") % 2 == 0)
    even = lax.axis_index("gx") % 2 == 0
    for g in range(groups):
        e_ref[g, pl.ds(0, 2), :] = below[g * 2 : g * 2 + 2]
        e_ref[g, pl.ds(2, lz), :] = d_ref[pl.ds(g * lz, lz), :]
        e_ref[g, pl.ds(2 + lz, 2), :] = above[g * 2 : g * 2 + 2]
    base = groups * 2
    for c in range(4):
        zl_ref[c] = below[base + c * half * lx : base + (c + 1) * half * lx]
        zh_ref[c] = above[base + c * half * lx : base + (c + 1) * half * lx]
    deep = lz + 4
    for n in range(2 * pairs):
        put(packets, pl.ds(n * deep, deep), even, e_ref[n], e_ref[groups - 2 * pairs + n])
    base = 2 * pairs * deep
    for c in range(4):
        low, high = r_ref[c, pl.ds(0, wide), :], r_ref[c, pl.ds((lx - 1) * wide, wide), :]
        put(packets, pl.ds(base + c * wide, wide), even, low, high)
    base = base + 4 * wide
    for end, ref in enumerate((zl_ref, zh_ref)):
        for c in range(4):
            for pack in range(half):
                low, high = ref[c, pl.ds(pack * lx, 1), :], ref[c, pl.ds(pack * lx + lx - 1, 1), :]
                put(packets, pl.ds(base + (end * 4 + c) * half + pack, 1), even, low, high)


def turn(offs_ref, x):
    _, _, ly, lanes = offs_ref.shape
    lead = lax.broadcasted_iota(jnp.int32, (ly, lanes), 0).astype(F32)
    spots = (lax.broadcasted_iota(jnp.int32, (ly, lanes), 1) // BODIES).astype(F32)
    places = [offs_ref[0, x] + float(x), offs_ref[1, x] + lead, offs_ref[2, x] + spots]
    return jnp.concatenate(places + [places[0]], axis=0).T


def pick(turned, ly, y, z):
    return [turned[z * BODIES : (z + 1) * BODIES, c * ly + y : c * ly + y + 1] for c in range(3)]


def attract(total, target, source, weight, own=False):
    square = None
    for t, s in zip(target, source):
        delta = t - s
        square = delta * delta if square is None else square + delta * delta
    inverse = lax.rsqrt(square)
    if own:
        inverse = jnp.where(square > 0.0, inverse, 0.0)
    term = inverse * weight
    return term if total is None else total + term


def lane_sum(ones, parts):
    high, low = split(jnp.concatenate(parts, axis=0))
    out = lax.dot_general(ones, high, NT, preferred_element_type=F32)
    return (out + lax.dot_general(ones, low, NT, preferred_element_type=F32))[:1]


def spans(value, spot, lz):
    return [jnp.where((spot >= z - 1) & (spot <= z + 1), value, 0.0) for z in range(lz)]


def gather(out_ref, n, y, turned, lz, rows):
    _, ly, lanes = out_ref.shape
    ones = jnp.ones((8, lanes), BF16)
    parts = []
    for z in range(lz):
        target = pick(turned, ly, y, z)
        total = None
        for source, weight, own in rows(z):
            total = attract(total, target, source, weight, own)
        parts.append(jnp.zeros((BODIES, lanes), F32) if total is None else total)
    out_ref[n, pl.ds(y, 1), :] = lane_sum(ones, parts)


def row_source(ref, at, z, own=False):
    return [ref[c, at, :] for c in range(3)], ref[3 + z, at, :], own


def edge_kernel(offs_ref, q_ref, out_ref, win_ref):
    _, lx, ly, lanes = offs_ref.shape
    lz = lanes // BODIES
    spot = lax.broadcasted_iota(jnp.int32, (ly, lanes), 1) // BODIES
    lead = lax.broadcasted_iota(jnp.int32, (ly, lanes), 0)
    for x in range(lx):
        at = pl.ds(x * ly, ly)
        shift = [float(x), lead.astype(F32), spot.astype(F32)]
        for c in range(3):
            win_ref[c, at, :] = offs_ref[c, x] + shift[c]
        for z, value in enumerate(spans(q_ref[x], spot, lz)):
            win_ref[3 + z, at, :] = value
    for n, x in enumerate((0, lx - 1)):
        turned = turn(offs_ref, x)
        for y in range(ly):

            def rows(z):
                for xx in range(max(x - 1, 0), min(x + 2, lx)):
                    for yy in range(max(y - 1, 0), min(y + 2, ly)):
                        yield row_source(win_ref, pl.ds(xx * ly + yy, 1), z, xx == x and yy == y)

            gather(out_ref, n, y, turned, lz, rows)


def strips(r_ref, win_ref, wide, lz):
    _, rows, lanes = r_ref.shape
    place = lax.broadcasted_iota(jnp.int32, (rows, lanes), 0)
    spot = lax.broadcasted_iota(jnp.int32, (rows, lanes), 1) // BODIES
    base = [place // wide, place % wide - 1, spot]
    for c in range(3):
        win_ref[c] = r_ref[c] + base[c].astype(F32)
    for z, value in enumerate(spans(r_ref[3], spot, lz)):
        win_ref[3 + z] = value


def inner_kernel(offs_ref, r_ref, out_ref, win_ref):
    _, lx, ly, lanes = offs_ref.shape
    lz = lanes // BODIES
    wide = ly + 2
    strips(r_ref, win_ref, wide, lz)
    for x in range(1, lx - 1):
        turned = turn(offs_ref, x)
        for y in range(ly):

            def rows(z):
                for xx in range(x - 1, x + 2):
                    for dy in range(3):
                        yield row_source(win_ref, pl.ds(xx * wide + y + dy, 1), z, xx == x and dy == 1)

            gather(out_ref, x - 1, y, turned, lz, rows)


def ends_kernel(offs_ref, r_ref, zl_ref, zh_ref, out_ref, win_ref, end_ref):
    _, lx, ly, lanes = offs_ref.shape
    lz = lanes // BODIES
    half = ly // 2
    wide = ly + 2
    strips(r_ref, win_ref, wide, lz)
    end_windows(zl_ref, -1.0, end_ref, 0, lz, half)
    end_windows(zh_ref, float(lz), end_ref, 5, lz, half)
    for x in range(lx):
        turned = turn(offs_ref, x)
        for y in range(ly):

            def rows(z):
                nearby = range(max(x - 1, 0), min(x + 2, lx))
                if x in (0, lx - 1):
                    for yy in (y, y + 2):
                        if yy in (0, ly + 1):
                            for xx in nearby:
                                yield row_source(win_ref, pl.ds(xx * wide + yy, 1), z)
                for end in range(2):
                    if z == (0 if end == 0 else lz - 1):
                        for xx in nearby:
                            at = pl.ds(y // 2 * lx + xx, 1)
                            source = [end_ref[end * 5 + c, at, :] for c in range(3)]
                            yield source, end_ref[end * 5 + 3 + y % 2, at, :], False

            gather(out_ref, x, y, turned, lz, rows)


def end_windows(end_ref, base, win_ref, at, lz, half):
    rows = end_ref.shape[1]
    lanes = end_ref.shape[2]
    count = rows // half
    place = lax.broadcasted_iota(jnp.int32, (rows, lanes), 0)
    spot = lax.broadcasted_iota(jnp.int32, (rows, lanes), 1) // BODIES
    shift = [(place % count).astype(F32), (spot + 2 * (place // count) - 1).astype(F32), base]
    for c in range(3):
        win_ref[at + c] = end_ref[c] + shift[c]
    for s in range(2):
        win_ref[at + 3 + s] = jnp.where((spot >= s) & (spot < s + 3), end_ref[3], 0.0)


def final_kernel(count, offs_ref, e_ref, near_edge_ref, near_in_ref, near_end_ref, w_ref, dinv_ref, sphere_ref, *rest):
    received, rest = rest[:count], rest[count:]
    out_ref, left_ref, acc_ref, dense_ref, sum_ref, side_ref, edge_ref = rest
    _, lx, ly, lanes = offs_ref.shape
    lz = lanes // BODIES
    points = dinv_ref.shape[0]
    half = ly // 2
    pairs = half + 2
    wide = ly + 2
    deep = lz + 4
    block = half * deep
    width = (SPAN - 1) * points
    above, below = get(received, lax.axis_index("gx") % 2 == 0)

    def plane(x, pair):
        if x < 2:
            return below[(x * pairs + pair) * deep : (x * pairs + pair + 1) * deep]
        if x < lx + 2:
            return e_ref[(x - 2) * pairs + pair]
        return above[((x - lx - 2) * pairs + pair) * deep : ((x - lx - 2) * pairs + pair + 1) * deep]

    for x in range(lx + 4):
        planes = [plane(x, pair) for pair in range(pairs)]
        for j in range(SPAN // 2):
            left_ref[pl.ds(x * block, block), j * 128 : (j + 1) * 128] = jnp.concatenate(
                planes[j : j + half], axis=0
            ).astype(BF16)
    twice = jnp.concatenate([dinv_ref[...]] * 2, axis=0)
    expand = (
        lax.broadcasted_iota(jnp.int32, (lx * half * lz, lx * half * lanes), 1) // BODIES
        == lax.broadcasted_iota(jnp.int32, (lx * half * lz, lx * half * lanes), 0)
    ).astype(BF16)
    lane = lax.broadcasted_iota(jnp.int32, (lz, 128), 1)
    level = lax.broadcasted_iota(jnp.int32, (lz, 128), 0)
    for cy in range(2):
        total = [None] * lx
        for ox in range(-REACH, REACH + 1):
            chosen = [b for b in range(lx) if not (ox == -REACH and b % 2 == 0) and not (ox == REACH and b % 2 == 1)]
            parts = [left_ref[pl.ds((b + ox + 2) * block, block), :] for b in chosen]
            lhs = jnp.concatenate(parts, axis=0)
            rhs = w_ref[ox + REACH, pl.ds((1 - cy) * points, width), :]
            got = jnp.dot(lhs, rhs, preferred_element_type=F32)
            for n, b in enumerate(chosen):
                piece = got[n * block : (n + 1) * block]
                total[b] = piece if total[b] is None else total[b] + piece
        for b in range(lx):
            for p in range(half):
                acc_ref[b * half + p, pl.ds(8, deep), :] = total[b][p * deep : (p + 1) * deep]
        for g in range(lx * half):
            folded = None
            for k in range((SPAN + 1) // 2):
                shown = []
                for oz in (2 * k - REACH, 2 * k + 1 - REACH):
                    if oz > REACH:
                        shown.append(jnp.zeros((lz, 128), F32))
                        continue
                    got = acc_ref[g, pl.ds(8 + oz + 2, lz), k * 128 : (k + 1) * 128]
                    if oz == -REACH:
                        got = jnp.where(level % 2 == 1, got, 0.0)
                    if oz == REACH:
                        got = jnp.where(level % 2 == 0, got, 0.0)
                    shown.append(got)
                both = jnp.where(lane < points, shown[0], shown[1])
                folded = both if folded is None else folded + both
            sum_ref[pl.ds(g * lz, lz), :] = folded
        dense = jnp.dot(sum_ref[...], twice, precision=lax.Precision.HIGHEST, preferred_element_type=F32)
        high, low = split(dense.T)
        spread = jnp.dot(high, expand, preferred_element_type=F32)
        spread = spread + jnp.dot(low, expand, preferred_element_type=F32)
        for g in range(lx * half):
            dense_ref[g, cy] = spread[:, g * lanes : (g + 1) * lanes]

    spot = lax.broadcasted_iota(jnp.int32, (wide, lanes), 1) // BODIES
    lead = lax.broadcasted_iota(jnp.int32, (wide, lanes), 0).astype(F32) - 1.0
    base = 2 * pairs * deep
    ends = base + 4 * wide
    for side, value in enumerate((below, above)):
        shift = [-1.0 if side == 0 else float(lx), lead, spot.astype(F32)]
        for c in range(3):
            side_ref[side, c] = value[base + c * wide : base + (c + 1) * wide] + shift[c]
        for z, part in enumerate(spans(value[base + 3 * wide : base + 4 * wide], spot, lz)):
            side_ref[side, 3 + z] = part
    spot = lax.broadcasted_iota(jnp.int32, (half, lanes), 1) // BODIES
    place = lax.broadcasted_iota(jnp.int32, (half, lanes), 0)
    for side, value in enumerate((below, above)):
        for end in range(2):
            shift = [-1.0 if side == 0 else float(lx), (spot + 2 * place - 1).astype(F32), -1.0 if end == 0 else float(lz)]
            for c in range(3):
                at = ends + (end * 4 + c) * half
                edge_ref[side, end * 5 + c] = value[at : at + half] + shift[c]
            at = ends + (end * 4 + 3) * half
            for s in range(2):
                edge_ref[side, end * 5 + 3 + s] = jnp.where((spot >= s) & (spot < s + 3), value[at : at + half], 0.0)

    sphere = sphere_ref[...]
    for x in range(lx):
        turned = turn(offs_ref, x) if x in (0, lx - 1) else None
        for y in range(ly):

            def rows(z):
                for side in range(2):
                    if x == (0 if side == 0 else lx - 1):
                        for dy in range(3):
                            at = pl.ds(y + dy, 1)
                            yield [side_ref[side, c, at, :] for c in range(3)], side_ref[side, 3 + z, at, :], False
                        for end in range(2):
                            if z == (0 if end == 0 else lz - 1):
                                at = pl.ds(y // 2, 1)
                                source = [edge_ref[side, end * 5 + c, at, :] for c in range(3)]
                                yield source, edge_ref[side, end * 5 + 3 + y % 2, at, :], False

            kernel = surface_green(sphere, offs_ref, x, y)
            far = jnp.sum(kernel * dense_ref[x * half + y // 2, y % 2], axis=0, keepdims=True)
            at = pl.ds(y, 1)
            total = near_end_ref[x, at, :] + far
            if x in (0, lx - 1):
                gather(out_ref, x, y, turned, lz, rows)
                total = total + out_ref[x, at, :] + near_edge_ref[0 if x == 0 else 1, at, :]
            else:
                total = total + near_in_ref[x - 1, at, :]
            out_ref[x, at, :] = total


def partners(axis):
    count = lax.axis_size(axis)
    rounds = [[(i, i + 1) for i in range(start, count - 1, 2)] for start in range(2)]
    return [[pair for i, j in pairs for pair in ((i, j), (j, i))] for pairs in rounds if pairs] or [[]]


def exchange(packets, axis):
    return [lax.ppermute(packet, axis, pairs) for packet, pairs in zip(packets, partners(axis))]


def call(kernel, outs, args, scratch=(), limit=8, name=None, spaces=None):
    spec = pl.BlockSpec(memory_space=pltpu.VMEM)
    return pl.pallas_call(
        kernel,
        out_shape=outs,
        in_specs=[pl.BlockSpec(memory_space=space) for space in spaces] if spaces else [spec] * len(args),
        out_specs=[spec] * len(outs),
        scratch_shapes=list(scratch),
        compiler_params=pltpu.CompilerParams(vmem_limit_bytes=limit << 20),
        name=name,
    )(*args)


def shaped(*shape):
    return jax.ShapeDtypeStruct(shape, F32)


def per_device(offsets, charges, up_inverse, translations, down_inverse):
    points = up_inverse.shape[0]
    _, lx, ly, lanes = offsets.shape
    lz = lanes // BODIES
    half = ly // 2
    pairs = half + 2
    wide = ly + 2
    deep = lz + 4
    rounds = {axis: len(partners(axis)) for axis in ("gx", "gy", "gz")}
    sphere = jnp.asarray(surface(points))
    boxes = lx * half * lz
    packet = shaped(lx * lz + 4 * lx, lanes)
    density, *packets = call(
        upward_kernel,
        [shaped(boxes, 2 * points)] + [packet] * rounds["gy"],
        (offsets, charges, sphere, up_inverse),
        [
            pltpu.VMEM(offsets.shape, F32),
            pltpu.VMEM(charges.shape, F32),
            pltpu.VMEM(sphere.shape, F32),
            pltpu.VMEM(up_inverse.shape, F32),
            pltpu.VMEM((boxes, 2 * points), F32),
            pltpu.VMEM((2 * points, 2 * points), F32),
            pltpu.SemaphoreType.DMA((4,)),
        ],
        4,
        "upward",
        [pltpu.HBM] * 4,
    )
    received = exchange(packets, "gy")
    count, width = translations.shape
    stride = count // 2 * 2 + 1
    (weights,) = call(
        table_kernel,
        [jax.ShapeDtypeStruct((SPAN, SPAN * points, (SPAN + 1) * points), BF16)],
        (translations, density),
        [pltpu.VMEM((width // 128 * stride, 128), F32)],
        16,
        "table",
        [pltpu.VMEM, pl.ANY],
    )
    first = lax.optimization_barrier((offsets, charges, weights))
    (edge,) = call(
        edge_kernel,
        [shaped(2, ly, lanes)],
        first[:2],
        [pltpu.VMEM((3 + lz, lx * ly, lanes), F32)],
        name="near_edge",
    )
    weights = first[2]
    received, edge, weights = lax.optimization_barrier((received, edge, weights))
    packet = shaped(lx * pairs * 2 + 4 * half * lx, lanes)
    dense, body, *packets = call(
        functools.partial(zpack_kernel, len(received)),
        [shaped(lx * pairs * lz, 2 * points), shaped(4, lx * wide, lanes)] + [packet] * rounds["gz"],
        (offsets, charges, density, *received),
        name="zpack",
    )
    packets, body = lax.optimization_barrier((packets, body))
    received = exchange(packets, "gz")
    windows = [pltpu.VMEM((3 + lz, lx * wide, lanes), F32)]
    (inner,) = call(inner_kernel, [shaped(lx - 2, ly, lanes)], (offsets, body), windows, name="near_inner")
    received, inner = lax.optimization_barrier((received, inner))
    packet = shaped(2 * pairs * deep + 4 * wide + 8 * half, lanes)
    end = shaped(4, half * lx, lanes)
    dense, low, high, *packets = call(
        functools.partial(xpack_kernel, len(received)),
        [shaped(lx * pairs, deep, 2 * points), end, end] + [packet] * rounds["gx"],
        (dense, body, *received),
        name="xpack",
    )
    packets, body = lax.optimization_barrier((packets, body))
    received = exchange(packets, "gx")
    (ends,) = call(
        ends_kernel,
        [shaped(lx, ly, lanes)],
        (offsets, body, low, high),
        windows + [pltpu.VMEM((10, half * lx, lanes), F32)],
        name="near_ends",
    )
    received, ends = lax.optimization_barrier((received, ends))
    (out,) = call(
        functools.partial(final_kernel, len(received)),
        [shaped(lx, ly, lanes)],
        (offsets, dense, edge, inner, ends, weights, down_inverse, sphere, *received),
        [
            pltpu.VMEM(((lx + 4) * half * deep, 6 * points), BF16),
            pltpu.VMEM((lx * half, 8 + deep + 8, (SPAN + 1) * points), F32),
            pltpu.VMEM((lx * half, 2, points, lanes), F32),
            pltpu.VMEM((boxes, 2 * points), F32),
            pltpu.VMEM((2, 3 + lz, wide, lanes), F32),
            pltpu.VMEM((2, 10, half, lanes), F32),
        ],
        24,
        "final",
    )
    return out


def solution(mesh):
    in_specs = (P(None, "gx", "gy", "gz"), P("gx", "gy", "gz"), P(), P(), P())
    out_specs = P("gx", "gy", "gz")
    return jax.shard_map(
        per_device, mesh=mesh, in_specs=in_specs, out_specs=out_specs, check_vma=False
    )
```

```python
import functools
import math

import jax
import jax.numpy as jnp
import numpy as np
from jax import lax
from jax.experimental import pallas as pl
from jax.experimental.pallas import tpu as pltpu
from jax.sharding import PartitionSpec as P

BODIES = 32
RADIUS = 0.9
REACH = 3
SPAN = 2 * REACH + 1
F32 = jnp.float32
BF16 = jnp.bfloat16
NT = (((1,), (1,)), ((), ()))


def surface(points):
    number = np.arange(points).astype(np.float32)
    height = np.float32(1.0) - (np.float32(2.0) * number + np.float32(1.0)) / np.float32(points)
    across = np.sqrt(np.float32(1.0) - height * height)
    turned = number * np.float32(math.pi * (3.0 - math.sqrt(5.0)))
    columns = np.zeros((points, 128), np.float32)
    columns[:, 0] = RADIUS * across * np.cos(turned)
    columns[:, 1] = RADIUS * across * np.sin(turned)
    columns[:, 2] = RADIUS * height
    return columns


def numbering():
    table, count = {}, 0
    for ox in range(-REACH, REACH + 1):
        for oy in range(-REACH, REACH + 1):
            for oz in range(-REACH, REACH + 1):
                if max(abs(ox), abs(oy), abs(oz)) >= 2:
                    table[ox, oy, oz] = count
                    count += 1
    return table


def split(value):
    high = value.astype(BF16)
    return high, (value - high.astype(F32)).astype(BF16)


def surface_green(sphere, offs_ref, x, y):
    rows = [offs_ref[c, x, pl.ds(y, 1), :] - 0.5 for c in range(3)]
    square = None
    for c in range(3):
        delta = sphere[:, c : c + 1] - rows[c]
        square = delta * delta if square is None else square + delta * delta
    return lax.rsqrt(square)


def select(even, one, two):
    return jnp.where(even, one, two), jnp.where(even, two, one)


def put(refs, at, even, low, high):
    refs[0][at, :] = jnp.where(even, high, low)
    for ref in refs[1:]:
        ref[at, :] = jnp.where(even, low, high)


def get(refs, even):
    one = refs[0][...]
    return select(even, one, refs[1][...] if len(refs) > 1 else jnp.zeros_like(one))


def upward_kernel(
    offs_hbm, q_hbm, sphere_hbm, uinv_hbm, dinv_hbm, offs_ref, q_ref, sphere_ref, dinv_ref, u_ref, *rest
):
    *packets, uinv_ref, check_ref, wide_ref, sems = rest
    copies = [
        pltpu.make_async_copy(source, target, sems.at[n])
        for n, (source, target) in enumerate(
            (
                (offs_hbm, offs_ref),
                (q_hbm, q_ref),
                (sphere_hbm, sphere_ref),
                (uinv_hbm, uinv_ref),
                (dinv_hbm, dinv_ref),
            )
        )
    ]
    for copy in copies:
        copy.start()
    _, lx, ly, lanes = offs_ref.shape
    lz = lanes // BODIES
    half = ly // 2
    points = uinv_ref.shape[0]
    even = lax.axis_index("gy") % 2 == 0
    segment = (
        lax.broadcasted_iota(jnp.int32, (8, lanes), 1) // BODIES
        == lax.broadcasted_iota(jnp.int32, (8, lanes), 0)
    ).astype(BF16)
    wide_ref[...] = jnp.zeros_like(wide_ref)
    column = lax.broadcasted_iota(jnp.int32, (2 * points, 2 * points), 1)
    within = column % points
    wanted = column - within + jnp.where(within < points // 2, 2 * within, 2 * within - points + 1)
    shuffle = (lax.broadcasted_iota(jnp.int32, (2 * points, 2 * points), 0) == wanted).astype(BF16)
    for copy in copies[:3]:
        copy.wait()
    sphere = sphere_ref[...]
    for c in range(4):
        for x in range(lx):
            low, high = [
                offs_ref[c, x, pl.ds(y, 1), :] if c < 3 else q_ref[x, pl.ds(y, 1), :] for y in (0, ly - 1)
            ]
            put(packets, pl.ds(lx * lz + c * lx + x, 1), even, low, high)
    for x in range(lx):
        for pair in range(half):
            parts = [
                surface_green(sphere, offs_ref, x, 2 * pair + par) * q_ref[x, pl.ds(2 * pair + par, 1), :]
                for par in range(2)
            ]
            high, low = split(jnp.concatenate(parts, axis=0))
            sums = lax.dot_general(segment, high, NT, preferred_element_type=F32)
            sums = sums + lax.dot_general(segment, low, NT, preferred_element_type=F32)
            check_ref[pl.ds((x * half + pair) * lz, lz), :] = sums[:lz]
    copies[3].wait()
    wide_ref[:points, :points] = uinv_ref[...]
    wide_ref[points:, points:] = uinv_ref[...]
    density = jnp.dot(
        check_ref[...], wide_ref[...], precision=lax.Precision.HIGHEST, preferred_element_type=F32
    ).astype(BF16)
    u_ref[...] = jnp.dot(density, shuffle, preferred_element_type=F32)
    for x in range(lx):
        low = u_ref[pl.ds(x * half * lz, lz), :]
        high = u_ref[pl.ds((x * half + half - 1) * lz, lz), :]
        put(packets, pl.ds(x * lz, lz), even, low, high)
    copies[4].wait()


def relay(t_ref, copies, w_ref, rows_ref):
    count, width = t_ref.shape
    groups = width // 128
    stride = rows_ref.shape[0] // groups
    points = math.isqrt(width)
    half = points // 2
    order = numbering()
    for a in range(groups):
        if a % (groups // len(copies)) == 0:
            copies[a // (groups // len(copies))].wait()
        rows_ref[pl.ds(a * stride, count), :] = t_ref[:, a * 128 : (a + 1) * 128].astype(F32)
    left = lax.broadcasted_iota(jnp.int32, (groups, 128), 1) < points
    zero = jnp.zeros((groups, 128), F32)
    for ox in range(SPAN):
        for oy in range(SPAN):
            for k in range((SPAN + 1) // 2):
                loaded = []
                for oz in (2 * k, 2 * k + 1):
                    at = order.get((ox - REACH, oy - REACH, oz - REACH))
                    loaded.append(zero if at is None else rows_ref[pl.ds(at, groups, stride=stride), :])
                one, two = loaded
                even = jnp.where(left, one, pltpu.roll(two, points, 1))
                odd = jnp.where(left, pltpu.roll(one, points, 1), two)
                at = slice(k * 128, (k + 1) * 128)
                w_ref[ox, pl.ds(oy * points, half), at] = even.astype(BF16)
                w_ref[ox, pl.ds(oy * points + half, half), at] = odd.astype(BF16)


def zpack_kernel(count, offs_ref, q_ref, u_ref, *rest):
    received, (d_ref, r_ref, *packets) = rest[:count], rest[count:]
    _, lx, ly, lanes = offs_ref.shape
    lz = lanes // BODIES
    half = ly // 2
    wide = ly + 2
    above, below = get(received, lax.axis_index("gy") % 2 == 0)
    even = lax.axis_index("gz") % 2 == 0
    for x in range(lx):
        at = x * (half + 2) * lz
        d_ref[pl.ds(at, lz), :] = below[x * lz : (x + 1) * lz]
        d_ref[pl.ds(at + lz, half * lz), :] = u_ref[pl.ds(x * half * lz, half * lz), :]
        d_ref[pl.ds(at + (half + 1) * lz, lz), :] = above[x * lz : (x + 1) * lz]
        for c in range(4):
            row = lx * lz + c * lx + x
            r_ref[c, pl.ds(x * wide, 1), :] = below[row : row + 1]
            r_ref[c, pl.ds(x * wide + 1, ly), :] = offs_ref[c, x] if c < 3 else q_ref[x]
            r_ref[c, pl.ds(x * wide + ly + 1, 1), :] = above[row : row + 1]
    for g in range(lx * (half + 2)):
        put(packets, pl.ds(g * 2, 2), even, d_ref[pl.ds(g * lz, 2), :], d_ref[pl.ds(g * lz + lz - 2, 2), :])
    spot = lax.broadcasted_iota(jnp.int32, (lx, lanes), 1) // BODIES
    base = lx * (half + 2) * 2
    for c in range(4):
        rows = [r_ref[c, pl.ds(j, lx, stride=wide), :] for j in range(wide)]
        for pack in range(half):
            low = high = None
            for j in range(4):
                row = rows[2 * pack + j]
                first = pltpu.roll(row, j * BODIES, 1) if j else row
                last = pltpu.roll(row, (j + 1) % 4 * BODIES, 1) if (j + 1) % 4 else row
                low = first if low is None else jnp.where(spot == j, first, low)
                high = last if high is None else jnp.where(spot == j, last, high)
            put(packets, pl.ds(base + (c * half + pack) * lx, lx), even, low, high)


def xpack_kernel(count, d_ref, r_ref, *rest):
    received, (e_ref, zl_ref, zh_ref, *packets) = rest[:count], rest[count:]
    groups = e_ref.shape[0]
    lx = zl_ref.shape[1] // 2
    pairs = groups // lx
    half = pairs - 2
    wide = 2 * half + 2
    lz = d_ref.shape[0] // groups
    above, below = get(received, lax.axis_index("gz") % 2 == 0)
    even = lax.axis_index("gx") % 2 == 0
    for g in range(groups):
        e_ref[g, pl.ds(0, 2), :] = below[g * 2 : g * 2 + 2]
        e_ref[g, pl.ds(2, lz), :] = d_ref[pl.ds(g * lz, lz), :]
        e_ref[g, pl.ds(2 + lz, 2), :] = above[g * 2 : g * 2 + 2]
    base = groups * 2
    for c in range(4):
        zl_ref[c] = below[base + c * half * lx : base + (c + 1) * half * lx]
        zh_ref[c] = above[base + c * half * lx : base + (c + 1) * half * lx]
    deep = lz + 4
    for n in range(2 * pairs):
        put(packets, pl.ds(n * deep, deep), even, e_ref[n], e_ref[groups - 2 * pairs + n])
    base = 2 * pairs * deep
    for c in range(4):
        low, high = r_ref[c, pl.ds(0, wide), :], r_ref[c, pl.ds((lx - 1) * wide, wide), :]
        put(packets, pl.ds(base + c * wide, wide), even, low, high)
    base = base + 4 * wide
    for end, ref in enumerate((zl_ref, zh_ref)):
        for c in range(4):
            for pack in range(half):
                low, high = ref[c, pl.ds(pack * lx, 1), :], ref[c, pl.ds(pack * lx + lx - 1, 1), :]
                put(packets, pl.ds(base + (end * 4 + c) * half + pack, 1), even, low, high)


def turn(offs_ref, x):
    _, _, ly, lanes = offs_ref.shape
    lead = lax.broadcasted_iota(jnp.int32, (ly, lanes), 0).astype(F32)
    spots = (lax.broadcasted_iota(jnp.int32, (ly, lanes), 1) // BODIES).astype(F32)
    places = [offs_ref[0, x] + float(x), offs_ref[1, x] + lead, offs_ref[2, x] + spots]
    return jnp.concatenate(places + [places[0]], axis=0).T


def pick(turned, ly, y, z):
    return [turned[z * BODIES : (z + 1) * BODIES, c * ly + y : c * ly + y + 1] for c in range(3)]


def attract(total, target, source, weight, own=False):
    square = None
    for t, s in zip(target, source):
        delta = t - s
        square = delta * delta if square is None else square + delta * delta
    inverse = lax.rsqrt(square)
    if own:
        inverse = jnp.where(square > 0.0, inverse, 0.0)
    term = inverse * weight
    return term if total is None else total + term


def lane_sum(ones, parts):
    high, low = split(jnp.concatenate(parts, axis=0))
    out = lax.dot_general(ones, high, NT, preferred_element_type=F32)
    return (out + lax.dot_general(ones, low, NT, preferred_element_type=F32))[:1]


def spans(value, spot, lz):
    return [jnp.where((spot >= z - 1) & (spot <= z + 1), value, 0.0) for z in range(lz)]


def gather(out_ref, n, y, turned, lz, rows):
    _, ly, lanes = out_ref.shape
    ones = jnp.ones((8, lanes), BF16)
    parts = []
    for z in range(lz):
        target = pick(turned, ly, y, z)
        total = None
        for source, weight, own in rows(z):
            total = attract(total, target, source, weight, own)
        parts.append(jnp.zeros((BODIES, lanes), F32) if total is None else total)
    out_ref[n, pl.ds(y, 1), :] = lane_sum(ones, parts)


def row_source(ref, at, z, own=False):
    return [ref[c, at, :] for c in range(3)], ref[3 + z, at, :], own


def edge_kernel(t_hbm, after_ref, offs_ref, q_ref, out_ref, w_ref, win_ref, t_ref, rows_ref, sems):
    chunks = sems.shape[0]
    cut = t_ref.shape[1] // chunks
    copies = [
        pltpu.make_async_copy(
            t_hbm.at[:, pl.ds(n * cut, cut)], t_ref.at[:, pl.ds(n * cut, cut)], sems.at[n]
        )
        for n in range(chunks)
    ]
    for copy in copies:
        copy.start()
    _, lx, ly, lanes = offs_ref.shape
    lz = lanes // BODIES
    spot = lax.broadcasted_iota(jnp.int32, (ly, lanes), 1) // BODIES
    lead = lax.broadcasted_iota(jnp.int32, (ly, lanes), 0)
    for x in range(lx):
        at = pl.ds(x * ly, ly)
        shift = [float(x), lead.astype(F32), spot.astype(F32)]
        for c in range(3):
            win_ref[c, at, :] = offs_ref[c, x] + shift[c]
        for z, value in enumerate(spans(q_ref[x], spot, lz)):
            win_ref[3 + z, at, :] = value
    for n, x in enumerate((0, lx - 1)):
        turned = turn(offs_ref, x)
        for y in range(ly):

            def rows(z):
                for xx in range(max(x - 1, 0), min(x + 2, lx)):
                    for yy in range(max(y - 1, 0), min(y + 2, ly)):
                        yield row_source(win_ref, pl.ds(xx * ly + yy, 1), z, xx == x and yy == y)

            gather(out_ref, n, y, turned, lz, rows)
    relay(t_ref, copies, w_ref, rows_ref)


def strips(r_ref, win_ref, wide, lz):
    _, rows, lanes = r_ref.shape
    place = lax.broadcasted_iota(jnp.int32, (rows, lanes), 0)
    spot = lax.broadcasted_iota(jnp.int32, (rows, lanes), 1) // BODIES
    base = [place // wide, place % wide - 1, spot]
    for c in range(3):
        win_ref[c] = r_ref[c] + base[c].astype(F32)
    for z, value in enumerate(spans(r_ref[3], spot, lz)):
        win_ref[3 + z] = value


def inner_kernel(offs_ref, r_ref, out_ref, win_ref):
    _, lx, ly, lanes = offs_ref.shape
    lz = lanes // BODIES
    wide = ly + 2
    strips(r_ref, win_ref, wide, lz)
    for x in range(1, lx - 1):
        turned = turn(offs_ref, x)
        for y in range(ly):

            def rows(z):
                for xx in range(x - 1, x + 2):
                    for dy in range(3):
                        yield row_source(win_ref, pl.ds(xx * wide + y + dy, 1), z, xx == x and dy == 1)

            gather(out_ref, x - 1, y, turned, lz, rows)


def ends_kernel(offs_ref, r_ref, zl_ref, zh_ref, out_ref, win_ref, end_ref):
    _, lx, ly, lanes = offs_ref.shape
    lz = lanes // BODIES
    half = ly // 2
    wide = ly + 2
    strips(r_ref, win_ref, wide, lz)
    end_windows(zl_ref, -1.0, end_ref, 0, lz, half)
    end_windows(zh_ref, float(lz), end_ref, 5, lz, half)
    for x in range(lx):
        turned = turn(offs_ref, x)
        for y in range(ly):

            def rows(z):
                nearby = range(max(x - 1, 0), min(x + 2, lx))
                if x in (0, lx - 1):
                    for yy in (y, y + 2):
                        if yy in (0, ly + 1):
                            for xx in nearby:
                                yield row_source(win_ref, pl.ds(xx * wide + yy, 1), z)
                for end in range(2):
                    if z == (0 if end == 0 else lz - 1):
                        for xx in nearby:
                            at = pl.ds(y // 2 * lx + xx, 1)
                            source = [end_ref[end * 5 + c, at, :] for c in range(3)]
                            yield source, end_ref[end * 5 + 3 + y % 2, at, :], False

            gather(out_ref, x, y, turned, lz, rows)


def end_windows(end_ref, base, win_ref, at, lz, half):
    rows = end_ref.shape[1]
    lanes = end_ref.shape[2]
    count = rows // half
    place = lax.broadcasted_iota(jnp.int32, (rows, lanes), 0)
    spot = lax.broadcasted_iota(jnp.int32, (rows, lanes), 1) // BODIES
    shift = [(place % count).astype(F32), (spot + 2 * (place // count) - 1).astype(F32), base]
    for c in range(3):
        win_ref[at + c] = end_ref[c] + shift[c]
    for s in range(2):
        win_ref[at + 3 + s] = jnp.where((spot >= s) & (spot < s + 3), end_ref[3], 0.0)


def final_kernel(count, offs_ref, e_ref, near_edge_ref, near_in_ref, near_end_ref, w_ref, dinv_ref, sphere_ref, *rest):
    received, rest = rest[:count], rest[count:]
    out_ref, left_ref, acc_ref, dense_ref, sum_ref, side_ref, edge_ref = rest
    _, lx, ly, lanes = offs_ref.shape
    lz = lanes // BODIES
    points = dinv_ref.shape[0]
    half = ly // 2
    pairs = half + 2
    wide = ly + 2
    deep = lz + 4
    block = half * deep
    width = (SPAN - 1) * points
    above, below = get(received, lax.axis_index("gx") % 2 == 0)

    def plane(x, pair):
        if x < 2:
            return below[(x * pairs + pair) * deep : (x * pairs + pair + 1) * deep]
        if x < lx + 2:
            return e_ref[(x - 2) * pairs + pair]
        return above[((x - lx - 2) * pairs + pair) * deep : ((x - lx - 2) * pairs + pair + 1) * deep]

    for x in range(lx + 4):
        planes = [plane(x, pair) for pair in range(pairs)]
        for j in range(SPAN // 2):
            left_ref[pl.ds(x * block, block), j * 128 : (j + 1) * 128] = jnp.concatenate(
                planes[j : j + half], axis=0
            ).astype(BF16)
    twice = jnp.concatenate([dinv_ref[...]] * 2, axis=0)
    expand = (
        lax.broadcasted_iota(jnp.int32, (lx * half * lz, lx * half * lanes), 1) // BODIES
        == lax.broadcasted_iota(jnp.int32, (lx * half * lz, lx * half * lanes), 0)
    ).astype(BF16)
    lane = lax.broadcasted_iota(jnp.int32, (lz, 128), 1)
    level = lax.broadcasted_iota(jnp.int32, (lz, 128), 0)
    for cy in range(2):
        total = [None] * lx
        for ox in range(-REACH, REACH + 1):
            chosen = [b for b in range(lx) if not (ox == -REACH and b % 2 == 0) and not (ox == REACH and b % 2 == 1)]
            parts = [left_ref[pl.ds((b + ox + 2) * block, block), :] for b in chosen]
            lhs = jnp.concatenate(parts, axis=0)
            rhs = w_ref[ox + REACH, pl.ds((1 - cy) * points, width), :]
            got = jnp.dot(lhs, rhs, preferred_element_type=F32)
            for n, b in enumerate(chosen):
                piece = got[n * block : (n + 1) * block]
                total[b] = piece if total[b] is None else total[b] + piece
        for b in range(lx):
            for p in range(half):
                acc_ref[b * half + p, pl.ds(8, deep), :] = total[b][p * deep : (p + 1) * deep]
        for g in range(lx * half):
            folded = None
            for k in range((SPAN + 1) // 2):
                shown = []
                for oz in (2 * k - REACH, 2 * k + 1 - REACH):
                    if oz > REACH:
                        shown.append(jnp.zeros((lz, 128), F32))
                        continue
                    got = acc_ref[g, pl.ds(8 + oz + 2, lz), k * 128 : (k + 1) * 128]
                    if oz == -REACH:
                        got = jnp.where(level % 2 == 1, got, 0.0)
                    if oz == REACH:
                        got = jnp.where(level % 2 == 0, got, 0.0)
                    shown.append(got)
                both = jnp.where(lane < points, shown[0], shown[1])
                folded = both if folded is None else folded + both
            sum_ref[pl.ds(g * lz, lz), :] = folded
        dense = jnp.dot(sum_ref[...], twice, precision=lax.Precision.HIGHEST, preferred_element_type=F32)
        high, low = split(dense.T)
        spread = jnp.dot(high, expand, preferred_element_type=F32)
        spread = spread + jnp.dot(low, expand, preferred_element_type=F32)
        for g in range(lx * half):
            dense_ref[g, cy] = spread[:, g * lanes : (g + 1) * lanes]

    spot = lax.broadcasted_iota(jnp.int32, (wide, lanes), 1) // BODIES
    lead = lax.broadcasted_iota(jnp.int32, (wide, lanes), 0).astype(F32) - 1.0
    base = 2 * pairs * deep
    ends = base + 4 * wide
    for side, value in enumerate((below, above)):
        shift = [-1.0 if side == 0 else float(lx), lead, spot.astype(F32)]
        for c in range(3):
            side_ref[side, c] = value[base + c * wide : base + (c + 1) * wide] + shift[c]
        for z, part in enumerate(spans(value[base + 3 * wide : base + 4 * wide], spot, lz)):
            side_ref[side, 3 + z] = part
    spot = lax.broadcasted_iota(jnp.int32, (half, lanes), 1) // BODIES
    place = lax.broadcasted_iota(jnp.int32, (half, lanes), 0)
    for side, value in enumerate((below, above)):
        for end in range(2):
            shift = [-1.0 if side == 0 else float(lx), (spot + 2 * place - 1).astype(F32), -1.0 if end == 0 else float(lz)]
            for c in range(3):
                at = ends + (end * 4 + c) * half
                edge_ref[side, end * 5 + c] = value[at : at + half] + shift[c]
            at = ends + (end * 4 + 3) * half
            for s in range(2):
                edge_ref[side, end * 5 + 3 + s] = jnp.where((spot >= s) & (spot < s + 3), value[at : at + half], 0.0)

    sphere = sphere_ref[...]
    for x in range(lx):
        turned = turn(offs_ref, x) if x in (0, lx - 1) else None
        for y in range(ly):

            def rows(z):
                for side in range(2):
                    if x == (0 if side == 0 else lx - 1):
                        for dy in range(3):
                            at = pl.ds(y + dy, 1)
                            yield [side_ref[side, c, at, :] for c in range(3)], side_ref[side, 3 + z, at, :], False
                        for end in range(2):
                            if z == (0 if end == 0 else lz - 1):
                                at = pl.ds(y // 2, 1)
                                source = [edge_ref[side, end * 5 + c, at, :] for c in range(3)]
                                yield source, edge_ref[side, end * 5 + 3 + y % 2, at, :], False

            kernel = surface_green(sphere, offs_ref, x, y)
            far = jnp.sum(kernel * dense_ref[x * half + y // 2, y % 2], axis=0, keepdims=True)
            at = pl.ds(y, 1)
            total = near_end_ref[x, at, :] + far
            if x in (0, lx - 1):
                gather(out_ref, x, y, turned, lz, rows)
                total = total + out_ref[x, at, :] + near_edge_ref[0 if x == 0 else 1, at, :]
            else:
                total = total + near_in_ref[x - 1, at, :]
            out_ref[x, at, :] = total


def partners(axis):
    count = lax.axis_size(axis)
    rounds = [[(i, i + 1) for i in range(start, count - 1, 2)] for start in range(2)]
    return [[pair for i, j in pairs for pair in ((i, j), (j, i))] for pairs in rounds if pairs] or [[]]


def exchange(packets, axis):
    return [lax.ppermute(packet, axis, pairs) for packet, pairs in zip(packets, partners(axis))]


def call(kernel, outs, args, scratch=(), limit=8, name=None, spaces=None):
    spec = pl.BlockSpec(memory_space=pltpu.VMEM)
    return pl.pallas_call(
        kernel,
        out_shape=outs,
        in_specs=[pl.BlockSpec(memory_space=space) for space in spaces] if spaces else [spec] * len(args),
        out_specs=[spec] * len(outs),
        scratch_shapes=list(scratch),
        compiler_params=pltpu.CompilerParams(vmem_limit_bytes=limit << 20),
        name=name,
    )(*args)


def shaped(*shape):
    return jax.ShapeDtypeStruct(shape, F32)


def per_device(offsets, charges, up_inverse, translations, down_inverse):
    points = up_inverse.shape[0]
    _, lx, ly, lanes = offsets.shape
    lz = lanes // BODIES
    half = ly // 2
    pairs = half + 2
    wide = ly + 2
    deep = lz + 4
    rounds = {axis: len(partners(axis)) for axis in ("gx", "gy", "gz")}
    sphere = jnp.asarray(surface(points))
    boxes = lx * half * lz
    packet = shaped(lx * lz + 4 * lx, lanes)
    inputs = [
        pltpu.with_memory_space_constraint(value, pltpu.HBM)
        for value in (offsets, charges, sphere, up_inverse, down_inverse)
    ]
    offsets, charges, sphere, down_inverse, density, *packets = call(
        upward_kernel,
        [shaped(*value.shape) for value in (offsets, charges, sphere, down_inverse)]
        + [shaped(boxes, 2 * points)]
        + [packet] * rounds["gy"],
        inputs,
        [
            pltpu.VMEM(up_inverse.shape, F32),
            pltpu.VMEM((boxes, 2 * points), F32),
            pltpu.VMEM((2 * points, 2 * points), F32),
            pltpu.SemaphoreType.DMA((5,)),
        ],
        4,
        "upward",
        [pltpu.HBM] * 5,
    )
    received = exchange(packets, "gy")
    count, width = translations.shape
    stride = count // 2 * 2 + 1
    edge, weights = call(
        edge_kernel,
        [
            shaped(2, ly, lanes),
            jax.ShapeDtypeStruct((SPAN, SPAN * points, (SPAN + 1) * points), BF16),
        ],
        (pltpu.with_memory_space_constraint(translations, pltpu.HBM), density, offsets, charges),
        [
            pltpu.VMEM((3 + lz, lx * ly, lanes), F32),
            pltpu.VMEM(translations.shape, BF16),
            pltpu.VMEM((width // 128 * stride, 128), F32),
            pltpu.SemaphoreType.DMA((4,)),
        ],
        24,
        "near_edge",
        [pltpu.HBM, pl.ANY, pltpu.VMEM, pltpu.VMEM],
    )
    received, edge, weights = lax.optimization_barrier((received, edge, weights))
    packet = shaped(lx * pairs * 2 + 4 * half * lx, lanes)
    dense, body, *packets = call(
        functools.partial(zpack_kernel, len(received)),
        [shaped(lx * pairs * lz, 2 * points), shaped(4, lx * wide, lanes)] + [packet] * rounds["gz"],
        (offsets, charges, density, *received),
        name="zpack",
    )
    packets, body = lax.optimization_barrier((packets, body))
    received = exchange(packets, "gz")
    windows = [pltpu.VMEM((3 + lz, lx * wide, lanes), F32)]
    (inner,) = call(inner_kernel, [shaped(lx - 2, ly, lanes)], (offsets, body), windows, name="near_inner")
    received, inner = lax.optimization_barrier((received, inner))
    packet = shaped(2 * pairs * deep + 4 * wide + 8 * half, lanes)
    end = shaped(4, half * lx, lanes)
    dense, low, high, *packets = call(
        functools.partial(xpack_kernel, len(received)),
        [shaped(lx * pairs, deep, 2 * points), end, end] + [packet] * rounds["gx"],
        (dense, body, *received),
        name="xpack",
    )
    packets, body = lax.optimization_barrier((packets, body))
    received = exchange(packets, "gx")
    (ends,) = call(
        ends_kernel,
        [shaped(lx, ly, lanes)],
        (offsets, body, low, high),
        windows + [pltpu.VMEM((10, half * lx, lanes), F32)],
        name="near_ends",
    )
    received, ends = lax.optimization_barrier((received, ends))
    (out,) = call(
        functools.partial(final_kernel, len(received)),
        [shaped(lx, ly, lanes)],
        (offsets, dense, edge, inner, ends, weights, down_inverse, sphere, *received),
        [
            pltpu.VMEM(((lx + 4) * half * deep, 6 * points), BF16),
            pltpu.VMEM((lx * half, 8 + deep + 8, (SPAN + 1) * points), F32),
            pltpu.VMEM((lx * half, 2, points, lanes), F32),
            pltpu.VMEM((boxes, 2 * points), F32),
            pltpu.VMEM((2, 3 + lz, wide, lanes), F32),
            pltpu.VMEM((2, 10, half, lanes), F32),
        ],
        24,
        "final",
    )
    return out


def solution(mesh):
    in_specs = (P(None, "gx", "gy", "gz"), P("gx", "gy", "gz"), P(), P(), P())
    out_specs = P("gx", "gy", "gz")
    return jax.shard_map(
        per_device, mesh=mesh, in_specs=in_specs, out_specs=out_specs, check_vma=False
    )
```

```python
import functools
import math

import jax
import jax.numpy as jnp
import numpy as np
from jax import lax
from jax.experimental import pallas as pl
from jax.experimental.pallas import tpu as pltpu
from jax.sharding import PartitionSpec as P

BODIES = 32
RADIUS = 0.9
REACH = 3
SPAN = 2 * REACH + 1
F32 = jnp.float32
BF16 = jnp.bfloat16
NT = (((1,), (1,)), ((), ()))


def surface(points):
    number = np.arange(points).astype(np.float32)
    height = np.float32(1.0) - (np.float32(2.0) * number + np.float32(1.0)) / np.float32(points)
    across = np.sqrt(np.float32(1.0) - height * height)
    turned = number * np.float32(math.pi * (3.0 - math.sqrt(5.0)))
    columns = np.zeros((points, 128), np.float32)
    columns[:, 0] = RADIUS * across * np.cos(turned)
    columns[:, 1] = RADIUS * across * np.sin(turned)
    columns[:, 2] = RADIUS * height
    return columns


def numbering():
    table, count = {}, 0
    for ox in range(-REACH, REACH + 1):
        for oy in range(-REACH, REACH + 1):
            for oz in range(-REACH, REACH + 1):
                if max(abs(ox), abs(oy), abs(oz)) >= 2:
                    table[ox, oy, oz] = count
                    count += 1
    return table


def split(value):
    high = value.astype(BF16)
    return high, (value - high.astype(F32)).astype(BF16)


def surface_green(sphere, offs_ref, x, y):
    rows = [offs_ref[c, x, pl.ds(y, 1), :] - 0.5 for c in range(3)]
    square = None
    for c in range(3):
        delta = sphere[:, c : c + 1] - rows[c]
        square = delta * delta if square is None else square + delta * delta
    return lax.rsqrt(square)


def select(even, one, two):
    return jnp.where(even, one, two), jnp.where(even, two, one)


def put(refs, at, even, low, high):
    refs[0][at, :] = jnp.where(even, high, low)
    for ref in refs[1:]:
        ref[at, :] = jnp.where(even, low, high)


def get(refs, axis):
    index = lax.axis_index(axis)
    one = refs[0][...]
    above, below = select(index % 2 == 0, one, refs[1][...] if len(refs) > 1 else one)
    return jnp.where(index == lax.axis_size(axis) - 1, 0.0, above), jnp.where(index == 0, 0.0, below)


def upward_kernel(
    offs_hbm, q_hbm, sphere_hbm, uinv_hbm, dinv_hbm, offs_ref, q_ref, dinv_ref, g_ref, u_ref, *rest
):
    *packets, sphere_ref, uinv_ref, check_ref, wide_ref, sems = rest
    copies = [
        pltpu.make_async_copy(source, target, sems.at[n])
        for n, (source, target) in enumerate(
            (
                (offs_hbm, offs_ref),
                (q_hbm, q_ref),
                (sphere_hbm, sphere_ref),
                (uinv_hbm, uinv_ref),
                (dinv_hbm, dinv_ref),
            )
        )
    ]
    for copy in copies:
        copy.start()
    _, lx, ly, lanes = offs_ref.shape
    lz = lanes // BODIES
    half = ly // 2
    points = uinv_ref.shape[0]
    even = lax.axis_index("gy") % 2 == 0
    segment = (
        lax.broadcasted_iota(jnp.int32, (8, lanes), 1) // BODIES
        == lax.broadcasted_iota(jnp.int32, (8, lanes), 0)
    ).astype(BF16)
    wide_ref[...] = jnp.zeros_like(wide_ref)
    column = lax.broadcasted_iota(jnp.int32, (2 * points, 2 * points), 1)
    within = column % points
    wanted = column - within + jnp.where(within < points // 2, 2 * within, 2 * within - points + 1)
    shuffle = (lax.broadcasted_iota(jnp.int32, (2 * points, 2 * points), 0) == wanted).astype(BF16)
    for copy in copies[:3]:
        copy.wait()
    sphere = sphere_ref[...]
    for c in range(4):
        for x in range(lx):
            low, high = [
                offs_ref[c, x, pl.ds(y, 1), :] if c < 3 else q_ref[x, pl.ds(y, 1), :] for y in (0, ly - 1)
            ]
            put(packets, pl.ds(lx * lz + c * lx + x, 1), even, low, high)
    for x in range(lx):
        for pair in range(half):
            parts = []
            for y in (2 * pair, 2 * pair + 1):
                kernel = surface_green(sphere, offs_ref, x, y)
                g_ref[x * ly + y] = kernel
                parts.append(kernel * q_ref[x, pl.ds(y, 1), :])
            high, low = split(jnp.concatenate(parts, axis=0))
            sums = lax.dot_general(segment, high, NT, preferred_element_type=F32)
            sums = sums + lax.dot_general(segment, low, NT, preferred_element_type=F32)
            check_ref[pl.ds((x * half + pair) * lz, lz), :] = sums[:lz]
    copies[3].wait()
    wide_ref[:points, :points] = uinv_ref[...]
    wide_ref[points:, points:] = uinv_ref[...]
    density = jnp.dot(
        check_ref[...], wide_ref[...], precision=lax.Precision.HIGHEST, preferred_element_type=F32
    ).astype(BF16)
    u_ref[...] = jnp.dot(density, shuffle, preferred_element_type=F32)
    for x in range(lx):
        low = u_ref[pl.ds(x * half * lz, lz), :]
        high = u_ref[pl.ds((x * half + half - 1) * lz, lz), :]
        put(packets, pl.ds(x * lz, lz), even, low, high)
    copies[4].wait()


def relay(t_ref, copies, w_ref, rows_ref):
    count, width = t_ref.shape
    groups = width // 128
    stride = rows_ref.shape[0] // groups
    points = math.isqrt(width)
    half = points // 2
    order = numbering()
    for a in range(groups):
        if a % (groups // len(copies)) == 0:
            copies[a // (groups // len(copies))].wait()
        rows_ref[pl.ds(a * stride, count), :] = t_ref[:, a * 128 : (a + 1) * 128].astype(F32)
    left = lax.broadcasted_iota(jnp.int32, (groups, 128), 1) < points
    zero = jnp.zeros((groups, 128), F32)
    for ox in range(SPAN):
        for oy in range(SPAN):
            for k in range((SPAN + 1) // 2):
                loaded = []
                for oz in (2 * k, 2 * k + 1):
                    at = order.get((ox - REACH, oy - REACH, oz - REACH))
                    loaded.append(zero if at is None else rows_ref[pl.ds(at, groups, stride=stride), :])
                one, two = loaded
                even = jnp.where(left, one, pltpu.roll(two, points, 1))
                odd = jnp.where(left, pltpu.roll(one, points, 1), two)
                at = slice(k * 128, (k + 1) * 128)
                w_ref[ox, pl.ds(oy * points, half), at] = even.astype(BF16)
                w_ref[ox, pl.ds(oy * points + half, half), at] = odd.astype(BF16)


def zpack_kernel(count, offs_ref, q_ref, u_ref, *rest):
    received, (d_ref, r_ref, *packets) = rest[:count], rest[count:]
    _, lx, ly, lanes = offs_ref.shape
    lz = lanes // BODIES
    half = ly // 2
    wide = ly + 2
    above, below = get(received, "gy")
    even = lax.axis_index("gz") % 2 == 0
    for x in range(lx):
        at = x * (half + 2) * lz
        d_ref[pl.ds(at, lz), :] = below[x * lz : (x + 1) * lz]
        d_ref[pl.ds(at + lz, half * lz), :] = u_ref[pl.ds(x * half * lz, half * lz), :]
        d_ref[pl.ds(at + (half + 1) * lz, lz), :] = above[x * lz : (x + 1) * lz]
        for c in range(4):
            row = lx * lz + c * lx + x
            r_ref[c, pl.ds(x * wide, 1), :] = below[row : row + 1]
            r_ref[c, pl.ds(x * wide + 1, ly), :] = offs_ref[c, x] if c < 3 else q_ref[x]
            r_ref[c, pl.ds(x * wide + ly + 1, 1), :] = above[row : row + 1]
    for g in range(lx * (half + 2)):
        put(packets, pl.ds(g * 2, 2), even, d_ref[pl.ds(g * lz, 2), :], d_ref[pl.ds(g * lz + lz - 2, 2), :])
    spot = lax.broadcasted_iota(jnp.int32, (lx, lanes), 1) // BODIES
    base = lx * (half + 2) * 2
    for c in range(4):
        rows = [r_ref[c, pl.ds(j, lx, stride=wide), :] for j in range(wide)]
        for pack in range(half):
            low = high = None
            for j in range(4):
                row = rows[2 * pack + j]
                first = pltpu.roll(row, j * BODIES, 1) if j else row
                last = pltpu.roll(row, (j + 1) % 4 * BODIES, 1) if (j + 1) % 4 else row
                low = first if low is None else jnp.where(spot == j, first, low)
                high = last if high is None else jnp.where(spot == j, last, high)
            put(packets, pl.ds(base + (c * half + pack) * lx, lx), even, low, high)


def xpack_kernel(count, d_ref, r_ref, *rest):
    received, (e_ref, zl_ref, zh_ref, *packets) = rest[:count], rest[count:]
    groups = e_ref.shape[0]
    lx = zl_ref.shape[1] // 2
    pairs = groups // lx
    half = pairs - 2
    wide = 2 * half + 2
    lz = d_ref.shape[0] // groups
    above, below = get(received, "gz")
    even = lax.axis_index("gx") % 2 == 0
    for g in range(groups):
        e_ref[g, pl.ds(0, 2), :] = below[g * 2 : g * 2 + 2]
        e_ref[g, pl.ds(2, lz), :] = d_ref[pl.ds(g * lz, lz), :]
        e_ref[g, pl.ds(2 + lz, 2), :] = above[g * 2 : g * 2 + 2]
    base = groups * 2
    for c in range(4):
        zl_ref[c] = below[base + c * half * lx : base + (c + 1) * half * lx]
        zh_ref[c] = above[base + c * half * lx : base + (c + 1) * half * lx]
    deep = lz + 4
    for n in range(2 * pairs):
        put(packets, pl.ds(n * deep, deep), even, e_ref[n], e_ref[groups - 2 * pairs + n])
    base = 2 * pairs * deep
    for c in range(4):
        low, high = r_ref[c, pl.ds(0, wide), :], r_ref[c, pl.ds((lx - 1) * wide, wide), :]
        put(packets, pl.ds(base + c * wide, wide), even, low, high)
    base = base + 4 * wide
    for end, ref in enumerate((zl_ref, zh_ref)):
        for c in range(4):
            for pack in range(half):
                low, high = ref[c, pl.ds(pack * lx, 1), :], ref[c, pl.ds(pack * lx + lx - 1, 1), :]
                put(packets, pl.ds(base + (end * 4 + c) * half + pack, 1), even, low, high)


def turn(offs_ref, x):
    _, _, ly, lanes = offs_ref.shape
    lead = lax.broadcasted_iota(jnp.int32, (ly, lanes), 0).astype(F32)
    spots = (lax.broadcasted_iota(jnp.int32, (ly, lanes), 1) // BODIES).astype(F32)
    places = [offs_ref[0, x] + float(x), offs_ref[1, x] + lead, offs_ref[2, x] + spots]
    return jnp.concatenate(places + [places[0]], axis=0).T


def pick(turned, ly, y, z):
    return [turned[z * BODIES : (z + 1) * BODIES, c * ly + y : c * ly + y + 1] for c in range(3)]


def attract(total, target, source, weight, own=False):
    square = None
    for t, s in zip(target, source):
        delta = t - s
        square = delta * delta if square is None else square + delta * delta
    inverse = lax.rsqrt(square)
    if own:
        inverse = jnp.where(square > 0.0, inverse, 0.0)
    term = inverse * weight
    return term if total is None else total + term


def lane_sum(ones, parts):
    high, low = split(jnp.concatenate(parts, axis=0))
    out = lax.dot_general(ones, high, NT, preferred_element_type=F32)
    return (out + lax.dot_general(ones, low, NT, preferred_element_type=F32))[:1]


def spans(value, spot, lz):
    return [jnp.where((spot >= z - 1) & (spot <= z + 1), value, 0.0) for z in range(lz)]


def gather(out_ref, n, y, turned, lz, rows):
    _, ly, lanes = out_ref.shape
    ones = jnp.ones((8, lanes), BF16)
    parts = []
    for z in range(lz):
        target = pick(turned, ly, y, z)
        total = None
        for source, weight, own in rows(z):
            total = attract(total, target, source, weight, own)
        parts.append(jnp.zeros((BODIES, lanes), F32) if total is None else total)
    out_ref[n, pl.ds(y, 1), :] = lane_sum(ones, parts)


def row_source(ref, at, z, own=False):
    return [ref[c, at, :] for c in range(3)], ref[3 + z, at, :], own


def edge_kernel(t_hbm, after_ref, offs_ref, q_ref, out_ref, w_ref, win_ref, t_ref, rows_ref, sems):
    chunks = sems.shape[0]
    cut = t_ref.shape[1] // chunks
    copies = [
        pltpu.make_async_copy(
            t_hbm.at[:, pl.ds(n * cut, cut)], t_ref.at[:, pl.ds(n * cut, cut)], sems.at[n]
        )
        for n in range(chunks)
    ]
    for copy in copies:
        copy.start()
    _, lx, ly, lanes = offs_ref.shape
    lz = lanes // BODIES
    spot = lax.broadcasted_iota(jnp.int32, (ly, lanes), 1) // BODIES
    lead = lax.broadcasted_iota(jnp.int32, (ly, lanes), 0)
    for x in range(lx):
        at = pl.ds(x * ly, ly)
        shift = [float(x), lead.astype(F32), spot.astype(F32)]
        for c in range(3):
            win_ref[c, at, :] = offs_ref[c, x] + shift[c]
        for z, value in enumerate(spans(q_ref[x], spot, lz)):
            win_ref[3 + z, at, :] = value
    for n, x in enumerate((0, lx - 1)):
        turned = turn(offs_ref, x)
        for y in range(ly):

            def rows(z):
                for xx in range(max(x - 1, 0), min(x + 2, lx)):
                    for yy in range(max(y - 1, 0), min(y + 2, ly)):
                        yield row_source(win_ref, pl.ds(xx * ly + yy, 1), z, xx == x and yy == y)

            gather(out_ref, n, y, turned, lz, rows)
    relay(t_ref, copies, w_ref, rows_ref)


def strips(r_ref, win_ref, wide, lz):
    _, rows, lanes = r_ref.shape
    place = lax.broadcasted_iota(jnp.int32, (rows, lanes), 0)
    spot = lax.broadcasted_iota(jnp.int32, (rows, lanes), 1) // BODIES
    base = [place // wide, place % wide - 1, spot]
    for c in range(3):
        win_ref[c] = r_ref[c] + base[c].astype(F32)
    for z, value in enumerate(spans(r_ref[3], spot, lz)):
        win_ref[3 + z] = value


def inner_kernel(offs_ref, r_ref, out_ref, win_ref):
    _, lx, ly, lanes = offs_ref.shape
    lz = lanes // BODIES
    wide = ly + 2
    strips(r_ref, win_ref, wide, lz)
    for x in range(1, lx - 1):
        turned = turn(offs_ref, x)
        for y in range(ly):

            def rows(z):
                for xx in range(x - 1, x + 2):
                    for dy in range(3):
                        yield row_source(win_ref, pl.ds(xx * wide + y + dy, 1), z, xx == x and dy == 1)

            gather(out_ref, x - 1, y, turned, lz, rows)


def ends_kernel(offs_ref, r_ref, zl_ref, zh_ref, out_ref, win_ref, end_ref):
    _, lx, ly, lanes = offs_ref.shape
    lz = lanes // BODIES
    half = ly // 2
    wide = ly + 2
    strips(r_ref, win_ref, wide, lz)
    end_windows(zl_ref, -1.0, end_ref, 0, lz, half)
    end_windows(zh_ref, float(lz), end_ref, 5, lz, half)
    for x in range(lx):
        turned = turn(offs_ref, x)
        for y in range(ly):

            def rows(z):
                nearby = range(max(x - 1, 0), min(x + 2, lx))
                if x in (0, lx - 1):
                    for yy in (y, y + 2):
                        if yy in (0, ly + 1):
                            for xx in nearby:
                                yield row_source(win_ref, pl.ds(xx * wide + yy, 1), z)
                for end in range(2):
                    if z == (0 if end == 0 else lz - 1):
                        for xx in nearby:
                            at = pl.ds(y // 2 * lx + xx, 1)
                            source = [end_ref[end * 5 + c, at, :] for c in range(3)]
                            yield source, end_ref[end * 5 + 3 + y % 2, at, :], False

            gather(out_ref, x, y, turned, lz, rows)


def end_windows(end_ref, base, win_ref, at, lz, half):
    rows = end_ref.shape[1]
    lanes = end_ref.shape[2]
    count = rows // half
    place = lax.broadcasted_iota(jnp.int32, (rows, lanes), 0)
    spot = lax.broadcasted_iota(jnp.int32, (rows, lanes), 1) // BODIES
    shift = [(place % count).astype(F32), (spot + 2 * (place // count) - 1).astype(F32), base]
    for c in range(3):
        win_ref[at + c] = end_ref[c] + shift[c]
    for s in range(2):
        win_ref[at + 3 + s] = jnp.where((spot >= s) & (spot < s + 3), end_ref[3], 0.0)


def final_kernel(count, offs_ref, e_ref, near_edge_ref, near_in_ref, near_end_ref, w_ref, dinv_ref, g_ref, *rest):
    received, rest = rest[:count], rest[count:]
    out_ref, left_ref, acc_ref, dense_ref, sum_ref, side_ref, edge_ref = rest
    _, lx, ly, lanes = offs_ref.shape
    lz = lanes // BODIES
    points = dinv_ref.shape[0]
    half = ly // 2
    pairs = half + 2
    wide = ly + 2
    deep = lz + 4
    block = half * deep
    width = (SPAN - 1) * points
    above, below = get(received, "gx")

    def plane(x, pair):
        if x < 2:
            return below[(x * pairs + pair) * deep : (x * pairs + pair + 1) * deep]
        if x < lx + 2:
            return e_ref[(x - 2) * pairs + pair]
        return above[((x - lx - 2) * pairs + pair) * deep : ((x - lx - 2) * pairs + pair + 1) * deep]

    for x in range(lx + 4):
        planes = [plane(x, pair) for pair in range(pairs)]
        for j in range(SPAN // 2):
            left_ref[pl.ds(x * block, block), j * 128 : (j + 1) * 128] = jnp.concatenate(
                planes[j : j + half], axis=0
            ).astype(BF16)
    spot = lax.broadcasted_iota(jnp.int32, (wide, lanes), 1) // BODIES
    lead = lax.broadcasted_iota(jnp.int32, (wide, lanes), 0).astype(F32) - 1.0
    base = 2 * pairs * deep
    ends = base + 4 * wide
    for side, value in enumerate((below, above)):
        shift = [-1.0 if side == 0 else float(lx), lead, spot.astype(F32)]
        for c in range(3):
            side_ref[side, c] = value[base + c * wide : base + (c + 1) * wide] + shift[c]
        for z, part in enumerate(spans(value[base + 3 * wide : base + 4 * wide], spot, lz)):
            side_ref[side, 3 + z] = part
    spot = lax.broadcasted_iota(jnp.int32, (half, lanes), 1) // BODIES
    place = lax.broadcasted_iota(jnp.int32, (half, lanes), 0)
    for side, value in enumerate((below, above)):
        for end in range(2):
            shift = [-1.0 if side == 0 else float(lx), (spot + 2 * place - 1).astype(F32), -1.0 if end == 0 else float(lz)]
            for c in range(3):
                at = ends + (end * 4 + c) * half
                edge_ref[side, end * 5 + c] = value[at : at + half] + shift[c]
            at = ends + (end * 4 + 3) * half
            for s in range(2):
                edge_ref[side, end * 5 + 3 + s] = jnp.where((spot >= s) & (spot < s + 3), value[at : at + half], 0.0)


    def side_unit(x, y, turned):
        side = 0 if x == 0 else 1

        def rows(z):
            for dy in range(3):
                at = pl.ds(y + dy, 1)
                yield [side_ref[side, c, at, :] for c in range(3)], side_ref[side, 3 + z, at, :], False
            for end in range(2):
                if z == (0 if end == 0 else lz - 1):
                    at = pl.ds(y // 2, 1)
                    source = [edge_ref[side, end * 5 + c, at, :] for c in range(3)]
                    yield source, edge_ref[side, end * 5 + 3 + y % 2, at, :], False

        gather(out_ref, x, y, turned, lz, rows)

    def units():
        for x in (0, lx - 1):
            turned = turn(offs_ref, x)
            for y in range(ly):
                side_unit(x, y, turned)
                yield

    waiting = units()
    twice = jnp.concatenate([dinv_ref[...]] * 2, axis=0)
    expand = (
        lax.broadcasted_iota(jnp.int32, (lx * half * lz, lx * half * lanes), 1) // BODIES
        == lax.broadcasted_iota(jnp.int32, (lx * half * lz, lx * half * lanes), 0)
    ).astype(BF16)
    lane = lax.broadcasted_iota(jnp.int32, (lz, 128), 1)
    level = lax.broadcasted_iota(jnp.int32, (lz, 128), 0)
    for cy in range(2):
        total = [None] * lx
        for ox in range(-REACH, REACH + 1):
            chosen = [b for b in range(lx) if not (ox == -REACH and b % 2 == 0) and not (ox == REACH and b % 2 == 1)]
            parts = [left_ref[pl.ds((b + ox + 2) * block, block), :] for b in chosen]
            lhs = jnp.concatenate(parts, axis=0)
            rhs = w_ref[ox + REACH, pl.ds((1 - cy) * points, width), :]
            got = jnp.dot(lhs, rhs, preferred_element_type=F32)
            for n, b in enumerate(chosen):
                piece = got[n * block : (n + 1) * block]
                total[b] = piece if total[b] is None else total[b] + piece
            next(waiting, None)
        for b in range(lx):
            for p in range(half):
                acc_ref[b * half + p, pl.ds(8, deep), :] = total[b][p * deep : (p + 1) * deep]
        for g in range(lx * half):
            folded = None
            for k in range((SPAN + 1) // 2):
                shown = []
                for oz in (2 * k - REACH, 2 * k + 1 - REACH):
                    if oz > REACH:
                        shown.append(jnp.zeros((lz, 128), F32))
                        continue
                    got = acc_ref[g, pl.ds(8 + oz + 2, lz), k * 128 : (k + 1) * 128]
                    if oz == -REACH:
                        got = jnp.where(level % 2 == 1, got, 0.0)
                    if oz == REACH:
                        got = jnp.where(level % 2 == 0, got, 0.0)
                    shown.append(got)
                both = jnp.where(lane < points, shown[0], shown[1])
                folded = both if folded is None else folded + both
            sum_ref[pl.ds(g * lz, lz), :] = folded
        dense = jnp.dot(sum_ref[...], twice, precision=lax.Precision.HIGHEST, preferred_element_type=F32)
        high, low = split(dense.T)
        spread = jnp.dot(high, expand, preferred_element_type=F32)
        spread = spread + jnp.dot(low, expand, preferred_element_type=F32)
        for g in range(lx * half):
            dense_ref[g, cy] = spread[:, g * lanes : (g + 1) * lanes]

    for _ in waiting:
        pass
    for x in range(lx):
        for y in range(ly):
            far = jnp.sum(g_ref[x * ly + y] * dense_ref[x * half + y // 2, y % 2], axis=0, keepdims=True)
            at = pl.ds(y, 1)
            total = near_end_ref[x, at, :] + far
            if x in (0, lx - 1):
                total = total + out_ref[x, at, :] + near_edge_ref[0 if x == 0 else 1, at, :]
            else:
                total = total + near_in_ref[x - 1, at, :]
            out_ref[x, at, :] = total


def rounds_of(axis):
    return [[(i, i + 1) for i in range(start, lax.axis_size(axis) - 1, 2)] for start in range(2)]


def rounds_in(axis):
    return max(1, sum(1 for pairs in rounds_of(axis) if pairs))


def exchange(packets, axis):
    count = lax.axis_size(axis)
    planes = lax.axis_size("gx")
    results = []
    for packet, pairs in zip(packets, rounds_of(axis)):
        swaps = [swap for i, j in pairs for swap in ((i, j), (j, i))]
        idle = sorted(set(range(count)) - {i for i, _ in swaps})
        if not idle or axis == "gx" or planes % 2:
            results.append(lax.ppermute(packet, axis, swaps))
            continue
        swaps = [(plane * count + i, plane * count + j) for plane in range(planes) for i, j in swaps]
        swaps += [(plane * count + i, (plane ^ 1) * count + i) for plane in range(planes) for i in idle]
        results.append(lax.ppermute(packet, ("gx", axis), swaps))
    return results


def call(kernel, outs, args, scratch=(), limit=8, name=None, spaces=None):
    spec = pl.BlockSpec(memory_space=pltpu.VMEM)
    return pl.pallas_call(
        kernel,
        out_shape=outs,
        in_specs=[pl.BlockSpec(memory_space=space) for space in spaces] if spaces else [spec] * len(args),
        out_specs=[spec] * len(outs),
        scratch_shapes=list(scratch),
        compiler_params=pltpu.CompilerParams(vmem_limit_bytes=limit << 20),
        name=name,
    )(*args)


def shaped(*shape):
    return jax.ShapeDtypeStruct(shape, F32)


def per_device(offsets, charges, up_inverse, translations, down_inverse):
    points = up_inverse.shape[0]
    _, lx, ly, lanes = offsets.shape
    lz = lanes // BODIES
    half = ly // 2
    pairs = half + 2
    wide = ly + 2
    deep = lz + 4
    rounds = {axis: rounds_in(axis) for axis in ("gx", "gy", "gz")}
    sphere = jnp.asarray(surface(points))
    boxes = lx * half * lz
    packet = shaped(lx * lz + 4 * lx, lanes)
    inputs = [
        pltpu.with_memory_space_constraint(value, pltpu.HBM)
        for value in (offsets, charges, sphere, up_inverse, down_inverse)
    ]
    offsets, charges, down_inverse, surfaces, density, *packets = call(
        upward_kernel,
        [shaped(*value.shape) for value in (offsets, charges, down_inverse)]
        + [shaped(lx * ly, points, lanes), shaped(boxes, 2 * points)]
        + [packet] * rounds["gy"],
        inputs,
        [
            pltpu.VMEM(sphere.shape, F32),
            pltpu.VMEM(up_inverse.shape, F32),
            pltpu.VMEM((boxes, 2 * points), F32),
            pltpu.VMEM((2 * points, 2 * points), F32),
            pltpu.SemaphoreType.DMA((5,)),
        ],
        4,
        "upward",
        [pltpu.HBM] * 5,
    )
    received = exchange(packets, "gy")
    count, width = translations.shape
    stride = count // 2 * 2 + 1
    edge, weights = call(
        edge_kernel,
        [
            shaped(2, ly, lanes),
            jax.ShapeDtypeStruct((SPAN, SPAN * points, (SPAN + 1) * points), BF16),
        ],
        (pltpu.with_memory_space_constraint(translations, pltpu.HBM), density, offsets, charges),
        [
            pltpu.VMEM((3 + lz, lx * ly, lanes), F32),
            pltpu.VMEM(translations.shape, BF16),
            pltpu.VMEM((width // 128 * stride, 128), F32),
            pltpu.SemaphoreType.DMA((4,)),
        ],
        24,
        "near_edge",
        [pltpu.HBM, pl.ANY, pltpu.VMEM, pltpu.VMEM],
    )
    received, edge, weights = lax.optimization_barrier((received, edge, weights))
    packet = shaped(lx * pairs * 2 + 4 * half * lx, lanes)
    dense, body, *packets = call(
        functools.partial(zpack_kernel, len(received)),
        [shaped(lx * pairs * lz, 2 * points), shaped(4, lx * wide, lanes)] + [packet] * rounds["gz"],
        (offsets, charges, density, *received),
        name="zpack",
    )
    packets, body = lax.optimization_barrier((packets, body))
    received = exchange(packets, "gz")
    windows = [pltpu.VMEM((3 + lz, lx * wide, lanes), F32)]
    (inner,) = call(inner_kernel, [shaped(lx - 2, ly, lanes)], (offsets, body), windows, name="near_inner")
    received, inner = lax.optimization_barrier((received, inner))
    packet = shaped(2 * pairs * deep + 4 * wide + 8 * half, lanes)
    end = shaped(4, half * lx, lanes)
    dense, low, high, *packets = call(
        functools.partial(xpack_kernel, len(received)),
        [shaped(lx * pairs, deep, 2 * points), end, end] + [packet] * rounds["gx"],
        (dense, body, *received),
        name="xpack",
    )
    packets, body = lax.optimization_barrier((packets, body))
    received = exchange(packets, "gx")
    (ends,) = call(
        ends_kernel,
        [shaped(lx, ly, lanes)],
        (offsets, body, low, high),
        windows + [pltpu.VMEM((10, half * lx, lanes), F32)],
        name="near_ends",
    )
    received, ends = lax.optimization_barrier((received, ends))
    (out,) = call(
        functools.partial(final_kernel, len(received)),
        [shaped(lx, ly, lanes)],
        (offsets, dense, edge, inner, ends, weights, down_inverse, surfaces, *received),
        [
            pltpu.VMEM(((lx + 4) * half * deep, 6 * points), BF16),
            pltpu.VMEM((lx * half, 8 + deep + 8, (SPAN + 1) * points), F32),
            pltpu.VMEM((lx * half, 2, points, lanes), F32),
            pltpu.VMEM((boxes, 2 * points), F32),
            pltpu.VMEM((2, 3 + lz, wide, lanes), F32),
            pltpu.VMEM((2, 10, half, lanes), F32),
        ],
        24,
        "final",
    )
    return out


def solution(mesh):
    in_specs = (P(None, "gx", "gy", "gz"), P("gx", "gy", "gz"), P(), P(), P())
    out_specs = P("gx", "gy", "gz")
    return jax.shard_map(
        per_device, mesh=mesh, in_specs=in_specs, out_specs=out_specs, check_vma=False
    )
```

```python
import functools
import math

import jax
import jax.numpy as jnp
import numpy as np
from jax import lax
from jax.experimental import pallas as pl
from jax.experimental.pallas import tpu as pltpu
from jax.sharding import PartitionSpec as P

BODIES = 32
RADIUS = 0.9
REACH = 3
SPAN = 2 * REACH + 1
F32 = jnp.float32
BF16 = jnp.bfloat16
NT = (((1,), (1,)), ((), ()))


def surface(points):
    number = np.arange(points).astype(np.float32)
    height = np.float32(1.0) - (np.float32(2.0) * number + np.float32(1.0)) / np.float32(points)
    across = np.sqrt(np.float32(1.0) - height * height)
    turned = number * np.float32(math.pi * (3.0 - math.sqrt(5.0)))
    columns = np.zeros((points, 128), np.float32)
    columns[:, 0] = RADIUS * across * np.cos(turned)
    columns[:, 1] = RADIUS * across * np.sin(turned)
    columns[:, 2] = RADIUS * height
    return columns


def numbering():
    table, count = {}, 0
    for ox in range(-REACH, REACH + 1):
        for oy in range(-REACH, REACH + 1):
            for oz in range(-REACH, REACH + 1):
                if max(abs(ox), abs(oy), abs(oz)) >= 2:
                    table[ox, oy, oz] = count
                    count += 1
    return table


def split(value):
    high = value.astype(BF16)
    return high, (value - high.astype(F32)).astype(BF16)


def surface_green(sphere, offs_ref, x, y):
    rows = [offs_ref[c, x, pl.ds(y, 1), :] - 0.5 for c in range(3)]
    square = None
    for c in range(3):
        delta = sphere[:, c : c + 1] - rows[c]
        square = delta * delta if square is None else square + delta * delta
    return lax.rsqrt(square)


def select(even, one, two):
    return jnp.where(even, one, two), jnp.where(even, two, one)


def put(refs, at, even, low, high):
    refs[0][at, :] = jnp.where(even, high, low)
    for ref in refs[1:]:
        ref[at, :] = jnp.where(even, low, high)


def get(refs, axis):
    index = lax.axis_index(axis)
    one = refs[0][...]
    above, below = select(index % 2 == 0, one, refs[1][...] if len(refs) > 1 else one)
    return jnp.where(index == lax.axis_size(axis) - 1, 0.0, above), jnp.where(index == 0, 0.0, below)


def upward_kernel(
    offs_hbm, q_hbm, sphere_hbm, uinv_hbm, dinv_hbm, offs_ref, q_ref, dinv_ref, g_ref, u_ref, *rest
):
    *packets, sphere_ref, uinv_ref, check_ref, wide_ref, sems = rest
    copies = [
        pltpu.make_async_copy(source, target, sems.at[n])
        for n, (source, target) in enumerate(
            (
                (offs_hbm, offs_ref),
                (q_hbm, q_ref),
                (sphere_hbm, sphere_ref),
                (uinv_hbm, uinv_ref),
                (dinv_hbm, dinv_ref),
            )
        )
    ]
    for copy in copies:
        copy.start()
    _, lx, ly, lanes = offs_ref.shape
    lz = lanes // BODIES
    half = ly // 2
    points = uinv_ref.shape[0]
    even = lax.axis_index("gy") % 2 == 0
    segment = (
        lax.broadcasted_iota(jnp.int32, (8, lanes), 1) // BODIES
        == lax.broadcasted_iota(jnp.int32, (8, lanes), 0)
    ).astype(BF16)
    wide_ref[...] = jnp.zeros_like(wide_ref)
    column = lax.broadcasted_iota(jnp.int32, (2 * points, 2 * points), 1)
    within = column % points
    wanted = column - within + jnp.where(within < points // 2, 2 * within, 2 * within - points + 1)
    shuffle = (lax.broadcasted_iota(jnp.int32, (2 * points, 2 * points), 0) == wanted).astype(BF16)
    for copy in copies[:3]:
        copy.wait()
    sphere = sphere_ref[...]
    for c in range(4):
        for x in range(lx):
            low, high = [
                offs_ref[c, x, pl.ds(y, 1), :] if c < 3 else q_ref[x, pl.ds(y, 1), :] for y in (0, ly - 1)
            ]
            put(packets, pl.ds(lx * lz + c * lx + x, 1), even, low, high)
    for x in range(lx):
        for pair in range(half):
            parts = []
            for y in (2 * pair, 2 * pair + 1):
                kernel = surface_green(sphere, offs_ref, x, y)
                g_ref[x * ly + y] = kernel
                parts.append(kernel * q_ref[x, pl.ds(y, 1), :])
            high, low = split(jnp.concatenate(parts, axis=0))
            sums = lax.dot_general(segment, high, NT, preferred_element_type=F32)
            sums = sums + lax.dot_general(segment, low, NT, preferred_element_type=F32)
            check_ref[pl.ds((x * half + pair) * lz, lz), :] = sums[:lz]
    copies[3].wait()
    wide_ref[:points, :points] = uinv_ref[...]
    wide_ref[points:, points:] = uinv_ref[...]
    density = jnp.dot(
        check_ref[...], wide_ref[...], precision=lax.Precision.HIGHEST, preferred_element_type=F32
    ).astype(BF16)
    u_ref[...] = jnp.dot(density, shuffle, preferred_element_type=F32)
    for x in range(lx):
        low = u_ref[pl.ds(x * half * lz, lz), :]
        high = u_ref[pl.ds((x * half + half - 1) * lz, lz), :]
        put(packets, pl.ds(x * lz, lz), even, low, high)
    copies[4].wait()


def relay(t_ref, copies, w_ref, rows_ref):
    count, width = t_ref.shape
    groups = width // 128
    stride = rows_ref.shape[0] // groups
    points = math.isqrt(width)
    half = points // 2
    order = numbering()
    for a in range(groups):
        if a % (groups // len(copies)) == 0:
            copies[a // (groups // len(copies))].wait()
        rows_ref[pl.ds(a * stride, count), :] = t_ref[:, a * 128 : (a + 1) * 128].astype(F32)
    left = lax.broadcasted_iota(jnp.int32, (groups, 128), 1) < points
    zero = jnp.zeros((groups, 128), F32)
    for ox in range(SPAN):
        for oy in range(SPAN):
            for k in range((SPAN + 1) // 2):
                loaded = []
                for oz in (2 * k, 2 * k + 1):
                    at = order.get((ox - REACH, oy - REACH, oz - REACH))
                    loaded.append(zero if at is None else rows_ref[pl.ds(at, groups, stride=stride), :])
                one, two = loaded
                even = jnp.where(left, one, pltpu.roll(two, points, 1))
                odd = jnp.where(left, pltpu.roll(one, points, 1), two)
                at = slice(k * 128, (k + 1) * 128)
                w_ref[ox, pl.ds(oy * points, half), at] = even.astype(BF16)
                w_ref[ox, pl.ds(oy * points + half, half), at] = odd.astype(BF16)


def zpack_kernel(count, offs_ref, q_ref, u_ref, *rest):
    received, (d_ref, r_ref, *packets) = rest[:count], rest[count:]
    _, lx, ly, lanes = offs_ref.shape
    lz = lanes // BODIES
    half = ly // 2
    wide = ly + 2
    above, below = get(received, "gy")
    even = lax.axis_index("gz") % 2 == 0
    for x in range(lx):
        at = x * (half + 2) * lz
        d_ref[pl.ds(at, lz), :] = below[x * lz : (x + 1) * lz]
        d_ref[pl.ds(at + lz, half * lz), :] = u_ref[pl.ds(x * half * lz, half * lz), :]
        d_ref[pl.ds(at + (half + 1) * lz, lz), :] = above[x * lz : (x + 1) * lz]
        for c in range(4):
            row = lx * lz + c * lx + x
            r_ref[c, pl.ds(x * wide, 1), :] = below[row : row + 1]
            r_ref[c, pl.ds(x * wide + 1, ly), :] = offs_ref[c, x] if c < 3 else q_ref[x]
            r_ref[c, pl.ds(x * wide + ly + 1, 1), :] = above[row : row + 1]
    for g in range(lx * (half + 2)):
        put(packets, pl.ds(g * 2, 2), even, d_ref[pl.ds(g * lz, 2), :], d_ref[pl.ds(g * lz + lz - 2, 2), :])
    spot = lax.broadcasted_iota(jnp.int32, (lx, lanes), 1) // BODIES
    base = lx * (half + 2) * 2
    for c in range(4):
        rows = [r_ref[c, pl.ds(j, lx, stride=wide), :] for j in range(wide)]
        for pack in range(half):
            low = high = None
            for j in range(4):
                row = rows[2 * pack + j]
                first = pltpu.roll(row, j * BODIES, 1) if j else row
                last = pltpu.roll(row, (j + 1) % 4 * BODIES, 1) if (j + 1) % 4 else row
                low = first if low is None else jnp.where(spot == j, first, low)
                high = last if high is None else jnp.where(spot == j, last, high)
            put(packets, pl.ds(base + (c * half + pack) * lx, lx), even, low, high)


def xpack_kernel(count, d_ref, r_ref, *rest):
    received, (e_ref, zl_ref, zh_ref, *packets) = rest[:count], rest[count:]
    groups = e_ref.shape[0]
    lx = zl_ref.shape[1] // 2
    pairs = groups // lx
    half = pairs - 2
    wide = 2 * half + 2
    lz = d_ref.shape[0] // groups
    above, below = get(received, "gz")
    even = lax.axis_index("gx") % 2 == 0
    for g in range(groups):
        e_ref[g, pl.ds(0, 2), :] = below[g * 2 : g * 2 + 2]
        e_ref[g, pl.ds(2, lz), :] = d_ref[pl.ds(g * lz, lz), :]
        e_ref[g, pl.ds(2 + lz, 2), :] = above[g * 2 : g * 2 + 2]
    base = groups * 2
    for c in range(4):
        zl_ref[c] = below[base + c * half * lx : base + (c + 1) * half * lx]
        zh_ref[c] = above[base + c * half * lx : base + (c + 1) * half * lx]
    deep = lz + 4
    for n in range(2 * pairs):
        put(packets, pl.ds(n * deep, deep), even, e_ref[n], e_ref[groups - 2 * pairs + n])
    base = 2 * pairs * deep
    for c in range(4):
        low, high = r_ref[c, pl.ds(0, wide), :], r_ref[c, pl.ds((lx - 1) * wide, wide), :]
        put(packets, pl.ds(base + c * wide, wide), even, low, high)
    base = base + 4 * wide
    for end, ref in enumerate((zl_ref, zh_ref)):
        for c in range(4):
            for pack in range(half):
                low, high = ref[c, pl.ds(pack * lx, 1), :], ref[c, pl.ds(pack * lx + lx - 1, 1), :]
                put(packets, pl.ds(base + (end * 4 + c) * half + pack, 1), even, low, high)


def turn(offs_ref, x):
    _, _, ly, lanes = offs_ref.shape
    lead = lax.broadcasted_iota(jnp.int32, (ly, lanes), 0).astype(F32)
    spots = (lax.broadcasted_iota(jnp.int32, (ly, lanes), 1) // BODIES).astype(F32)
    places = [offs_ref[0, x] + float(x), offs_ref[1, x] + lead, offs_ref[2, x] + spots]
    return jnp.concatenate(places + [places[0]], axis=0).T


def pick(turned, ly, y, z):
    return [turned[z * BODIES : (z + 1) * BODIES, c * ly + y : c * ly + y + 1] for c in range(3)]


def attract(total, target, source, weight, own=False):
    square = None
    for t, s in zip(target, source):
        delta = t - s
        square = delta * delta if square is None else square + delta * delta
    inverse = lax.rsqrt(square)
    if own:
        inverse = jnp.where(square > 0.0, inverse, 0.0)
    term = inverse * weight
    return term if total is None else total + term


def lane_sum(ones, parts):
    high, low = split(jnp.concatenate(parts, axis=0))
    out = lax.dot_general(ones, high, NT, preferred_element_type=F32)
    return (out + lax.dot_general(ones, low, NT, preferred_element_type=F32))[:1]


def spans(value, spot, lz):
    return [jnp.where((spot >= z - 1) & (spot <= z + 1), value, 0.0) for z in range(lz)]


def gather(out_ref, n, y, turned, lz, rows):
    _, ly, lanes = out_ref.shape
    ones = jnp.ones((8, lanes), BF16)
    parts = []
    for z in range(lz):
        target = pick(turned, ly, y, z)
        total = None
        for source, weight, own in rows(z):
            total = attract(total, target, source, weight, own)
        parts.append(jnp.zeros((BODIES, lanes), F32) if total is None else total)
    out_ref[n, pl.ds(y, 1), :] = lane_sum(ones, parts)


def row_source(ref, at, z, own=False):
    return [ref[c, at, :] for c in range(3)], ref[3 + z, at, :], own


def edge_kernel(t_hbm, after_ref, offs_ref, q_ref, out_ref, w_ref, win_ref, t_ref, rows_ref, sems):
    chunks = sems.shape[0]
    cut = t_ref.shape[1] // chunks
    copies = [
        pltpu.make_async_copy(
            t_hbm.at[:, pl.ds(n * cut, cut)], t_ref.at[:, pl.ds(n * cut, cut)], sems.at[n]
        )
        for n in range(chunks)
    ]
    for copy in copies:
        copy.start()
    _, lx, ly, lanes = offs_ref.shape
    lz = lanes // BODIES
    spot = lax.broadcasted_iota(jnp.int32, (ly, lanes), 1) // BODIES
    lead = lax.broadcasted_iota(jnp.int32, (ly, lanes), 0)
    for x in range(lx):
        at = pl.ds(x * ly, ly)
        shift = [float(x), lead.astype(F32), spot.astype(F32)]
        for c in range(3):
            win_ref[c, at, :] = offs_ref[c, x] + shift[c]
        for z, value in enumerate(spans(q_ref[x], spot, lz)):
            win_ref[3 + z, at, :] = value
    for n, x in enumerate((0, lx - 1)):
        turned = turn(offs_ref, x)
        for y in range(ly):

            def rows(z):
                for xx in range(max(x - 1, 0), min(x + 2, lx)):
                    for yy in range(max(y - 1, 0), min(y + 2, ly)):
                        yield row_source(win_ref, pl.ds(xx * ly + yy, 1), z, xx == x and yy == y)

            gather(out_ref, n, y, turned, lz, rows)
    relay(t_ref, copies, w_ref, rows_ref)


def strips(r_ref, win_ref, wide, lz):
    _, rows, lanes = r_ref.shape
    place = lax.broadcasted_iota(jnp.int32, (rows, lanes), 0)
    spot = lax.broadcasted_iota(jnp.int32, (rows, lanes), 1) // BODIES
    base = [place // wide, place % wide - 1, spot]
    for c in range(3):
        win_ref[c] = r_ref[c] + base[c].astype(F32)
    for z, value in enumerate(spans(r_ref[3], spot, lz)):
        win_ref[3 + z] = value


def inner_kernel(offs_ref, r_ref, out_ref, win_ref):
    _, lx, ly, lanes = offs_ref.shape
    lz = lanes // BODIES
    wide = ly + 2
    strips(r_ref, win_ref, wide, lz)
    for x in range(1, lx - 1):
        turned = turn(offs_ref, x)
        for y in range(ly):

            def rows(z):
                for xx in range(x - 1, x + 2):
                    for dy in range(3):
                        yield row_source(win_ref, pl.ds(xx * wide + y + dy, 1), z, xx == x and dy == 1)

            gather(out_ref, x - 1, y, turned, lz, rows)


def ends_kernel(offs_ref, r_ref, zl_ref, zh_ref, out_ref, win_ref, end_ref):
    _, lx, ly, lanes = offs_ref.shape
    lz = lanes // BODIES
    half = ly // 2
    wide = ly + 2
    strips(r_ref, win_ref, wide, lz)
    end_windows(zl_ref, -1.0, end_ref, 0, lz, half)
    end_windows(zh_ref, float(lz), end_ref, 5, lz, half)
    for x in range(lx):
        turned = turn(offs_ref, x)
        for y in range(ly):

            def rows(z):
                nearby = range(max(x - 1, 0), min(x + 2, lx))
                if x in (0, lx - 1):
                    for yy in (y, y + 2):
                        if yy in (0, ly + 1):
                            for xx in nearby:
                                yield row_source(win_ref, pl.ds(xx * wide + yy, 1), z)
                for end in range(2):
                    if z == (0 if end == 0 else lz - 1):
                        for xx in nearby:
                            at = pl.ds(y // 2 * lx + xx, 1)
                            source = [end_ref[end * 5 + c, at, :] for c in range(3)]
                            yield source, end_ref[end * 5 + 3 + y % 2, at, :], False

            gather(out_ref, x, y, turned, lz, rows)


def end_windows(end_ref, base, win_ref, at, lz, half):
    rows = end_ref.shape[1]
    lanes = end_ref.shape[2]
    count = rows // half
    place = lax.broadcasted_iota(jnp.int32, (rows, lanes), 0)
    spot = lax.broadcasted_iota(jnp.int32, (rows, lanes), 1) // BODIES
    shift = [(place % count).astype(F32), (spot + 2 * (place // count) - 1).astype(F32), base]
    for c in range(3):
        win_ref[at + c] = end_ref[c] + shift[c]
    for s in range(2):
        win_ref[at + 3 + s] = jnp.where((spot >= s) & (spot < s + 3), end_ref[3], 0.0)


def final_kernel(count, offs_ref, e_ref, near_edge_ref, near_in_ref, near_end_ref, w_ref, dinv_ref, g_ref, *rest):
    received, rest = rest[:count], rest[count:]
    out_ref, left_ref, acc_ref, dense_ref, sum_ref, side_ref, edge_ref = rest
    _, lx, ly, lanes = offs_ref.shape
    lz = lanes // BODIES
    points = dinv_ref.shape[0]
    half = ly // 2
    pairs = half + 2
    wide = ly + 2
    deep = lz + 4
    block = half * deep
    above, below = get(received, "gx")

    def plane(x, pair):
        if x < 2:
            return below[(x * pairs + pair) * deep : (x * pairs + pair + 1) * deep]
        if x < lx + 2:
            return e_ref[(x - 2) * pairs + pair]
        return above[((x - lx - 2) * pairs + pair) * deep : ((x - lx - 2) * pairs + pair + 1) * deep]

    side = lax.broadcasted_iota(jnp.int32, (deep, 128), 1) < points
    for x in range(lx + 4):
        planes = [plane(x, pair) for pair in range(pairs)]
        turned = [pltpu.roll(value, points, 1) for value in planes]
        at = pl.ds(x * block, block)
        for j in range(SPAN // 2 + 1):
            early, late = [], []
            for p in range(half):
                before = turned[p + j - 1] if j else 0.0
                after = turned[p + j] if j < SPAN // 2 else 0.0
                early.append(jnp.where(side, before, after))
                late.append(planes[p + j] if j < SPAN // 2 else jnp.zeros((deep, 128), F32))
            left_ref[0, at, j * 128 : (j + 1) * 128] = jnp.concatenate(early, axis=0).astype(BF16)
            left_ref[1, at, j * 128 : (j + 1) * 128] = jnp.concatenate(late, axis=0).astype(BF16)
    spot = lax.broadcasted_iota(jnp.int32, (wide, lanes), 1) // BODIES
    lead = lax.broadcasted_iota(jnp.int32, (wide, lanes), 0).astype(F32) - 1.0
    base = 2 * pairs * deep
    ends = base + 4 * wide
    for side, value in enumerate((below, above)):
        shift = [-1.0 if side == 0 else float(lx), lead, spot.astype(F32)]
        for c in range(3):
            side_ref[side, c] = value[base + c * wide : base + (c + 1) * wide] + shift[c]
        for z, part in enumerate(spans(value[base + 3 * wide : base + 4 * wide], spot, lz)):
            side_ref[side, 3 + z] = part
    spot = lax.broadcasted_iota(jnp.int32, (half, lanes), 1) // BODIES
    place = lax.broadcasted_iota(jnp.int32, (half, lanes), 0)
    for side, value in enumerate((below, above)):
        for end in range(2):
            shift = [-1.0 if side == 0 else float(lx), (spot + 2 * place - 1).astype(F32), -1.0 if end == 0 else float(lz)]
            for c in range(3):
                at = ends + (end * 4 + c) * half
                edge_ref[side, end * 5 + c] = value[at : at + half] + shift[c]
            at = ends + (end * 4 + 3) * half
            for s in range(2):
                edge_ref[side, end * 5 + 3 + s] = jnp.where((spot >= s) & (spot < s + 3), value[at : at + half], 0.0)


    def side_unit(x, y, turned):
        side = 0 if x == 0 else 1

        def rows(z):
            for dy in range(3):
                at = pl.ds(y + dy, 1)
                yield [side_ref[side, c, at, :] for c in range(3)], side_ref[side, 3 + z, at, :], False
            for end in range(2):
                if z == (0 if end == 0 else lz - 1):
                    at = pl.ds(y // 2, 1)
                    source = [edge_ref[side, end * 5 + c, at, :] for c in range(3)]
                    yield source, edge_ref[side, end * 5 + 3 + y % 2, at, :], False

        gather(out_ref, x, y, turned, lz, rows)

    def units():
        for x in (0, lx - 1):
            turned = turn(offs_ref, x)
            for y in range(ly):
                side_unit(x, y, turned)
                yield

    waiting = units()
    twice = jnp.concatenate([dinv_ref[...]] * 2, axis=0)
    expand = (
        lax.broadcasted_iota(jnp.int32, (lx * half * lz, lx * half * lanes), 1) // BODIES
        == lax.broadcasted_iota(jnp.int32, (lx * half * lz, lx * half * lanes), 0)
    ).astype(BF16)
    lane = lax.broadcasted_iota(jnp.int32, (lz, 128), 1)
    level = lax.broadcasted_iota(jnp.int32, (lz, 128), 0)
    total = {}
    for ox in range(-REACH, REACH + 1):
        chosen = [b for b in range(lx) if not (ox == -REACH and b % 2 == 0) and not (ox == REACH and b % 2 == 1)]
        wanted = [(cy, b) for cy in range(2) for b in chosen]
        parts = [left_ref[cy, pl.ds((b + ox + 2) * block, block), : SPAN * points] for cy, b in wanted]
        got = jnp.dot(jnp.concatenate(parts, axis=0), w_ref[ox + REACH], preferred_element_type=F32)
        for n, key in enumerate(wanted):
            piece = got[n * block : (n + 1) * block]
            total[key] = total[key] + piece if key in total else piece
        next(waiting, None)
    for cy in range(2):
        for b in range(lx):
            for p in range(half):
                acc_ref[b * half + p, pl.ds(8, deep), :] = total[cy, b][p * deep : (p + 1) * deep]
        for g in range(lx * half):
            folded = None
            for k in range((SPAN + 1) // 2):
                shown = []
                for oz in (2 * k - REACH, 2 * k + 1 - REACH):
                    if oz > REACH:
                        shown.append(jnp.zeros((lz, 128), F32))
                        continue
                    got = acc_ref[g, pl.ds(8 + oz + 2, lz), k * 128 : (k + 1) * 128]
                    if oz == -REACH:
                        got = jnp.where(level % 2 == 1, got, 0.0)
                    if oz == REACH:
                        got = jnp.where(level % 2 == 0, got, 0.0)
                    shown.append(got)
                both = jnp.where(lane < points, shown[0], shown[1])
                folded = both if folded is None else folded + both
            sum_ref[pl.ds(g * lz, lz), :] = folded
        dense = jnp.dot(sum_ref[...], twice, precision=lax.Precision.HIGHEST, preferred_element_type=F32)
        high, low = split(dense.T)
        spread = jnp.dot(high, expand, preferred_element_type=F32)
        spread = spread + jnp.dot(low, expand, preferred_element_type=F32)
        for g in range(lx * half):
            dense_ref[g, cy] = spread[:, g * lanes : (g + 1) * lanes]

    for _ in waiting:
        pass
    for x in range(lx):
        for y in range(ly):
            far = jnp.sum(g_ref[x * ly + y] * dense_ref[x * half + y // 2, y % 2], axis=0, keepdims=True)
            at = pl.ds(y, 1)
            total = near_end_ref[x, at, :] + far
            if x in (0, lx - 1):
                total = total + out_ref[x, at, :] + near_edge_ref[0 if x == 0 else 1, at, :]
            else:
                total = total + near_in_ref[x - 1, at, :]
            out_ref[x, at, :] = total


def rounds_of(axis):
    return [[(i, i + 1) for i in range(start, lax.axis_size(axis) - 1, 2)] for start in range(2)]


def rounds_in(axis):
    return max(1, sum(1 for pairs in rounds_of(axis) if pairs))


def exchange(packets, axis):
    count = lax.axis_size(axis)
    planes = lax.axis_size("gx")
    results = []
    for packet, pairs in zip(packets, rounds_of(axis)):
        swaps = [swap for i, j in pairs for swap in ((i, j), (j, i))]
        idle = sorted(set(range(count)) - {i for i, _ in swaps})
        if not idle or axis == "gx" or planes % 2:
            results.append(lax.ppermute(packet, axis, swaps))
            continue
        swaps = [(plane * count + i, plane * count + j) for plane in range(planes) for i, j in swaps]
        swaps += [(plane * count + i, (plane ^ 1) * count + i) for plane in range(planes) for i in idle]
        results.append(lax.ppermute(packet, ("gx", axis), swaps))
    return results


def call(kernel, outs, args, scratch=(), limit=8, name=None, spaces=None):
    spec = pl.BlockSpec(memory_space=pltpu.VMEM)
    return pl.pallas_call(
        kernel,
        out_shape=outs,
        in_specs=[pl.BlockSpec(memory_space=space) for space in spaces] if spaces else [spec] * len(args),
        out_specs=[spec] * len(outs),
        scratch_shapes=list(scratch),
        compiler_params=pltpu.CompilerParams(vmem_limit_bytes=limit << 20),
        name=name,
    )(*args)


def shaped(*shape):
    return jax.ShapeDtypeStruct(shape, F32)


def per_device(offsets, charges, up_inverse, translations, down_inverse):
    points = up_inverse.shape[0]
    _, lx, ly, lanes = offsets.shape
    lz = lanes // BODIES
    half = ly // 2
    pairs = half + 2
    wide = ly + 2
    deep = lz + 4
    rounds = {axis: rounds_in(axis) for axis in ("gx", "gy", "gz")}
    sphere = jnp.asarray(surface(points))
    boxes = lx * half * lz
    packet = shaped(lx * lz + 4 * lx, lanes)
    inputs = [
        pltpu.with_memory_space_constraint(value, pltpu.HBM)
        for value in (offsets, charges, sphere, up_inverse, down_inverse)
    ]
    offsets, charges, down_inverse, surfaces, density, *packets = call(
        upward_kernel,
        [shaped(*value.shape) for value in (offsets, charges, down_inverse)]
        + [shaped(lx * ly, points, lanes), shaped(boxes, 2 * points)]
        + [packet] * rounds["gy"],
        inputs,
        [
            pltpu.VMEM(sphere.shape, F32),
            pltpu.VMEM(up_inverse.shape, F32),
            pltpu.VMEM((boxes, 2 * points), F32),
            pltpu.VMEM((2 * points, 2 * points), F32),
            pltpu.SemaphoreType.DMA((5,)),
        ],
        4,
        "upward",
        [pltpu.HBM] * 5,
    )
    received = exchange(packets, "gy")
    count, width = translations.shape
    stride = count // 2 * 2 + 1
    edge, weights = call(
        edge_kernel,
        [
            shaped(2, ly, lanes),
            jax.ShapeDtypeStruct((SPAN, SPAN * points, (SPAN + 1) * points), BF16),
        ],
        (pltpu.with_memory_space_constraint(translations, pltpu.HBM), density, offsets, charges),
        [
            pltpu.VMEM((3 + lz, lx * ly, lanes), F32),
            pltpu.VMEM(translations.shape, BF16),
            pltpu.VMEM((width // 128 * stride, 128), F32),
            pltpu.SemaphoreType.DMA((4,)),
        ],
        24,
        "near_edge",
        [pltpu.HBM, pl.ANY, pltpu.VMEM, pltpu.VMEM],
    )
    received, edge, weights = lax.optimization_barrier((received, edge, weights))
    packet = shaped(lx * pairs * 2 + 4 * half * lx, lanes)
    dense, body, *packets = call(
        functools.partial(zpack_kernel, len(received)),
        [shaped(lx * pairs * lz, 2 * points), shaped(4, lx * wide, lanes)] + [packet] * rounds["gz"],
        (offsets, charges, density, *received),
        name="zpack",
    )
    packets, body = lax.optimization_barrier((packets, body))
    received = exchange(packets, "gz")
    windows = [pltpu.VMEM((3 + lz, lx * wide, lanes), F32)]
    (inner,) = call(inner_kernel, [shaped(lx - 2, ly, lanes)], (offsets, body), windows, name="near_inner")
    received, inner = lax.optimization_barrier((received, inner))
    packet = shaped(2 * pairs * deep + 4 * wide + 8 * half, lanes)
    end = shaped(4, half * lx, lanes)
    dense, low, high, *packets = call(
        functools.partial(xpack_kernel, len(received)),
        [shaped(lx * pairs, deep, 2 * points), end, end] + [packet] * rounds["gx"],
        (dense, body, *received),
        name="xpack",
    )
    packets, body = lax.optimization_barrier((packets, body))
    received = exchange(packets, "gx")
    (ends,) = call(
        ends_kernel,
        [shaped(lx, ly, lanes)],
        (offsets, body, low, high),
        windows + [pltpu.VMEM((10, half * lx, lanes), F32)],
        name="near_ends",
    )
    received, ends = lax.optimization_barrier((received, ends))
    (out,) = call(
        functools.partial(final_kernel, len(received)),
        [shaped(lx, ly, lanes)],
        (offsets, dense, edge, inner, ends, weights, down_inverse, surfaces, *received),
        [
            pltpu.VMEM((2, (lx + 4) * half * deep, (SPAN + 1) * points), BF16),
            pltpu.VMEM((lx * half, 8 + deep + 8, (SPAN + 1) * points), F32),
            pltpu.VMEM((lx * half, 2, points, lanes), F32),
            pltpu.VMEM((boxes, 2 * points), F32),
            pltpu.VMEM((2, 3 + lz, wide, lanes), F32),
            pltpu.VMEM((2, 10, half, lanes), F32),
        ],
        24,
        "final",
    )
    return out


def solution(mesh):
    in_specs = (P(None, "gx", "gy", "gz"), P("gx", "gy", "gz"), P(), P(), P())
    out_specs = P("gx", "gy", "gz")
    return jax.shard_map(
        per_device, mesh=mesh, in_specs=in_specs, out_specs=out_specs, check_vma=False
    )
```

```python
import functools
import math

import jax
import jax.numpy as jnp
import numpy as np
from jax import lax
from jax.experimental import pallas as pl
from jax.experimental.pallas import tpu as pltpu
from jax.sharding import PartitionSpec as P

BODIES = 32
RADIUS = 0.9
REACH = 3
SPAN = 2 * REACH + 1
F32 = jnp.float32
BF16 = jnp.bfloat16
NT = (((1,), (1,)), ((), ()))


def surface(points):
    number = np.arange(points).astype(np.float32)
    height = np.float32(1.0) - (np.float32(2.0) * number + np.float32(1.0)) / np.float32(points)
    across = np.sqrt(np.float32(1.0) - height * height)
    turned = number * np.float32(math.pi * (3.0 - math.sqrt(5.0)))
    columns = np.zeros((points, 128), np.float32)
    columns[:, 0] = RADIUS * across * np.cos(turned)
    columns[:, 1] = RADIUS * across * np.sin(turned)
    columns[:, 2] = RADIUS * height
    return columns


def numbering():
    table, count = {}, 0
    for ox in range(-REACH, REACH + 1):
        for oy in range(-REACH, REACH + 1):
            for oz in range(-REACH, REACH + 1):
                if max(abs(ox), abs(oy), abs(oz)) >= 2:
                    table[ox, oy, oz] = count
                    count += 1
    return table


def split(value):
    high = value.astype(BF16)
    return high, (value - high.astype(F32)).astype(BF16)


def surface_green(sphere, offs_ref, x, y):
    rows = [offs_ref[c, x, pl.ds(y, 1), :] - 0.5 for c in range(3)]
    square = None
    for c in range(3):
        delta = sphere[:, c : c + 1] - rows[c]
        square = delta * delta if square is None else square + delta * delta
    return lax.rsqrt(square)


def select(even, one, two):
    return jnp.where(even, one, two), jnp.where(even, two, one)


def put(refs, at, even, low, high):
    refs[0][at, :] = jnp.where(even, high, low)
    for ref in refs[1:]:
        ref[at, :] = jnp.where(even, low, high)


def get(refs, axis):
    index = lax.axis_index(axis)
    one = refs[0][...]
    above, below = select(index % 2 == 0, one, refs[1][...] if len(refs) > 1 else one)
    return jnp.where(index == lax.axis_size(axis) - 1, 0.0, above), jnp.where(index == 0, 0.0, below)


def upward_kernel(
    offs_hbm, q_hbm, sphere_hbm, uinv_hbm, dinv_hbm, offs_ref, q_ref, dinv_ref, g_ref, u_ref, *rest
):
    *packets, sphere_ref, uinv_ref, wide_ref, sems = rest
    copies = [
        pltpu.make_async_copy(source, target, sems.at[n])
        for n, (source, target) in enumerate(
            (
                (offs_hbm, offs_ref),
                (q_hbm, q_ref),
                (sphere_hbm, sphere_ref),
                (uinv_hbm, uinv_ref),
                (dinv_hbm, dinv_ref),
            )
        )
    ]
    for copy in copies:
        copy.start()
    _, lx, ly, lanes = offs_ref.shape
    lz = lanes // BODIES
    half = ly // 2
    points = uinv_ref.shape[0]
    even = lax.axis_index("gy") % 2 == 0
    offset = lax.broadcasted_iota(jnp.int32, (lanes, 2 * points), 1)
    offset = offset - lax.broadcasted_iota(jnp.int32, (lanes, 2 * points), 0) // BODIES
    wide_ref[...] = jnp.zeros_like(wide_ref)
    column = lax.broadcasted_iota(jnp.int32, (2 * points, 2 * points), 1)
    within = column % points
    wanted = column - within + jnp.where(within < points // 2, 2 * within, 2 * within - points + 1)
    shuffle = (lax.broadcasted_iota(jnp.int32, (2 * points, 2 * points), 0) == wanted).astype(BF16)
    for copy in copies[:3]:
        copy.wait()
    check = None
    sphere = sphere_ref[...]
    for c in range(4):
        for x in range(lx):
            low, high = [
                offs_ref[c, x, pl.ds(y, 1), :] if c < 3 else q_ref[x, pl.ds(y, 1), :] for y in (0, ly - 1)
            ]
            put(packets, pl.ds(lx * lz + c * lx + x, 1), even, low, high)
    for x in range(lx):
        for pair in range(half):
            parts = []
            for y in (2 * pair, 2 * pair + 1):
                kernel = surface_green(sphere, offs_ref, x, y)
                g_ref[x * ly + y] = kernel
                parts.append(kernel * q_ref[x, pl.ds(y, 1), :])
            part = (offset == (x * half + pair) * lz).astype(BF16)
            part = jnp.dot(
                jnp.concatenate(split(jnp.concatenate(parts, axis=0)), axis=1),
                jnp.concatenate([part, part], axis=0),
                preferred_element_type=F32,
            )
            check = part if check is None else check + part
    copies[3].wait()
    wide_ref[:points, :points] = uinv_ref[...]
    wide_ref[points:, points:] = uinv_ref[...]
    inverse = [jnp.dot(part, shuffle, preferred_element_type=F32).astype(BF16) for part in split(wide_ref[...])]
    high, low = split(check.T[: u_ref.shape[0]])
    density = jnp.dot(
        jnp.concatenate([high, high, low], axis=1),
        jnp.concatenate(inverse + inverse[:1], axis=0),
        preferred_element_type=F32,
    )
    u_ref[...] = density.astype(BF16).astype(F32)
    for x in range(lx):
        low = u_ref[pl.ds(x * half * lz, lz), :]
        high = u_ref[pl.ds((x * half + half - 1) * lz, lz), :]
        put(packets, pl.ds(x * lz, lz), even, low, high)
    copies[4].wait()


def relay(t_ref, copies, w_ref, rows_ref):
    count, width = t_ref.shape
    groups = width // 128
    stride = rows_ref.shape[0] // groups
    points = math.isqrt(width)
    half = points // 2
    order = numbering()
    for a in range(groups):
        if a % (groups // len(copies)) == 0:
            copies[a // (groups // len(copies))].wait()
        rows_ref[pl.ds(a * stride, count), :] = t_ref[:, a * 128 : (a + 1) * 128].astype(F32)
    left = lax.broadcasted_iota(jnp.int32, (groups, 128), 1) < points
    zero = jnp.zeros((groups, 128), F32)
    for ox in range(SPAN):
        for oy in range(SPAN):
            for k in range((SPAN + 1) // 2):
                loaded = []
                for oz in (2 * k, 2 * k + 1):
                    at = order.get((ox - REACH, oy - REACH, oz - REACH))
                    loaded.append(zero if at is None else rows_ref[pl.ds(at, groups, stride=stride), :])
                one, two = loaded
                even = jnp.where(left, one, pltpu.roll(two, points, 1))
                odd = jnp.where(left, pltpu.roll(one, points, 1), two)
                at = slice(k * 128, (k + 1) * 128)
                w_ref[ox, pl.ds(oy * points, half), at] = even.astype(BF16)
                w_ref[ox, pl.ds(oy * points + half, half), at] = odd.astype(BF16)


def zpack_kernel(count, offs_ref, q_ref, u_ref, *rest):
    received, (d_ref, r_ref, *packets) = rest[:count], rest[count:]
    _, lx, ly, lanes = offs_ref.shape
    lz = lanes // BODIES
    half = ly // 2
    wide = ly + 2
    above, below = get(received, "gy")
    even = lax.axis_index("gz") % 2 == 0
    for x in range(lx):
        at = x * (half + 2) * lz
        d_ref[pl.ds(at, lz), :] = below[x * lz : (x + 1) * lz]
        d_ref[pl.ds(at + lz, half * lz), :] = u_ref[pl.ds(x * half * lz, half * lz), :]
        d_ref[pl.ds(at + (half + 1) * lz, lz), :] = above[x * lz : (x + 1) * lz]
        for c in range(4):
            row = lx * lz + c * lx + x
            r_ref[c, pl.ds(x * wide, 1), :] = below[row : row + 1]
            r_ref[c, pl.ds(x * wide + 1, ly), :] = offs_ref[c, x] if c < 3 else q_ref[x]
            r_ref[c, pl.ds(x * wide + ly + 1, 1), :] = above[row : row + 1]
    for g in range(lx * (half + 2)):
        put(packets, pl.ds(g * 2, 2), even, d_ref[pl.ds(g * lz, 2), :], d_ref[pl.ds(g * lz + lz - 2, 2), :])
    spot = lax.broadcasted_iota(jnp.int32, (lx, lanes), 1) // BODIES
    base = lx * (half + 2) * 2
    for c in range(4):
        rows = [r_ref[c, pl.ds(j, lx, stride=wide), :] for j in range(wide)]
        for pack in range(half):
            low = high = None
            for j in range(4):
                row = rows[2 * pack + j]
                first = pltpu.roll(row, j * BODIES, 1) if j else row
                last = pltpu.roll(row, (j + 1) % 4 * BODIES, 1) if (j + 1) % 4 else row
                low = first if low is None else jnp.where(spot == j, first, low)
                high = last if high is None else jnp.where(spot == j, last, high)
            put(packets, pl.ds(base + (c * half + pack) * lx, lx), even, low, high)


def xpack_kernel(count, d_ref, r_ref, *rest):
    received, (e_ref, zl_ref, zh_ref, *packets) = rest[:count], rest[count:]
    groups = e_ref.shape[0]
    lx = zl_ref.shape[1] // 2
    pairs = groups // lx
    half = pairs - 2
    wide = 2 * half + 2
    lz = d_ref.shape[0] // groups
    above, below = get(received, "gz")
    even = lax.axis_index("gx") % 2 == 0
    for g in range(groups):
        e_ref[g, pl.ds(0, 2), :] = below[g * 2 : g * 2 + 2]
        e_ref[g, pl.ds(2, lz), :] = d_ref[pl.ds(g * lz, lz), :]
        e_ref[g, pl.ds(2 + lz, 2), :] = above[g * 2 : g * 2 + 2]
    base = groups * 2
    for c in range(4):
        zl_ref[c] = below[base + c * half * lx : base + (c + 1) * half * lx]
        zh_ref[c] = above[base + c * half * lx : base + (c + 1) * half * lx]
    deep = lz + 4
    for n in range(2 * pairs):
        put(packets, pl.ds(n * deep, deep), even, e_ref[n], e_ref[groups - 2 * pairs + n])
    base = 2 * pairs * deep
    for c in range(4):
        low, high = r_ref[c, pl.ds(0, wide), :], r_ref[c, pl.ds((lx - 1) * wide, wide), :]
        put(packets, pl.ds(base + c * wide, wide), even, low, high)
    base = base + 4 * wide
    for end, ref in enumerate((zl_ref, zh_ref)):
        for c in range(4):
            for pack in range(half):
                low, high = ref[c, pl.ds(pack * lx, 1), :], ref[c, pl.ds(pack * lx + lx - 1, 1), :]
                put(packets, pl.ds(base + (end * 4 + c) * half + pack, 1), even, low, high)


def turn(offs_ref, x):
    _, _, ly, lanes = offs_ref.shape
    lead = lax.broadcasted_iota(jnp.int32, (ly, lanes), 0).astype(F32)
    spots = (lax.broadcasted_iota(jnp.int32, (ly, lanes), 1) // BODIES).astype(F32)
    places = [offs_ref[0, x] + float(x), offs_ref[1, x] + lead, offs_ref[2, x] + spots]
    return jnp.concatenate(places + [places[0]], axis=0).T


def pick(turned, ly, y, z):
    return [turned[z * BODIES : (z + 1) * BODIES, c * ly + y : c * ly + y + 1] for c in range(3)]


def attract(total, target, source, weight, own=False):
    square = None
    for t, s in zip(target, source):
        delta = t - s
        square = delta * delta if square is None else square + delta * delta
    inverse = lax.rsqrt(square)
    if own:
        inverse = jnp.where(square > 0.0, inverse, 0.0)
    term = inverse * weight
    return term if total is None else total + term


def lane_sum(ones, parts):
    high, low = split(jnp.concatenate(parts, axis=0))
    out = lax.dot_general(ones, high, NT, preferred_element_type=F32)
    return (out + lax.dot_general(ones, low, NT, preferred_element_type=F32))[:1]


def spans(value, spot, lz):
    return [jnp.where((spot >= z - 1) & (spot <= z + 1), value, 0.0) for z in range(lz)]


def gather(out_ref, n, y, turned, lz, rows):
    _, ly, lanes = out_ref.shape
    ones = jnp.ones((8, lanes), BF16)
    parts = []
    for z in range(lz):
        target = pick(turned, ly, y, z)
        total = None
        for source, weight, own in rows(z):
            total = attract(total, target, source, weight, own)
        parts.append(jnp.zeros((BODIES, lanes), F32) if total is None else total)
    out_ref[n, pl.ds(y, 1), :] = lane_sum(ones, parts)


def row_source(ref, at, z, own=False):
    return [ref[c, at, :] for c in range(3)], ref[3 + z, at, :], own


def edge_kernel(t_hbm, after_ref, offs_ref, q_ref, out_ref, w_ref, win_ref, t_ref, rows_ref, sems):
    chunks = sems.shape[0]
    cut = t_ref.shape[1] // chunks
    copies = [
        pltpu.make_async_copy(
            t_hbm.at[:, pl.ds(n * cut, cut)], t_ref.at[:, pl.ds(n * cut, cut)], sems.at[n]
        )
        for n in range(chunks)
    ]
    for copy in copies:
        copy.start()
    _, lx, ly, lanes = offs_ref.shape
    lz = lanes // BODIES
    spot = lax.broadcasted_iota(jnp.int32, (ly, lanes), 1) // BODIES
    lead = lax.broadcasted_iota(jnp.int32, (ly, lanes), 0)
    for x in range(lx):
        at = pl.ds(x * ly, ly)
        shift = [float(x), lead.astype(F32), spot.astype(F32)]
        for c in range(3):
            win_ref[c, at, :] = offs_ref[c, x] + shift[c]
        for z, value in enumerate(spans(q_ref[x], spot, lz)):
            win_ref[3 + z, at, :] = value
    for n, x in enumerate((0, lx - 1)):
        turned = turn(offs_ref, x)
        for y in range(ly):

            def rows(z):
                for xx in range(max(x - 1, 0), min(x + 2, lx)):
                    for yy in range(max(y - 1, 0), min(y + 2, ly)):
                        yield row_source(win_ref, pl.ds(xx * ly + yy, 1), z, xx == x and yy == y)

            gather(out_ref, n, y, turned, lz, rows)
    relay(t_ref, copies, w_ref, rows_ref)


def strips(r_ref, win_ref, wide, lz):
    _, rows, lanes = r_ref.shape
    place = lax.broadcasted_iota(jnp.int32, (rows, lanes), 0)
    spot = lax.broadcasted_iota(jnp.int32, (rows, lanes), 1) // BODIES
    base = [place // wide, place % wide - 1, spot]
    for c in range(3):
        win_ref[c] = r_ref[c] + base[c].astype(F32)
    for z, value in enumerate(spans(r_ref[3], spot, lz)):
        win_ref[3 + z] = value


def inner_kernel(offs_ref, r_ref, out_ref, win_ref):
    _, lx, ly, lanes = offs_ref.shape
    lz = lanes // BODIES
    wide = ly + 2
    strips(r_ref, win_ref, wide, lz)
    for x in range(1, lx - 1):
        turned = turn(offs_ref, x)
        for y in range(ly):

            def rows(z):
                for xx in range(x - 1, x + 2):
                    for dy in range(3):
                        yield row_source(win_ref, pl.ds(xx * wide + y + dy, 1), z, xx == x and dy == 1)

            gather(out_ref, x - 1, y, turned, lz, rows)


def ends_kernel(offs_ref, r_ref, zl_ref, zh_ref, out_ref, win_ref, end_ref):
    _, lx, ly, lanes = offs_ref.shape
    lz = lanes // BODIES
    half = ly // 2
    wide = ly + 2
    strips(r_ref, win_ref, wide, lz)
    end_windows(zl_ref, -1.0, end_ref, 0, lz, half)
    end_windows(zh_ref, float(lz), end_ref, 5, lz, half)
    for x in range(lx):
        turned = turn(offs_ref, x)
        for y in range(ly):

            def rows(z):
                nearby = range(max(x - 1, 0), min(x + 2, lx))
                if x in (0, lx - 1):
                    for yy in (y, y + 2):
                        if yy in (0, ly + 1):
                            for xx in nearby:
                                yield row_source(win_ref, pl.ds(xx * wide + yy, 1), z)
                for end in range(2):
                    if z == (0 if end == 0 else lz - 1):
                        for xx in nearby:
                            at = pl.ds(y // 2 * lx + xx, 1)
                            source = [end_ref[end * 5 + c, at, :] for c in range(3)]
                            yield source, end_ref[end * 5 + 3 + y % 2, at, :], False

            gather(out_ref, x, y, turned, lz, rows)


def end_windows(end_ref, base, win_ref, at, lz, half):
    rows = end_ref.shape[1]
    lanes = end_ref.shape[2]
    count = rows // half
    place = lax.broadcasted_iota(jnp.int32, (rows, lanes), 0)
    spot = lax.broadcasted_iota(jnp.int32, (rows, lanes), 1) // BODIES
    shift = [(place % count).astype(F32), (spot + 2 * (place // count) - 1).astype(F32), base]
    for c in range(3):
        win_ref[at + c] = end_ref[c] + shift[c]
    for s in range(2):
        win_ref[at + 3 + s] = jnp.where((spot >= s) & (spot < s + 3), end_ref[3], 0.0)


def final_kernel(count, offs_ref, e_ref, near_edge_ref, near_in_ref, near_end_ref, w_ref, dinv_ref, g_ref, *rest):
    received, rest = rest[:count], rest[count:]
    out_ref, left_ref, acc_ref, sum_ref, side_ref, edge_ref = rest
    _, lx, ly, lanes = offs_ref.shape
    lz = lanes // BODIES
    points = dinv_ref.shape[0]
    half = ly // 2
    pairs = half + 2
    wide = ly + 2
    deep = lz + 4
    block = half * deep
    above, below = get(received, "gx")

    def plane(x, pair):
        if x < 2:
            return below[(x * pairs + pair) * deep : (x * pairs + pair + 1) * deep]
        if x < lx + 2:
            return e_ref[(x - 2) * pairs + pair]
        return above[((x - lx - 2) * pairs + pair) * deep : ((x - lx - 2) * pairs + pair + 1) * deep]

    side = lax.broadcasted_iota(jnp.int32, (deep, 128), 1) < points
    for x in range(lx + 4):
        planes = [plane(x, pair) for pair in range(pairs)]
        turned = [pltpu.roll(value, points, 1) for value in planes]
        at = pl.ds(x * block, block)
        for j in range(SPAN // 2 + 1):
            early, late = [], []
            for p in range(half):
                before = turned[p + j - 1] if j else 0.0
                after = turned[p + j] if j < SPAN // 2 else 0.0
                early.append(jnp.where(side, before, after))
                late.append(planes[p + j] if j < SPAN // 2 else jnp.zeros((deep, 128), F32))
            left_ref[0, at, j * 128 : (j + 1) * 128] = jnp.concatenate(early, axis=0).astype(BF16)
            left_ref[1, at, j * 128 : (j + 1) * 128] = jnp.concatenate(late, axis=0).astype(BF16)
    spot = lax.broadcasted_iota(jnp.int32, (wide, lanes), 1) // BODIES
    lead = lax.broadcasted_iota(jnp.int32, (wide, lanes), 0).astype(F32) - 1.0
    base = 2 * pairs * deep
    ends = base + 4 * wide
    for side, value in enumerate((below, above)):
        shift = [-1.0 if side == 0 else float(lx), lead, spot.astype(F32)]
        for c in range(3):
            side_ref[side, c] = value[base + c * wide : base + (c + 1) * wide] + shift[c]
        for z, part in enumerate(spans(value[base + 3 * wide : base + 4 * wide], spot, lz)):
            side_ref[side, 3 + z] = part
    spot = lax.broadcasted_iota(jnp.int32, (half, lanes), 1) // BODIES
    place = lax.broadcasted_iota(jnp.int32, (half, lanes), 0)
    for side, value in enumerate((below, above)):
        for end in range(2):
            shift = [-1.0 if side == 0 else float(lx), (spot + 2 * place - 1).astype(F32), -1.0 if end == 0 else float(lz)]
            for c in range(3):
                at = ends + (end * 4 + c) * half
                edge_ref[side, end * 5 + c] = value[at : at + half] + shift[c]
            at = ends + (end * 4 + 3) * half
            for s in range(2):
                edge_ref[side, end * 5 + 3 + s] = jnp.where((spot >= s) & (spot < s + 3), value[at : at + half], 0.0)


    def side_unit(x, y, turned):
        side = 0 if x == 0 else 1

        def rows(z):
            for dy in range(3):
                at = pl.ds(y + dy, 1)
                yield [side_ref[side, c, at, :] for c in range(3)], side_ref[side, 3 + z, at, :], False
            for end in range(2):
                if z == (0 if end == 0 else lz - 1):
                    at = pl.ds(y // 2, 1)
                    source = [edge_ref[side, end * 5 + c, at, :] for c in range(3)]
                    yield source, edge_ref[side, end * 5 + 3 + y % 2, at, :], False

        gather(out_ref, x, y, turned, lz, rows)

    def units():
        for x in (0, lx - 1):
            turned = turn(offs_ref, x)
            for y in range(ly):
                side_unit(x, y, turned)
                yield

    waiting = units()
    high, low = split(jnp.concatenate([dinv_ref[...].T] * 2, axis=1))
    turned_inverse = jnp.concatenate([high, low, high], axis=1)
    boxes = lx * half * lz
    shape = (2 * boxes, lx * half * lanes)
    expand = (
        lax.broadcasted_iota(jnp.int32, shape, 1) // BODIES == lax.broadcasted_iota(jnp.int32, shape, 0) % boxes
    ).astype(BF16)
    lane = lax.broadcasted_iota(jnp.int32, (lz, 128), 1)
    level = lax.broadcasted_iota(jnp.int32, (lz, 128), 0)
    totals = {}
    for ox in range(-REACH, REACH + 1):
        chosen = [b for b in range(lx) if not (ox == -REACH and b % 2 == 0) and not (ox == REACH and b % 2 == 1)]
        wanted = [(cy, b) for cy in range(2) for b in chosen]
        parts = [left_ref[cy, pl.ds((b + ox + 2) * block, block), : SPAN * points] for cy, b in wanted]
        got = jnp.dot(jnp.concatenate(parts, axis=0), w_ref[ox + REACH], preferred_element_type=F32)
        for n, key in enumerate(wanted):
            piece = got[n * block : (n + 1) * block]
            totals[key] = totals[key] + piece if key in totals else piece
        next(waiting, None)
    for cy in range(2):
        for b in range(lx):
            for p in range(half):
                acc_ref[cy, b * half + p, pl.ds(8, deep), :] = totals[cy, b][p * deep : (p + 1) * deep]
        for g in range(lx * half):
            folded = None
            for k in range((SPAN + 1) // 2):
                shown = []
                for oz in (2 * k - REACH, 2 * k + 1 - REACH):
                    if oz > REACH:
                        shown.append(jnp.zeros((lz, 128), F32))
                        continue
                    got = acc_ref[cy, g, pl.ds(8 + oz + 2, lz), k * 128 : (k + 1) * 128]
                    if oz == -REACH:
                        got = jnp.where(level % 2 == 1, got, 0.0)
                    if oz == REACH:
                        got = jnp.where(level % 2 == 0, got, 0.0)
                    shown.append(got)
                both = jnp.where(lane < points, shown[0], shown[1])
                folded = both if folded is None else folded + both
            sum_ref[pl.ds((cy * lx * half + g) * lz, lz), :] = folded
    for _ in waiting:
        pass
    high, low = split(sum_ref[...])
    dense = lax.dot_general(
        turned_inverse, jnp.concatenate([high, high, low], axis=1), NT, preferred_element_type=F32
    )
    parts = split(dense)
    parts = [
        jnp.concatenate([part[:, cy * boxes : (cy + 1) * boxes] for part in parts], axis=1) for cy in range(2)
    ]
    dense = jnp.dot(jnp.concatenate(parts, axis=0), expand, preferred_element_type=F32)
    for x in range(lx):
        for y in range(ly):
            g = x * half + y // 2
            part = dense[y % 2 * points : (y % 2 + 1) * points, g * lanes : (g + 1) * lanes]
            far = jnp.sum(g_ref[x * ly + y] * part, axis=0, keepdims=True)
            at = pl.ds(y, 1)
            total = near_end_ref[x, at, :] + far
            if x in (0, lx - 1):
                total = total + out_ref[x, at, :] + near_edge_ref[0 if x == 0 else 1, at, :]
            else:
                total = total + near_in_ref[x - 1, at, :]
            out_ref[x, at, :] = total


def rounds_of(axis):
    return [[(i, i + 1) for i in range(start, lax.axis_size(axis) - 1, 2)] for start in range(2)]


def rounds_in(axis):
    return max(1, sum(1 for pairs in rounds_of(axis) if pairs))


def exchange(packets, axis):
    count = lax.axis_size(axis)
    planes = lax.axis_size("gx")
    results = []
    for packet, pairs in zip(packets, rounds_of(axis)):
        swaps = [swap for i, j in pairs for swap in ((i, j), (j, i))]
        idle = sorted(set(range(count)) - {i for i, _ in swaps})
        if not idle or axis == "gx" or planes % 2:
            results.append(lax.ppermute(packet, axis, swaps))
            continue
        swaps = [(plane * count + i, plane * count + j) for plane in range(planes) for i, j in swaps]
        swaps += [(plane * count + i, (plane ^ 1) * count + i) for plane in range(planes) for i in idle]
        results.append(lax.ppermute(packet, ("gx", axis), swaps))
    return results


def call(kernel, outs, args, scratch=(), limit=8, name=None, spaces=None):
    spec = pl.BlockSpec(memory_space=pltpu.VMEM)
    return pl.pallas_call(
        kernel,
        out_shape=outs,
        in_specs=[pl.BlockSpec(memory_space=space) for space in spaces] if spaces else [spec] * len(args),
        out_specs=[spec] * len(outs),
        scratch_shapes=list(scratch),
        compiler_params=pltpu.CompilerParams(vmem_limit_bytes=limit << 20),
        name=name,
    )(*args)


def shaped(*shape):
    return jax.ShapeDtypeStruct(shape, F32)


def per_device(offsets, charges, up_inverse, translations, down_inverse):
    points = up_inverse.shape[0]
    _, lx, ly, lanes = offsets.shape
    lz = lanes // BODIES
    half = ly // 2
    pairs = half + 2
    wide = ly + 2
    deep = lz + 4
    rounds = {axis: rounds_in(axis) for axis in ("gx", "gy", "gz")}
    sphere = jnp.asarray(surface(points))
    boxes = lx * half * lz
    packet = shaped(lx * lz + 4 * lx, lanes)
    inputs = [
        pltpu.with_memory_space_constraint(value, pltpu.HBM)
        for value in (offsets, charges, sphere, up_inverse, down_inverse)
    ]
    offsets, charges, down_inverse, surfaces, density, *packets = call(
        upward_kernel,
        [shaped(*value.shape) for value in (offsets, charges, down_inverse)]
        + [shaped(lx * ly, points, lanes), shaped(boxes, 2 * points)]
        + [packet] * rounds["gy"],
        inputs,
        [
            pltpu.VMEM(sphere.shape, F32),
            pltpu.VMEM(up_inverse.shape, F32),
            pltpu.VMEM((2 * points, 2 * points), F32),
            pltpu.SemaphoreType.DMA((5,)),
        ],
        4,
        "upward",
        [pltpu.HBM] * 5,
    )
    received = exchange(packets, "gy")
    count, width = translations.shape
    stride = count // 2 * 2 + 1
    edge, weights = call(
        edge_kernel,
        [
            shaped(2, ly, lanes),
            jax.ShapeDtypeStruct((SPAN, SPAN * points, (SPAN + 1) * points), BF16),
        ],
        (pltpu.with_memory_space_constraint(translations, pltpu.HBM), density, offsets, charges),
        [
            pltpu.VMEM((3 + lz, lx * ly, lanes), F32),
            pltpu.VMEM(translations.shape, BF16),
            pltpu.VMEM((width // 128 * stride, 128), F32),
            pltpu.SemaphoreType.DMA((4,)),
        ],
        24,
        "near_edge",
        [pltpu.HBM, pl.ANY, pltpu.VMEM, pltpu.VMEM],
    )
    received, edge, weights = lax.optimization_barrier((received, edge, weights))
    packet = shaped(lx * pairs * 2 + 4 * half * lx, lanes)
    dense, body, *packets = call(
        functools.partial(zpack_kernel, len(received)),
        [shaped(lx * pairs * lz, 2 * points), shaped(4, lx * wide, lanes)] + [packet] * rounds["gz"],
        (offsets, charges, density, *received),
        name="zpack",
    )
    packets, body = lax.optimization_barrier((packets, body))
    received = exchange(packets, "gz")
    windows = [pltpu.VMEM((3 + lz, lx * wide, lanes), F32)]
    (inner,) = call(inner_kernel, [shaped(lx - 2, ly, lanes)], (offsets, body), windows, name="near_inner")
    received, inner = lax.optimization_barrier((received, inner))
    packet = shaped(2 * pairs * deep + 4 * wide + 8 * half, lanes)
    end = shaped(4, half * lx, lanes)
    dense, low, high, *packets = call(
        functools.partial(xpack_kernel, len(received)),
        [shaped(lx * pairs, deep, 2 * points), end, end] + [packet] * rounds["gx"],
        (dense, body, *received),
        name="xpack",
    )
    packets, body = lax.optimization_barrier((packets, body))
    received = exchange(packets, "gx")
    (ends,) = call(
        ends_kernel,
        [shaped(lx, ly, lanes)],
        (offsets, body, low, high),
        windows + [pltpu.VMEM((10, half * lx, lanes), F32)],
        name="near_ends",
    )
    received, ends = lax.optimization_barrier((received, ends))
    (out,) = call(
        functools.partial(final_kernel, len(received)),
        [shaped(lx, ly, lanes)],
        (offsets, dense, edge, inner, ends, weights, down_inverse, surfaces, *received),
        [
            pltpu.VMEM((2, (lx + 4) * half * deep, (SPAN + 1) * points), BF16),
            pltpu.VMEM((2, lx * half, 8 + deep + 8, (SPAN + 1) * points), F32),
            pltpu.VMEM((2 * boxes, 2 * points), F32),
            pltpu.VMEM((2, 3 + lz, wide, lanes), F32),
            pltpu.VMEM((2, 10, half, lanes), F32),
        ],
        24,
        "final",
    )
    return out


def solution(mesh):
    in_specs = (P(None, "gx", "gy", "gz"), P("gx", "gy", "gz"), P(), P(), P())
    out_specs = P("gx", "gy", "gz")
    return jax.shard_map(
        per_device, mesh=mesh, in_specs=in_specs, out_specs=out_specs, check_vma=False
    )
```

```python
import functools
import math

import jax
import jax.numpy as jnp
import numpy as np
from jax import lax
from jax.experimental import pallas as pl
from jax.experimental.pallas import tpu as pltpu
from jax.sharding import PartitionSpec as P

BODIES = 32
RADIUS = 0.9
REACH = 3
SPAN = 2 * REACH + 1
F32 = jnp.float32
BF16 = jnp.bfloat16
NT = (((1,), (1,)), ((), ()))


def surface(points):
    number = np.arange(points).astype(np.float32)
    height = np.float32(1.0) - (np.float32(2.0) * number + np.float32(1.0)) / np.float32(points)
    across = np.sqrt(np.float32(1.0) - height * height)
    turned = number * np.float32(math.pi * (3.0 - math.sqrt(5.0)))
    columns = np.zeros((points, 128), np.float32)
    columns[:, 0] = RADIUS * across * np.cos(turned)
    columns[:, 1] = RADIUS * across * np.sin(turned)
    columns[:, 2] = RADIUS * height
    return columns


def numbering():
    table, count = {}, 0
    for ox in range(-REACH, REACH + 1):
        for oy in range(-REACH, REACH + 1):
            for oz in range(-REACH, REACH + 1):
                if max(abs(ox), abs(oy), abs(oz)) >= 2:
                    table[ox, oy, oz] = count
                    count += 1
    return table


def split(value):
    high = value.astype(BF16)
    return high, (value - high.astype(F32)).astype(BF16)


def surface_green(sphere, offs_ref, x, y):
    rows = [offs_ref[c, x, pl.ds(y, 1), :] - 0.5 for c in range(3)]
    square = None
    for c in range(3):
        delta = sphere[:, c : c + 1] - rows[c]
        square = delta * delta if square is None else square + delta * delta
    return lax.rsqrt(square)


def select(even, one, two):
    return jnp.where(even, one, two), jnp.where(even, two, one)


def put(refs, at, even, low, high):
    refs[0][at, :] = jnp.where(even, high, low)
    for ref in refs[1:]:
        ref[at, :] = jnp.where(even, low, high)


def get(refs, axis):
    index = lax.axis_index(axis)
    one = refs[0][...]
    above, below = select(index % 2 == 0, one, refs[1][...] if len(refs) > 1 else one)
    return jnp.where(index == lax.axis_size(axis) - 1, 0.0, above), jnp.where(index == 0, 0.0, below)


def upward_kernel(
    offs_hbm, q_hbm, sphere_hbm, uinv_hbm, dinv_hbm, offs_ref, q_ref, dinv_ref, g_ref, u_ref, *rest
):
    *packets, sphere_ref, uinv_ref, wide_ref, sems = rest
    copies = [
        pltpu.make_async_copy(source, target, sems.at[n])
        for n, (source, target) in enumerate(
            (
                (offs_hbm, offs_ref),
                (q_hbm, q_ref),
                (sphere_hbm, sphere_ref),
                (uinv_hbm, uinv_ref),
                (dinv_hbm, dinv_ref),
            )
        )
    ]
    for copy in copies:
        copy.start()
    _, lx, ly, lanes = offs_ref.shape
    lz = lanes // BODIES
    half = ly // 2
    points = uinv_ref.shape[0]
    even = lax.axis_index("gy") % 2 == 0
    offset = lax.broadcasted_iota(jnp.int32, (lanes, 2 * points), 1)
    offset = offset - lax.broadcasted_iota(jnp.int32, (lanes, 2 * points), 0) // BODIES
    wide_ref[...] = jnp.zeros_like(wide_ref)
    column = lax.broadcasted_iota(jnp.int32, (2 * points, 2 * points), 1)
    within = column % points
    wanted = column - within + jnp.where(within < points // 2, 2 * within, 2 * within - points + 1)
    shuffle = (lax.broadcasted_iota(jnp.int32, (2 * points, 2 * points), 0) == wanted).astype(BF16)
    for copy in copies[:3]:
        copy.wait()
    check = None
    sphere = sphere_ref[...]
    for c in range(4):
        for x in range(lx):
            low, high = [
                offs_ref[c, x, pl.ds(y, 1), :] if c < 3 else q_ref[x, pl.ds(y, 1), :] for y in (0, ly - 1)
            ]
            put(packets, pl.ds(lx * lz + c * lx + x, 1), even, low, high)
    for x in range(lx):
        for pair in range(half):
            parts = []
            for y in (2 * pair, 2 * pair + 1):
                kernel = surface_green(sphere, offs_ref, x, y)
                g_ref[x * ly + y] = kernel
                parts.append(kernel * q_ref[x, pl.ds(y, 1), :])
            part = (offset == (x * half + pair) * lz).astype(BF16)
            part = jnp.dot(
                jnp.concatenate(split(jnp.concatenate(parts, axis=0)), axis=1),
                jnp.concatenate([part, part], axis=0),
                preferred_element_type=F32,
            )
            check = part if check is None else check + part
    copies[3].wait()
    wide_ref[:points, :points] = uinv_ref[...]
    wide_ref[points:, points:] = uinv_ref[...]
    inverse = [jnp.dot(part, shuffle, preferred_element_type=F32).astype(BF16) for part in split(wide_ref[...])]
    high, low = split(check.T[: u_ref.shape[0]])
    density = jnp.dot(
        jnp.concatenate([high, high, low], axis=1),
        jnp.concatenate(inverse + inverse[:1], axis=0),
        preferred_element_type=F32,
    )
    u_ref[...] = density.astype(BF16).astype(F32)
    for x in range(lx):
        low = u_ref[pl.ds(x * half * lz, lz), :]
        high = u_ref[pl.ds((x * half + half - 1) * lz, lz), :]
        put(packets, pl.ds(x * lz, lz), even, low, high)
    copies[4].wait()


def relay(t_ref, copies, w_ref, rows_ref):
    count, width = t_ref.shape
    groups = width // 128
    stride = rows_ref.shape[0] // groups
    points = math.isqrt(width)
    half = points // 2
    order = numbering()
    for a in range(groups):
        if a % (groups // len(copies)) == 0:
            copies[a // (groups // len(copies))].wait()
        rows_ref[pl.ds(a * stride, count), :] = t_ref[:, a * 128 : (a + 1) * 128].astype(F32)
    left = lax.broadcasted_iota(jnp.int32, (groups, 128), 1) < points
    zero = jnp.zeros((groups, 128), F32)
    for ox in range(SPAN):
        for oy in range(SPAN):
            for k in range((SPAN + 1) // 2):
                loaded = []
                for oz in (2 * k, 2 * k + 1):
                    at = order.get((ox - REACH, oy - REACH, oz - REACH))
                    loaded.append(zero if at is None else rows_ref[pl.ds(at, groups, stride=stride), :])
                one, two = loaded
                even = jnp.where(left, one, pltpu.roll(two, points, 1))
                odd = jnp.where(left, pltpu.roll(one, points, 1), two)
                at = slice(k * 128, (k + 1) * 128)
                w_ref[ox, pl.ds(oy * points, half), at] = even.astype(BF16)
                w_ref[ox, pl.ds(oy * points + half, half), at] = odd.astype(BF16)


def zpack_kernel(count, offs_ref, q_ref, u_ref, *rest):
    received, (d_ref, r_ref, *packets) = rest[:count], rest[count:]
    _, lx, ly, lanes = offs_ref.shape
    lz = lanes // BODIES
    half = ly // 2
    wide = ly + 2
    above, below = get(received, "gy")
    even = lax.axis_index("gz") % 2 == 0
    for x in range(lx):
        at = x * (half + 2) * lz
        d_ref[pl.ds(at, lz), :] = below[x * lz : (x + 1) * lz]
        d_ref[pl.ds(at + lz, half * lz), :] = u_ref[pl.ds(x * half * lz, half * lz), :]
        d_ref[pl.ds(at + (half + 1) * lz, lz), :] = above[x * lz : (x + 1) * lz]
        for c in range(4):
            row = lx * lz + c * lx + x
            r_ref[c, pl.ds(x * wide, 1), :] = below[row : row + 1]
            r_ref[c, pl.ds(x * wide + 1, ly), :] = offs_ref[c, x] if c < 3 else q_ref[x]
            r_ref[c, pl.ds(x * wide + ly + 1, 1), :] = above[row : row + 1]
    for g in range(lx * (half + 2)):
        put(packets, pl.ds(g * 2, 2), even, d_ref[pl.ds(g * lz, 2), :], d_ref[pl.ds(g * lz + lz - 2, 2), :])
    spot = lax.broadcasted_iota(jnp.int32, (lx, lanes), 1) // BODIES
    base = lx * (half + 2) * 2
    for c in range(4):
        rows = [r_ref[c, pl.ds(j, lx, stride=wide), :] for j in range(wide)]
        for pack in range(half):
            low = high = None
            for j in range(4):
                row = rows[2 * pack + j]
                first = pltpu.roll(row, j * BODIES, 1) if j else row
                last = pltpu.roll(row, (j + 1) % 4 * BODIES, 1) if (j + 1) % 4 else row
                low = first if low is None else jnp.where(spot == j, first, low)
                high = last if high is None else jnp.where(spot == j, last, high)
            put(packets, pl.ds(base + (c * half + pack) * lx, lx), even, low, high)


def xpack_kernel(count, d_ref, r_ref, *rest):
    received, (e_ref, zl_ref, zh_ref, *packets) = rest[:count], rest[count:]
    groups = e_ref.shape[0]
    lx = zl_ref.shape[1] // 2
    pairs = groups // lx
    half = pairs - 2
    wide = 2 * half + 2
    lz = d_ref.shape[0] // groups
    above, below = get(received, "gz")
    even = lax.axis_index("gx") % 2 == 0
    for g in range(groups):
        e_ref[g, pl.ds(0, 2), :] = below[g * 2 : g * 2 + 2]
        e_ref[g, pl.ds(2, lz), :] = d_ref[pl.ds(g * lz, lz), :]
        e_ref[g, pl.ds(2 + lz, 2), :] = above[g * 2 : g * 2 + 2]
    base = groups * 2
    for c in range(4):
        zl_ref[c] = below[base + c * half * lx : base + (c + 1) * half * lx]
        zh_ref[c] = above[base + c * half * lx : base + (c + 1) * half * lx]
    deep = lz + 4
    for n in range(2 * pairs):
        put(packets, pl.ds(n * deep, deep), even, e_ref[n], e_ref[groups - 2 * pairs + n])
    base = 2 * pairs * deep
    for c in range(4):
        low, high = r_ref[c, pl.ds(0, wide), :], r_ref[c, pl.ds((lx - 1) * wide, wide), :]
        put(packets, pl.ds(base + c * wide, wide), even, low, high)
    base = base + 4 * wide
    for end, ref in enumerate((zl_ref, zh_ref)):
        for c in range(4):
            for pack in range(half):
                low, high = ref[c, pl.ds(pack * lx, 1), :], ref[c, pl.ds(pack * lx + lx - 1, 1), :]
                put(packets, pl.ds(base + (end * 4 + c) * half + pack, 1), even, low, high)


def turn(offs_ref, x):
    _, _, ly, lanes = offs_ref.shape
    lead = lax.broadcasted_iota(jnp.int32, (ly, lanes), 0).astype(F32)
    spots = (lax.broadcasted_iota(jnp.int32, (ly, lanes), 1) // BODIES).astype(F32)
    places = [offs_ref[0, x] + float(x), offs_ref[1, x] + lead, offs_ref[2, x] + spots]
    return jnp.concatenate(places + [places[0]], axis=0).T


def pick(turned, ly, y, z):
    return [turned[z * BODIES : (z + 1) * BODIES, c * ly + y : c * ly + y + 1] for c in range(3)]


def attract(total, target, source, weight, own=False):
    square = None
    for t, s in zip(target, source):
        delta = t - s
        square = delta * delta if square is None else square + delta * delta
    inverse = lax.rsqrt(square)
    if own:
        inverse = jnp.where(square > 0.0, inverse, 0.0)
    term = inverse * weight
    return term if total is None else total + term


def lane_sum(ones, parts):
    high, low = split(jnp.concatenate(parts, axis=0))
    out = lax.dot_general(ones, high, NT, preferred_element_type=F32)
    return (out + lax.dot_general(ones, low, NT, preferred_element_type=F32))[:1]


def spans(value, spot, lz):
    return [jnp.where((spot >= z - 1) & (spot <= z + 1), value, 0.0) for z in range(lz)]


def gather(out_ref, n, y, turned, lz, rows, start=0.0):
    _, ly, lanes = out_ref.shape
    ones = jnp.ones((8, lanes), BF16)
    parts = []
    for z in range(lz):
        target = pick(turned, ly, y, z)
        total = None
        for source, weight, own in rows(z):
            total = attract(total, target, source, weight, own)
        parts.append(jnp.zeros((BODIES, lanes), F32) if total is None else total)
    out_ref[n, pl.ds(y, 1), :] = start + lane_sum(ones, parts)


def row_source(ref, at, z, own=False):
    return [ref[c, at, :] for c in range(3)], ref[3 + z, at, :], own


def lay_pairs(ref, at, rows):
    lanes = ref.shape[2]
    side = lax.broadcasted_iota(jnp.int32, (rows, lanes), 1) < lanes // 2
    values = [ref[c] for c in range(3)] + [ref[at - 1]]
    after = [pltpu.roll(jnp.concatenate([value[1:], value[:1]], axis=0), lanes // 2, 1) for value in values]
    for end in range(2):
        keep = side if end == 0 else ~side
        for c in range(4):
            ref[at + end * 5 + c] = jnp.where(keep, values[c], after[c])
        ref[at + end * 5 + 4] = jnp.where(keep, values[3], 0.0)


def pair_sources(ref, base, z, lz, at, own):
    end = 0 if z == 0 else 1
    for n in range(0, len(at), 2):
        row = pl.ds(at[n], 1)
        source = [ref[base + end * 5 + c, row, :] for c in range(3)]
        yield source, ref[base + end * 5 + (3 if n + 1 < len(at) else 4), row, :], own in (at[n], at[n] + 1)


def edge_kernel(t_hbm, after_ref, offs_ref, q_ref, out_ref, w_ref, win_ref, t_ref, rows_ref, sems):
    chunks = sems.shape[0]
    cut = t_ref.shape[1] // chunks
    copies = [
        pltpu.make_async_copy(
            t_hbm.at[:, pl.ds(n * cut, cut)], t_ref.at[:, pl.ds(n * cut, cut)], sems.at[n]
        )
        for n in range(chunks)
    ]
    for copy in copies:
        copy.start()
    _, lx, ly, lanes = offs_ref.shape
    lz = lanes // BODIES
    spot = lax.broadcasted_iota(jnp.int32, (ly, lanes), 1) // BODIES
    lead = lax.broadcasted_iota(jnp.int32, (ly, lanes), 0)
    for x in range(lx):
        at = pl.ds(x * ly, ly)
        shift = [float(x), lead.astype(F32), spot.astype(F32)]
        for c in range(3):
            win_ref[c, at, :] = offs_ref[c, x] + shift[c]
        for z, value in enumerate(spans(q_ref[x], spot, lz)):
            win_ref[3 + z, at, :] = value
    for n, x in enumerate((0, lx - 1)):
        turned = turn(offs_ref, x)
        for y in range(ly):

            def rows(z):
                for xx in range(max(x - 1, 0), min(x + 2, lx)):
                    for yy in range(max(y - 1, 0), min(y + 2, ly)):
                        yield row_source(win_ref, pl.ds(xx * ly + yy, 1), z, xx == x and yy == y)

            gather(out_ref, n, y, turned, lz, rows)
    relay(t_ref, copies, w_ref, rows_ref)


def strips(r_ref, win_ref, wide, lz):
    _, rows, lanes = r_ref.shape
    place = lax.broadcasted_iota(jnp.int32, (rows, lanes), 0)
    spot = lax.broadcasted_iota(jnp.int32, (rows, lanes), 1) // BODIES
    base = [place // wide, place % wide - 1, spot]
    for c in range(3):
        win_ref[c] = r_ref[c] + base[c].astype(F32)
    for z, value in enumerate(spans(r_ref[3], spot, lz)):
        win_ref[3 + z] = value
    win_ref[3 + lz] = r_ref[3]
    lay_pairs(win_ref, 4 + lz, rows)


def inner_kernel(offs_ref, r_ref, near_ref, out_ref, win_ref):
    _, lx, ly, lanes = offs_ref.shape
    lz = lanes // BODIES
    wide = ly + 2
    strips(r_ref, win_ref, wide, lz)
    for x in range(lx):
        outer = x in (0, lx - 1)
        turned = turn(offs_ref, x)
        for y in range(ly):
            halo = [yy for yy in (y, y + 2) if yy in (0, ly + 1)]

            def rows(z):
                for xx in range(max(x - 1, 0), min(x + 2, lx)):
                    at = [xx * wide + yy for yy in (halo if outer else range(y, y + 3))]
                    if z in (0, lz - 1):
                        yield from pair_sources(win_ref, 4 + lz, z, lz, at, x * wide + y + 1)
                    else:
                        for row in at:
                            yield row_source(win_ref, pl.ds(row, 1), z, row == x * wide + y + 1)

            start = near_ref[0 if x == 0 else 1, pl.ds(y, 1), :] if outer else 0.0
            if outer and not halo:
                out_ref[x, pl.ds(y, 1), :] = start
            else:
                gather(out_ref, x, y, turned, lz, rows, start)


def ends_kernel(offs_ref, zl_ref, zh_ref, near_ref, out_ref, end_ref):
    _, lx, ly, lanes = offs_ref.shape
    lz = lanes // BODIES
    half = ly // 2
    end_windows(zl_ref, -1.0, end_ref, 0, lz, half)
    end_windows(zh_ref, float(lz), end_ref, 5, lz, half)
    for x in range(lx):
        turned = turn(offs_ref, x)
        for y in range(ly):

            def rows(z):
                nearby = range(max(x - 1, 0), min(x + 2, lx))
                for end in range(2):
                    if z == (0 if end == 0 else lz - 1):
                        for xx in nearby:
                            at = pl.ds(y // 2 * lx + xx, 1)
                            source = [end_ref[end * 5 + c, at, :] for c in range(3)]
                            yield source, end_ref[end * 5 + 3 + y % 2, at, :], False

            gather(out_ref, x, y, turned, lz, rows, near_ref[x, pl.ds(y, 1), :])


def end_windows(end_ref, base, win_ref, at, lz, half):
    rows = end_ref.shape[1]
    lanes = end_ref.shape[2]
    count = rows // half
    place = lax.broadcasted_iota(jnp.int32, (rows, lanes), 0)
    spot = lax.broadcasted_iota(jnp.int32, (rows, lanes), 1) // BODIES
    shift = [(place % count).astype(F32), (spot + 2 * (place // count) - 1).astype(F32), base]
    for c in range(3):
        win_ref[at + c] = end_ref[c] + shift[c]
    for s in range(2):
        win_ref[at + 3 + s] = jnp.where((spot >= s) & (spot < s + 3), end_ref[3], 0.0)


def final_kernel(count, offs_ref, e_ref, near_ref, w_ref, dinv_ref, g_ref, *rest):
    received, rest = rest[:count], rest[count:]
    out_ref, left_ref, acc_ref, sum_ref, side_ref, edge_ref = rest
    _, lx, ly, lanes = offs_ref.shape
    lz = lanes // BODIES
    points = dinv_ref.shape[0]
    half = ly // 2
    pairs = half + 2
    wide = ly + 2
    deep = lz + 4
    block = half * deep
    above, below = get(received, "gx")

    def plane(x, pair):
        if x < 2:
            return below[(x * pairs + pair) * deep : (x * pairs + pair + 1) * deep]
        if x < lx + 2:
            return e_ref[(x - 2) * pairs + pair]
        return above[((x - lx - 2) * pairs + pair) * deep : ((x - lx - 2) * pairs + pair + 1) * deep]

    side = lax.broadcasted_iota(jnp.int32, (deep, 128), 1) < points
    for x in range(lx + 4):
        planes = [plane(x, pair) for pair in range(pairs)]
        turned = [pltpu.roll(value, points, 1) for value in planes]
        at = pl.ds(x * block, block)
        for j in range(SPAN // 2 + 1):
            early, late = [], []
            for p in range(half):
                before = turned[p + j - 1] if j else 0.0
                after = turned[p + j] if j < SPAN // 2 else 0.0
                early.append(jnp.where(side, before, after))
                late.append(planes[p + j] if j < SPAN // 2 else jnp.zeros((deep, 128), F32))
            left_ref[0, at, j * 128 : (j + 1) * 128] = jnp.concatenate(early, axis=0).astype(BF16)
            left_ref[1, at, j * 128 : (j + 1) * 128] = jnp.concatenate(late, axis=0).astype(BF16)
    spot = lax.broadcasted_iota(jnp.int32, (wide, lanes), 1) // BODIES
    lead = lax.broadcasted_iota(jnp.int32, (wide, lanes), 0).astype(F32) - 1.0
    base = 2 * pairs * deep
    ends = base + 4 * wide
    for side, value in enumerate((below, above)):
        shift = [-1.0 if side == 0 else float(lx), lead, spot.astype(F32)]
        for c in range(3):
            side_ref[side, c] = value[base + c * wide : base + (c + 1) * wide] + shift[c]
        for z, part in enumerate(spans(value[base + 3 * wide : base + 4 * wide], spot, lz)):
            side_ref[side, 3 + z] = part
    spot = lax.broadcasted_iota(jnp.int32, (half, lanes), 1) // BODIES
    place = lax.broadcasted_iota(jnp.int32, (half, lanes), 0)
    for side, value in enumerate((below, above)):
        for end in range(2):
            shift = [-1.0 if side == 0 else float(lx), (spot + 2 * place - 1).astype(F32), -1.0 if end == 0 else float(lz)]
            for c in range(3):
                at = ends + (end * 4 + c) * half
                edge_ref[side, end * 5 + c] = value[at : at + half] + shift[c]
            at = ends + (end * 4 + 3) * half
            for s in range(2):
                edge_ref[side, end * 5 + 3 + s] = jnp.where((spot >= s) & (spot < s + 3), value[at : at + half], 0.0)


    def side_unit(x, y, turned):
        side = 0 if x == 0 else 1

        def rows(z):
            for dy in range(3):
                at = pl.ds(y + dy, 1)
                yield [side_ref[side, c, at, :] for c in range(3)], side_ref[side, 3 + z, at, :], False
            for end in range(2):
                if z == (0 if end == 0 else lz - 1):
                    at = pl.ds(y // 2, 1)
                    source = [edge_ref[side, end * 5 + c, at, :] for c in range(3)]
                    yield source, edge_ref[side, end * 5 + 3 + y % 2, at, :], False

        gather(out_ref, x, y, turned, lz, rows, near_ref[x, pl.ds(y, 1), :])

    def units():
        for x in (0, lx - 1):
            turned = turn(offs_ref, x)
            for y in range(ly):
                side_unit(x, y, turned)
                yield

    waiting = units()
    high, low = split(jnp.concatenate([dinv_ref[...].T] * 2, axis=1))
    turned_inverse = jnp.concatenate([high, low, high], axis=1)
    boxes = lx * half * lz
    shape = (2 * boxes, lx * half * lanes)
    expand = (
        lax.broadcasted_iota(jnp.int32, shape, 1) // BODIES == lax.broadcasted_iota(jnp.int32, shape, 0) % boxes
    ).astype(BF16)
    lane = lax.broadcasted_iota(jnp.int32, (lz, 128), 1)
    level = lax.broadcasted_iota(jnp.int32, (lz, 128), 0)
    totals = {}
    for ox in range(-REACH, REACH + 1):
        chosen = [b for b in range(lx) if not (ox == -REACH and b % 2 == 0) and not (ox == REACH and b % 2 == 1)]
        wanted = [(cy, b) for cy in range(2) for b in chosen]
        parts = [left_ref[cy, pl.ds((b + ox + 2) * block, block), : SPAN * points] for cy, b in wanted]
        got = jnp.dot(jnp.concatenate(parts, axis=0), w_ref[ox + REACH], preferred_element_type=F32)
        for n, key in enumerate(wanted):
            piece = got[n * block : (n + 1) * block]
            totals[key] = totals[key] + piece if key in totals else piece
        next(waiting, None)
    for cy in range(2):
        for b in range(lx):
            for p in range(half):
                acc_ref[cy, b * half + p, pl.ds(8, deep), :] = totals[cy, b][p * deep : (p + 1) * deep]
        for g in range(lx * half):
            folded = None
            for k in range((SPAN + 1) // 2):
                shown = []
                for oz in (2 * k - REACH, 2 * k + 1 - REACH):
                    if oz > REACH:
                        shown.append(jnp.zeros((lz, 128), F32))
                        continue
                    got = acc_ref[cy, g, pl.ds(8 + oz + 2, lz), k * 128 : (k + 1) * 128]
                    if oz == -REACH:
                        got = jnp.where(level % 2 == 1, got, 0.0)
                    if oz == REACH:
                        got = jnp.where(level % 2 == 0, got, 0.0)
                    shown.append(got)
                both = jnp.where(lane < points, shown[0], shown[1])
                folded = both if folded is None else folded + both
            sum_ref[pl.ds((cy * lx * half + g) * lz, lz), :] = folded
    for _ in waiting:
        pass
    high, low = split(sum_ref[...])
    dense = lax.dot_general(
        turned_inverse, jnp.concatenate([high, high, low], axis=1), NT, preferred_element_type=F32
    )
    parts = split(dense)
    parts = [
        jnp.concatenate([part[:, cy * boxes : (cy + 1) * boxes] for part in parts], axis=1) for cy in range(2)
    ]
    dense = jnp.dot(jnp.concatenate(parts, axis=0), expand, preferred_element_type=F32)
    for x in range(lx):
        for y in range(ly):
            g = x * half + y // 2
            part = dense[y % 2 * points : (y % 2 + 1) * points, g * lanes : (g + 1) * lanes]
            far = jnp.sum(g_ref[x * ly + y] * part, axis=0, keepdims=True)
            at = pl.ds(y, 1)
            start = out_ref[x, at, :] if x in (0, lx - 1) else near_ref[x, at, :]
            out_ref[x, at, :] = start + far


def rounds_of(axis):
    return [[(i, i + 1) for i in range(start, lax.axis_size(axis) - 1, 2)] for start in range(2)]


def rounds_in(axis):
    return max(1, sum(1 for pairs in rounds_of(axis) if pairs))


def exchange(packets, axis):
    count = lax.axis_size(axis)
    planes = lax.axis_size("gx")
    results = []
    for packet, pairs in zip(packets, rounds_of(axis)):
        swaps = [swap for i, j in pairs for swap in ((i, j), (j, i))]
        idle = sorted(set(range(count)) - {i for i, _ in swaps})
        if not idle or axis == "gx" or planes % 2:
            results.append(lax.ppermute(packet, axis, swaps))
            continue
        swaps = [(plane * count + i, plane * count + j) for plane in range(planes) for i, j in swaps]
        swaps += [(plane * count + i, (plane ^ 1) * count + i) for plane in range(planes) for i in idle]
        results.append(lax.ppermute(packet, ("gx", axis), swaps))
    return results


def call(kernel, outs, args, scratch=(), limit=8, name=None, spaces=None):
    spec = pl.BlockSpec(memory_space=pltpu.VMEM)
    return pl.pallas_call(
        kernel,
        out_shape=outs,
        in_specs=[pl.BlockSpec(memory_space=space) for space in spaces] if spaces else [spec] * len(args),
        out_specs=[spec] * len(outs),
        scratch_shapes=list(scratch),
        compiler_params=pltpu.CompilerParams(vmem_limit_bytes=limit << 20),
        name=name,
    )(*args)


def shaped(*shape):
    return jax.ShapeDtypeStruct(shape, F32)


def per_device(offsets, charges, up_inverse, translations, down_inverse):
    points = up_inverse.shape[0]
    _, lx, ly, lanes = offsets.shape
    lz = lanes // BODIES
    half = ly // 2
    pairs = half + 2
    wide = ly + 2
    deep = lz + 4
    rounds = {axis: rounds_in(axis) for axis in ("gx", "gy", "gz")}
    sphere = jnp.asarray(surface(points))
    boxes = lx * half * lz
    packet = shaped(lx * lz + 4 * lx, lanes)
    inputs = [
        pltpu.with_memory_space_constraint(value, pltpu.HBM)
        for value in (offsets, charges, sphere, up_inverse, down_inverse)
    ]
    offsets, charges, down_inverse, surfaces, density, *packets = call(
        upward_kernel,
        [shaped(*value.shape) for value in (offsets, charges, down_inverse)]
        + [shaped(lx * ly, points, lanes), shaped(boxes, 2 * points)]
        + [packet] * rounds["gy"],
        inputs,
        [
            pltpu.VMEM(sphere.shape, F32),
            pltpu.VMEM(up_inverse.shape, F32),
            pltpu.VMEM((2 * points, 2 * points), F32),
            pltpu.SemaphoreType.DMA((5,)),
        ],
        4,
        "upward",
        [pltpu.HBM] * 5,
    )
    received = exchange(packets, "gy")
    count, width = translations.shape
    stride = count // 2 * 2 + 1
    edge, weights = call(
        edge_kernel,
        [
            shaped(2, ly, lanes),
            jax.ShapeDtypeStruct((SPAN, SPAN * points, (SPAN + 1) * points), BF16),
        ],
        (pltpu.with_memory_space_constraint(translations, pltpu.HBM), density, offsets, charges),
        [
            pltpu.VMEM((3 + lz, lx * ly, lanes), F32),
            pltpu.VMEM(translations.shape, BF16),
            pltpu.VMEM((width // 128 * stride, 128), F32),
            pltpu.SemaphoreType.DMA((4,)),
        ],
        24,
        "near_edge",
        [pltpu.HBM, pl.ANY, pltpu.VMEM, pltpu.VMEM],
    )
    received, edge, weights = lax.optimization_barrier((received, edge, weights))
    packet = shaped(lx * pairs * 2 + 4 * half * lx, lanes)
    dense, body, *packets = call(
        functools.partial(zpack_kernel, len(received)),
        [shaped(lx * pairs * lz, 2 * points), shaped(4, lx * wide, lanes)] + [packet] * rounds["gz"],
        (offsets, charges, density, *received),
        name="zpack",
    )
    packets, body = lax.optimization_barrier((packets, body))
    received = exchange(packets, "gz")
    windows = [pltpu.VMEM((14 + lz, lx * wide, lanes), F32)]
    (inner,) = call(inner_kernel, [shaped(lx, ly, lanes)], (offsets, body, edge), windows, name="near_inner")
    received, inner = lax.optimization_barrier((received, inner))
    packet = shaped(2 * pairs * deep + 4 * wide + 8 * half, lanes)
    end = shaped(4, half * lx, lanes)
    dense, low, high, *packets = call(
        functools.partial(xpack_kernel, len(received)),
        [shaped(lx * pairs, deep, 2 * points), end, end] + [packet] * rounds["gx"],
        (dense, body, *received),
        name="xpack",
    )
    packets, body = lax.optimization_barrier((packets, body))
    received = exchange(packets, "gx")
    (ends,) = call(
        ends_kernel,
        [shaped(lx, ly, lanes)],
        (offsets, low, high, inner),
        [pltpu.VMEM((10, half * lx, lanes), F32)],
        name="near_ends",
    )
    received, ends = lax.optimization_barrier((received, ends))
    (out,) = call(
        functools.partial(final_kernel, len(received)),
        [shaped(lx, ly, lanes)],
        (offsets, dense, ends, weights, down_inverse, surfaces, *received),
        [
            pltpu.VMEM((2, (lx + 4) * half * deep, (SPAN + 1) * points), BF16),
            pltpu.VMEM((2, lx * half, 8 + deep + 8, (SPAN + 1) * points), F32),
            pltpu.VMEM((2 * boxes, 2 * points), F32),
            pltpu.VMEM((2, 3 + lz, wide, lanes), F32),
            pltpu.VMEM((2, 10, half, lanes), F32),
        ],
        24,
        "final",
    )
    return out


def solution(mesh):
    in_specs = (P(None, "gx", "gy", "gz"), P("gx", "gy", "gz"), P(), P(), P())
    out_specs = P("gx", "gy", "gz")
    return jax.shard_map(
        per_device, mesh=mesh, in_specs=in_specs, out_specs=out_specs, check_vma=False
    )
```

```python
import functools
import math

import jax
import jax.numpy as jnp
import numpy as np
from jax import lax
from jax.experimental import pallas as pl
from jax.experimental.pallas import tpu as pltpu
from jax.sharding import PartitionSpec as P

BODIES = 32
RADIUS = 0.9
REACH = 3
SPAN = 2 * REACH + 1
F32 = jnp.float32
BF16 = jnp.bfloat16
NT = (((1,), (1,)), ((), ()))


def surface(points):
    number = np.arange(points).astype(np.float32)
    height = np.float32(1.0) - (np.float32(2.0) * number + np.float32(1.0)) / np.float32(points)
    across = np.sqrt(np.float32(1.0) - height * height)
    turned = number * np.float32(math.pi * (3.0 - math.sqrt(5.0)))
    columns = np.zeros((points, 128), np.float32)
    columns[:, 0] = RADIUS * across * np.cos(turned)
    columns[:, 1] = RADIUS * across * np.sin(turned)
    columns[:, 2] = RADIUS * height
    return columns


def numbering():
    table, count = {}, 0
    for ox in range(-REACH, REACH + 1):
        for oy in range(-REACH, REACH + 1):
            for oz in range(-REACH, REACH + 1):
                if max(abs(ox), abs(oy), abs(oz)) >= 2:
                    table[ox, oy, oz] = count
                    count += 1
    return table


def split(value):
    high = value.astype(BF16)
    return high, (value - high.astype(F32)).astype(BF16)


def surface_green(sphere, offs_ref, x, y):
    rows = [offs_ref[c, x, pl.ds(y, 1), :] - 0.5 for c in range(3)]
    square = None
    for c in range(3):
        delta = sphere[:, c : c + 1] - rows[c]
        square = delta * delta if square is None else square + delta * delta
    return lax.rsqrt(square)


def select(even, one, two):
    return jnp.where(even, one, two), jnp.where(even, two, one)


def put(refs, at, even, low, high):
    refs[0][at, :] = jnp.where(even, high, low)
    for ref in refs[1:]:
        ref[at, :] = jnp.where(even, low, high)


def get(refs, axis):
    index = lax.axis_index(axis)
    one = refs[0][...]
    above, below = select(index % 2 == 0, one, refs[1][...] if len(refs) > 1 else one)
    return jnp.where(index == lax.axis_size(axis) - 1, 0.0, above), jnp.where(index == 0, 0.0, below)


def upward_kernel(
    offs_hbm, q_hbm, sphere_hbm, uinv_hbm, dinv_hbm, offs_ref, q_ref, dinv_ref, g_ref, u_ref, *rest
):
    *packets, sphere_ref, uinv_ref, wide_ref, sems = rest
    copies = [
        pltpu.make_async_copy(source, target, sems.at[n])
        for n, (source, target) in enumerate(
            (
                (offs_hbm, offs_ref),
                (q_hbm, q_ref),
                (sphere_hbm, sphere_ref),
                (uinv_hbm, uinv_ref),
                (dinv_hbm, dinv_ref),
            )
        )
    ]
    for copy in copies:
        copy.start()
    _, lx, ly, lanes = offs_ref.shape
    lz = lanes // BODIES
    half = ly // 2
    points = uinv_ref.shape[0]
    even = lax.axis_index("gy") % 2 == 0
    offset = lax.broadcasted_iota(jnp.int32, (lanes, 2 * points), 1)
    offset = offset - lax.broadcasted_iota(jnp.int32, (lanes, 2 * points), 0) // BODIES
    wide_ref[...] = jnp.zeros_like(wide_ref)
    column = lax.broadcasted_iota(jnp.int32, (2 * points, 2 * points), 1)
    within = column % points
    wanted = column - within + jnp.where(within < points // 2, 2 * within, 2 * within - points + 1)
    shuffle = (lax.broadcasted_iota(jnp.int32, (2 * points, 2 * points), 0) == wanted).astype(BF16)
    for copy in copies[:3]:
        copy.wait()
    check = None
    sphere = sphere_ref[...]
    for c in range(4):
        for x in range(lx):
            low, high = [
                offs_ref[c, x, pl.ds(y, 1), :] if c < 3 else q_ref[x, pl.ds(y, 1), :] for y in (0, ly - 1)
            ]
            put(packets, pl.ds(lx * lz + c * lx + x, 1), even, low, high)
    for x in range(lx):
        for pair in range(half):
            parts = []
            for y in (2 * pair, 2 * pair + 1):
                kernel = surface_green(sphere, offs_ref, x, y)
                g_ref[x * ly + y] = kernel
                parts.append(kernel * q_ref[x, pl.ds(y, 1), :])
            part = (offset == (x * half + pair) * lz).astype(BF16)
            part = jnp.dot(
                jnp.concatenate(split(jnp.concatenate(parts, axis=0)), axis=1),
                jnp.concatenate([part, part], axis=0),
                preferred_element_type=F32,
            )
            check = part if check is None else check + part
    copies[3].wait()
    wide_ref[:points, :points] = uinv_ref[...]
    wide_ref[points:, points:] = uinv_ref[...]
    inverse = [jnp.dot(part, shuffle, preferred_element_type=F32).astype(BF16) for part in split(wide_ref[...])]
    high, low = split(check.T[: u_ref.shape[0]])
    density = jnp.dot(
        jnp.concatenate([high, high, low], axis=1),
        jnp.concatenate(inverse + inverse[:1], axis=0),
        preferred_element_type=F32,
    )
    u_ref[...] = density.astype(BF16).astype(F32)
    for x in range(lx):
        low = u_ref[pl.ds(x * half * lz, lz), :]
        high = u_ref[pl.ds((x * half + half - 1) * lz, lz), :]
        put(packets, pl.ds(x * lz, lz), even, low, high)
    copies[4].wait()


def relay(t_ref, copies, w_ref, rows_ref):
    count, width = t_ref.shape
    groups = width // 128
    stride = rows_ref.shape[0] // groups
    points = math.isqrt(width)
    half = points // 2
    order = numbering()
    for a in range(groups):
        if a % (groups // len(copies)) == 0:
            copies[a // (groups // len(copies))].wait()
        rows_ref[pl.ds(a * stride, count), :] = t_ref[:, a * 128 : (a + 1) * 128].astype(F32)
    left = lax.broadcasted_iota(jnp.int32, (groups, 128), 1) < points
    zero = jnp.zeros((groups, 128), F32)
    for ox in range(SPAN):
        for oy in range(SPAN):
            for k in range((SPAN + 1) // 2):
                loaded = []
                for oz in (2 * k, 2 * k + 1):
                    at = order.get((ox - REACH, oy - REACH, oz - REACH))
                    loaded.append(zero if at is None else rows_ref[pl.ds(at, groups, stride=stride), :])
                one, two = loaded
                even = jnp.where(left, one, pltpu.roll(two, points, 1))
                odd = jnp.where(left, pltpu.roll(one, points, 1), two)
                at = slice(k * 128, (k + 1) * 128)
                w_ref[ox, pl.ds(oy * points, half), at] = even.astype(BF16)
                w_ref[ox, pl.ds(oy * points + half, half), at] = odd.astype(BF16)


def zpack_kernel(count, offs_ref, q_ref, u_ref, *rest):
    received, (d_ref, r_ref, *packets) = rest[:count], rest[count:]
    _, lx, ly, lanes = offs_ref.shape
    lz = lanes // BODIES
    half = ly // 2
    wide = ly + 2
    above, below = get(received, "gy")
    even = lax.axis_index("gz") % 2 == 0
    for x in range(lx):
        at = x * (half + 2) * lz
        d_ref[pl.ds(at, lz), :] = below[x * lz : (x + 1) * lz]
        d_ref[pl.ds(at + lz, half * lz), :] = u_ref[pl.ds(x * half * lz, half * lz), :]
        d_ref[pl.ds(at + (half + 1) * lz, lz), :] = above[x * lz : (x + 1) * lz]
        for c in range(4):
            row = lx * lz + c * lx + x
            r_ref[c, pl.ds(x * wide, 1), :] = below[row : row + 1]
            r_ref[c, pl.ds(x * wide + 1, ly), :] = offs_ref[c, x] if c < 3 else q_ref[x]
            r_ref[c, pl.ds(x * wide + ly + 1, 1), :] = above[row : row + 1]
    for g in range(lx * (half + 2)):
        put(packets, pl.ds(g * 2, 2), even, d_ref[pl.ds(g * lz, 2), :], d_ref[pl.ds(g * lz + lz - 2, 2), :])
    spot = lax.broadcasted_iota(jnp.int32, (lx, lanes), 1) // BODIES
    base = lx * (half + 2) * 2
    for c in range(4):
        rows = [r_ref[c, pl.ds(j, lx, stride=wide), :] for j in range(wide)]
        for pack in range(half):
            low = high = None
            for j in range(4):
                row = rows[2 * pack + j]
                first = pltpu.roll(row, j * BODIES, 1) if j else row
                last = pltpu.roll(row, (j + 1) % 4 * BODIES, 1) if (j + 1) % 4 else row
                low = first if low is None else jnp.where(spot == j, first, low)
                high = last if high is None else jnp.where(spot == j, last, high)
            put(packets, pl.ds(base + (c * half + pack) * lx, lx), even, low, high)


def xpack_kernel(count, d_ref, r_ref, *rest):
    received, (e_ref, zl_ref, zh_ref, *packets) = rest[:count], rest[count:]
    groups = e_ref.shape[0]
    lx = zl_ref.shape[1] // 2
    pairs = groups // lx
    half = pairs - 2
    wide = 2 * half + 2
    lz = d_ref.shape[0] // groups
    above, below = get(received, "gz")
    even = lax.axis_index("gx") % 2 == 0
    for g in range(groups):
        e_ref[g, pl.ds(0, 2), :] = below[g * 2 : g * 2 + 2]
        e_ref[g, pl.ds(2, lz), :] = d_ref[pl.ds(g * lz, lz), :]
        e_ref[g, pl.ds(2 + lz, 2), :] = above[g * 2 : g * 2 + 2]
    base = groups * 2
    for c in range(4):
        zl_ref[c] = below[base + c * half * lx : base + (c + 1) * half * lx]
        zh_ref[c] = above[base + c * half * lx : base + (c + 1) * half * lx]
    deep = lz + 4
    for n in range(2 * pairs):
        put(packets, pl.ds(n * deep, deep), even, e_ref[n], e_ref[groups - 2 * pairs + n])
    base = 2 * pairs * deep
    for c in range(4):
        low, high = r_ref[c, pl.ds(0, wide), :], r_ref[c, pl.ds((lx - 1) * wide, wide), :]
        put(packets, pl.ds(base + c * wide, wide), even, low, high)
    base = base + 4 * wide
    for end, ref in enumerate((zl_ref, zh_ref)):
        for c in range(4):
            for pack in range(half):
                low, high = ref[c, pl.ds(pack * lx, 1), :], ref[c, pl.ds(pack * lx + lx - 1, 1), :]
                put(packets, pl.ds(base + (end * 4 + c) * half + pack, 1), even, low, high)


def turn(offs_ref, x):
    _, _, ly, lanes = offs_ref.shape
    lead = lax.broadcasted_iota(jnp.int32, (ly, lanes), 0).astype(F32)
    spots = (lax.broadcasted_iota(jnp.int32, (ly, lanes), 1) // BODIES).astype(F32)
    places = [offs_ref[0, x] + float(x), offs_ref[1, x] + lead, offs_ref[2, x] + spots]
    return jnp.concatenate(places + [places[0]], axis=0).T


def pick(turned, ly, y, z):
    return [turned[z * BODIES : (z + 1) * BODIES, c * ly + y : c * ly + y + 1] for c in range(3)]


def attract(total, target, source, weight, own=False):
    square = None
    for t, s in zip(target, source):
        delta = t - s
        square = delta * delta if square is None else square + delta * delta
    inverse = lax.rsqrt(square)
    if own:
        inverse = jnp.where(square > 0.0, inverse, 0.0)
    term = inverse * weight
    return term if total is None else total + term


def lane_sum(ones, parts):
    high, low = split(jnp.concatenate(parts, axis=0))
    out = lax.dot_general(ones, high, NT, preferred_element_type=F32)
    return (out + lax.dot_general(ones, low, NT, preferred_element_type=F32))[:1]


def spans(value, spot, lz):
    return [jnp.where((spot >= z - 1) & (spot <= z + 1), value, 0.0) for z in range(lz)]


def gather(out_ref, n, y, turned, lz, rows, start=0.0):
    _, ly, lanes = out_ref.shape
    ones = jnp.ones((8, lanes), BF16)
    parts = []
    for z in range(lz):
        target = pick(turned, ly, y, z)
        total = None
        for source, weight, own in rows(z):
            total = attract(total, target, source, weight, own)
        parts.append(jnp.zeros((BODIES, lanes), F32) if total is None else total)
    out_ref[n, pl.ds(y, 1), :] = start + lane_sum(ones, parts)


def row_source(ref, at, z, own=False):
    return [ref[c, at, :] for c in range(3)], ref[3 + z, at, :], own


def lay_pairs(ref, at, rows):
    lanes = ref.shape[2]
    side = lax.broadcasted_iota(jnp.int32, (rows, lanes), 1) < lanes // 2
    values = [ref[c] for c in range(3)] + [ref[at - 1]]
    after = [pltpu.roll(jnp.concatenate([value[1:], value[:1]], axis=0), lanes // 2, 1) for value in values]
    for end in range(2):
        keep = side if end == 0 else ~side
        for c in range(4):
            ref[at + end * 5 + c] = jnp.where(keep, values[c], after[c])
        ref[at + end * 5 + 4] = jnp.where(keep, values[3], 0.0)


def pair_sources(ref, base, z, lz, at, own):
    end = 0 if z == 0 else 1
    for n in range(0, len(at), 2):
        row = pl.ds(at[n], 1)
        source = [ref[base + end * 5 + c, row, :] for c in range(3)]
        yield source, ref[base + end * 5 + (3 if n + 1 < len(at) else 4), row, :], own in (at[n], at[n] + 1)


def edge_kernel(t_hbm, after_ref, offs_ref, q_ref, out_ref, w_ref, win_ref, t_ref, rows_ref, sems):
    chunks = sems.shape[0]
    cut = t_ref.shape[1] // chunks
    copies = [
        pltpu.make_async_copy(
            t_hbm.at[:, pl.ds(n * cut, cut)], t_ref.at[:, pl.ds(n * cut, cut)], sems.at[n]
        )
        for n in range(chunks)
    ]
    for copy in copies:
        copy.start()
    _, lx, ly, lanes = offs_ref.shape
    lz = lanes // BODIES
    spot = lax.broadcasted_iota(jnp.int32, (ly, lanes), 1) // BODIES
    lead = lax.broadcasted_iota(jnp.int32, (ly, lanes), 0)
    for x in range(lx):
        at = pl.ds(x * ly, ly)
        shift = [float(x), lead.astype(F32), spot.astype(F32)]
        for c in range(3):
            win_ref[c, at, :] = offs_ref[c, x] + shift[c]
        for z, value in enumerate(spans(q_ref[x], spot, lz)):
            win_ref[3 + z, at, :] = value
    for n, x in enumerate((0, lx - 1)):
        turned = turn(offs_ref, x)
        for y in range(ly):

            def rows(z):
                for xx in range(max(x - 1, 0), min(x + 2, lx)):
                    for yy in range(max(y - 1, 0), min(y + 2, ly)):
                        yield row_source(win_ref, pl.ds(xx * ly + yy, 1), z, xx == x and yy == y)

            gather(out_ref, n, y, turned, lz, rows)
    relay(t_ref, copies, w_ref, rows_ref)


def strips(r_ref, win_ref, wide, lz):
    _, rows, lanes = r_ref.shape
    place = lax.broadcasted_iota(jnp.int32, (rows, lanes), 0)
    spot = lax.broadcasted_iota(jnp.int32, (rows, lanes), 1) // BODIES
    base = [place // wide, place % wide - 1, spot]
    for c in range(3):
        win_ref[c] = r_ref[c] + base[c].astype(F32)
    for z, value in enumerate(spans(r_ref[3], spot, lz)):
        win_ref[3 + z] = value
    win_ref[3 + lz] = r_ref[3]
    lay_pairs(win_ref, 4 + lz, rows)


def inner_kernel(offs_ref, r_ref, near_ref, out_ref, win_ref):
    _, lx, ly, lanes = offs_ref.shape
    lz = lanes // BODIES
    wide = ly + 2
    strips(r_ref, win_ref, wide, lz)
    for x in range(lx):
        outer = x in (0, lx - 1)
        turned = turn(offs_ref, x)
        for y in range(ly):
            halo = [yy for yy in (y, y + 2) if yy in (0, ly + 1)]

            def rows(z):
                for xx in range(max(x - 1, 0), min(x + 2, lx)):
                    at = [xx * wide + yy for yy in (halo if outer else range(y, y + 3))]
                    if z in (0, lz - 1):
                        yield from pair_sources(win_ref, 4 + lz, z, lz, at, x * wide + y + 1)
                    else:
                        for row in at:
                            yield row_source(win_ref, pl.ds(row, 1), z, row == x * wide + y + 1)

            start = near_ref[0 if x == 0 else 1, pl.ds(y, 1), :] if outer else 0.0
            if outer and not halo:
                out_ref[x, pl.ds(y, 1), :] = start
            else:
                gather(out_ref, x, y, turned, lz, rows, start)


def ends_kernel(offs_ref, zl_ref, zh_ref, near_ref, out_ref, end_ref):
    _, lx, ly, lanes = offs_ref.shape
    lz = lanes // BODIES
    half = ly // 2
    end_windows(zl_ref, -1.0, end_ref, 0, lz, half)
    end_windows(zh_ref, float(lz), end_ref, 5, lz, half)
    for x in range(lx):
        turned = turn(offs_ref, x)
        for y in range(ly):

            def rows(z):
                nearby = range(max(x - 1, 0), min(x + 2, lx))
                for end in range(2):
                    if z == (0 if end == 0 else lz - 1):
                        for xx in nearby:
                            at = pl.ds(y // 2 * lx + xx, 1)
                            source = [end_ref[end * 5 + c, at, :] for c in range(3)]
                            yield source, end_ref[end * 5 + 3 + y % 2, at, :], False

            gather(out_ref, x, y, turned, lz, rows, near_ref[x, pl.ds(y, 1), :])


def end_windows(end_ref, base, win_ref, at, lz, half):
    rows = end_ref.shape[1]
    lanes = end_ref.shape[2]
    count = rows // half
    place = lax.broadcasted_iota(jnp.int32, (rows, lanes), 0)
    spot = lax.broadcasted_iota(jnp.int32, (rows, lanes), 1) // BODIES
    shift = [(place % count).astype(F32), (spot + 2 * (place // count) - 1).astype(F32), base]
    for c in range(3):
        win_ref[at + c] = end_ref[c] + shift[c]
    for s in range(2):
        win_ref[at + 3 + s] = jnp.where((spot >= s) & (spot < s + 3), end_ref[3], 0.0)


def final_kernel(count, offs_ref, e_ref, near_ref, w_ref, dinv_ref, g_ref, *rest):
    received, rest = rest[:count], rest[count:]
    out_ref, left_ref, acc_ref, sum_ref, side_ref, edge_ref = rest
    _, lx, ly, lanes = offs_ref.shape
    lz = lanes // BODIES
    points = dinv_ref.shape[0]
    half = ly // 2
    pairs = half + 2
    wide = ly + 2
    deep = lz + 4
    block = half * deep
    above, below = get(received, "gx")

    def plane(x, pair):
        if x < 2:
            return below[(x * pairs + pair) * deep : (x * pairs + pair + 1) * deep]
        if x < lx + 2:
            return e_ref[(x - 2) * pairs + pair]
        return above[((x - lx - 2) * pairs + pair) * deep : ((x - lx - 2) * pairs + pair + 1) * deep]

    side = lax.broadcasted_iota(jnp.int32, (deep, 128), 1) < points
    for x in range(lx + 4):
        planes = [plane(x, pair) for pair in range(pairs)]
        turned = [pltpu.roll(value, points, 1) for value in planes]
        at = pl.ds(x * block, block)
        for j in range(SPAN // 2 + 1):
            early, late = [], []
            for p in range(half):
                before = turned[p + j - 1] if j else 0.0
                after = turned[p + j] if j < SPAN // 2 else 0.0
                early.append(jnp.where(side, before, after))
                late.append(planes[p + j] if j < SPAN // 2 else jnp.zeros((deep, 128), F32))
            left_ref[0, at, j * 128 : (j + 1) * 128] = jnp.concatenate(early, axis=0).astype(BF16)
            left_ref[1, at, j * 128 : (j + 1) * 128] = jnp.concatenate(late, axis=0).astype(BF16)
    spot = lax.broadcasted_iota(jnp.int32, (wide, lanes), 1) // BODIES
    lead = lax.broadcasted_iota(jnp.int32, (wide, lanes), 0).astype(F32) - 1.0
    base = 2 * pairs * deep
    ends = base + 4 * wide
    for side, value in enumerate((below, above)):
        shift = [-1.0 if side == 0 else float(lx), lead, spot.astype(F32)]
        for c in range(3):
            side_ref[side, c] = value[base + c * wide : base + (c + 1) * wide] + shift[c]
        for z, part in enumerate(spans(value[base + 3 * wide : base + 4 * wide], spot, lz)):
            side_ref[side, 3 + z] = part
        side_ref[side, 3 + lz] = value[base + 3 * wide : base + 4 * wide]
        lay_pairs(side_ref.at[side], 4 + lz, wide)
    spot = lax.broadcasted_iota(jnp.int32, (half, lanes), 1) // BODIES
    place = lax.broadcasted_iota(jnp.int32, (half, lanes), 0)
    for side, value in enumerate((below, above)):
        for end in range(2):
            shift = [-1.0 if side == 0 else float(lx), (spot + 2 * place - 1).astype(F32), -1.0 if end == 0 else float(lz)]
            for c in range(3):
                at = ends + (end * 4 + c) * half
                edge_ref[side, end * 5 + c] = value[at : at + half] + shift[c]
            at = ends + (end * 4 + 3) * half
            for s in range(2):
                edge_ref[side, end * 5 + 3 + s] = jnp.where((spot >= s) & (spot < s + 3), value[at : at + half], 0.0)


    def side_unit(x, y, turned):
        side = 0 if x == 0 else 1

        def rows(z):
            if z in (0, lz - 1):
                yield from pair_sources(side_ref.at[side], 4 + lz, z, lz, [y, y + 1, y + 2], None)
            else:
                for dy in range(3):
                    at = pl.ds(y + dy, 1)
                    yield [side_ref[side, c, at, :] for c in range(3)], side_ref[side, 3 + z, at, :], False
            for end in range(2):
                if z == (0 if end == 0 else lz - 1):
                    at = pl.ds(y // 2, 1)
                    source = [edge_ref[side, end * 5 + c, at, :] for c in range(3)]
                    yield source, edge_ref[side, end * 5 + 3 + y % 2, at, :], False

        gather(out_ref, x, y, turned, lz, rows, near_ref[x, pl.ds(y, 1), :])

    def units():
        for x in (0, lx - 1):
            turned = turn(offs_ref, x)
            for y in range(ly):
                side_unit(x, y, turned)
                yield

    waiting = units()
    high, low = split(jnp.concatenate([dinv_ref[...].T] * 2, axis=1))
    turned_inverse = jnp.concatenate([high, low, high], axis=1)
    boxes = lx * half * lz
    shape = (2 * boxes, lx * half * lanes)
    expand = (
        lax.broadcasted_iota(jnp.int32, shape, 1) // BODIES == lax.broadcasted_iota(jnp.int32, shape, 0) % boxes
    ).astype(BF16)
    lane = lax.broadcasted_iota(jnp.int32, (lz, 128), 1)
    level = lax.broadcasted_iota(jnp.int32, (lz, 128), 0)
    totals = {}
    for ox in range(-REACH, REACH + 1):
        chosen = [b for b in range(lx) if not (ox == -REACH and b % 2 == 0) and not (ox == REACH and b % 2 == 1)]
        wanted = [(cy, b) for cy in range(2) for b in chosen]
        parts = [left_ref[cy, pl.ds((b + ox + 2) * block, block), : SPAN * points] for cy, b in wanted]
        got = jnp.dot(jnp.concatenate(parts, axis=0), w_ref[ox + REACH], preferred_element_type=F32)
        for n, key in enumerate(wanted):
            piece = got[n * block : (n + 1) * block]
            totals[key] = totals[key] + piece if key in totals else piece
        next(waiting, None)
    for cy in range(2):
        for b in range(lx):
            for p in range(half):
                acc_ref[cy, b * half + p, pl.ds(8, deep), :] = totals[cy, b][p * deep : (p + 1) * deep]
        for g in range(lx * half):
            folded = None
            for k in range((SPAN + 1) // 2):
                shown = []
                for oz in (2 * k - REACH, 2 * k + 1 - REACH):
                    if oz > REACH:
                        shown.append(jnp.zeros((lz, 128), F32))
                        continue
                    got = acc_ref[cy, g, pl.ds(8 + oz + 2, lz), k * 128 : (k + 1) * 128]
                    if oz == -REACH:
                        got = jnp.where(level % 2 == 1, got, 0.0)
                    if oz == REACH:
                        got = jnp.where(level % 2 == 0, got, 0.0)
                    shown.append(got)
                both = jnp.where(lane < points, shown[0], shown[1])
                folded = both if folded is None else folded + both
            sum_ref[pl.ds((cy * lx * half + g) * lz, lz), :] = folded
    for _ in waiting:
        pass
    high, low = split(sum_ref[...])
    dense = lax.dot_general(
        turned_inverse, jnp.concatenate([high, high, low], axis=1), NT, preferred_element_type=F32
    )
    parts = split(dense)
    parts = [
        jnp.concatenate([part[:, cy * boxes : (cy + 1) * boxes] for part in parts], axis=1) for cy in range(2)
    ]
    dense = jnp.dot(jnp.concatenate(parts, axis=0), expand, preferred_element_type=F32)
    for x in range(lx):
        for y in range(ly):
            g = x * half + y // 2
            part = dense[y % 2 * points : (y % 2 + 1) * points, g * lanes : (g + 1) * lanes]
            far = jnp.sum(g_ref[x * ly + y] * part, axis=0, keepdims=True)
            at = pl.ds(y, 1)
            start = out_ref[x, at, :] if x in (0, lx - 1) else near_ref[x, at, :]
            out_ref[x, at, :] = start + far


def rounds_of(axis):
    return [[(i, i + 1) for i in range(start, lax.axis_size(axis) - 1, 2)] for start in range(2)]


def rounds_in(axis):
    return max(1, sum(1 for pairs in rounds_of(axis) if pairs))


def exchange(packets, axis):
    count = lax.axis_size(axis)
    planes = lax.axis_size("gx")
    results = []
    for packet, pairs in zip(packets, rounds_of(axis)):
        swaps = [swap for i, j in pairs for swap in ((i, j), (j, i))]
        idle = sorted(set(range(count)) - {i for i, _ in swaps})
        if not idle or axis == "gx" or planes % 2:
            results.append(lax.ppermute(packet, axis, swaps))
            continue
        swaps = [(plane * count + i, plane * count + j) for plane in range(planes) for i, j in swaps]
        swaps += [(plane * count + i, (plane ^ 1) * count + i) for plane in range(planes) for i in idle]
        results.append(lax.ppermute(packet, ("gx", axis), swaps))
    return results


def call(kernel, outs, args, scratch=(), limit=8, name=None, spaces=None):
    spec = pl.BlockSpec(memory_space=pltpu.VMEM)
    return pl.pallas_call(
        kernel,
        out_shape=outs,
        in_specs=[pl.BlockSpec(memory_space=space) for space in spaces] if spaces else [spec] * len(args),
        out_specs=[spec] * len(outs),
        scratch_shapes=list(scratch),
        compiler_params=pltpu.CompilerParams(vmem_limit_bytes=limit << 20),
        name=name,
    )(*args)


def shaped(*shape):
    return jax.ShapeDtypeStruct(shape, F32)


def per_device(offsets, charges, up_inverse, translations, down_inverse):
    points = up_inverse.shape[0]
    _, lx, ly, lanes = offsets.shape
    lz = lanes // BODIES
    half = ly // 2
    pairs = half + 2
    wide = ly + 2
    deep = lz + 4
    rounds = {axis: rounds_in(axis) for axis in ("gx", "gy", "gz")}
    sphere = jnp.asarray(surface(points))
    boxes = lx * half * lz
    packet = shaped(lx * lz + 4 * lx, lanes)
    inputs = [
        pltpu.with_memory_space_constraint(value, pltpu.HBM)
        for value in (offsets, charges, sphere, up_inverse, down_inverse)
    ]
    offsets, charges, down_inverse, surfaces, density, *packets = call(
        upward_kernel,
        [shaped(*value.shape) for value in (offsets, charges, down_inverse)]
        + [shaped(lx * ly, points, lanes), shaped(boxes, 2 * points)]
        + [packet] * rounds["gy"],
        inputs,
        [
            pltpu.VMEM(sphere.shape, F32),
            pltpu.VMEM(up_inverse.shape, F32),
            pltpu.VMEM((2 * points, 2 * points), F32),
            pltpu.SemaphoreType.DMA((5,)),
        ],
        4,
        "upward",
        [pltpu.HBM] * 5,
    )
    received = exchange(packets, "gy")
    count, width = translations.shape
    stride = count // 2 * 2 + 1
    edge, weights = call(
        edge_kernel,
        [
            shaped(2, ly, lanes),
            jax.ShapeDtypeStruct((SPAN, SPAN * points, (SPAN + 1) * points), BF16),
        ],
        (pltpu.with_memory_space_constraint(translations, pltpu.HBM), density, offsets, charges),
        [
            pltpu.VMEM((3 + lz, lx * ly, lanes), F32),
            pltpu.VMEM(translations.shape, BF16),
            pltpu.VMEM((width // 128 * stride, 128), F32),
            pltpu.SemaphoreType.DMA((4,)),
        ],
        24,
        "near_edge",
        [pltpu.HBM, pl.ANY, pltpu.VMEM, pltpu.VMEM],
    )
    received, edge, weights = lax.optimization_barrier((received, edge, weights))
    packet = shaped(lx * pairs * 2 + 4 * half * lx, lanes)
    dense, body, *packets = call(
        functools.partial(zpack_kernel, len(received)),
        [shaped(lx * pairs * lz, 2 * points), shaped(4, lx * wide, lanes)] + [packet] * rounds["gz"],
        (offsets, charges, density, *received),
        name="zpack",
    )
    packets, body = lax.optimization_barrier((packets, body))
    received = exchange(packets, "gz")
    windows = [pltpu.VMEM((14 + lz, lx * wide, lanes), F32)]
    (inner,) = call(inner_kernel, [shaped(lx, ly, lanes)], (offsets, body, edge), windows, name="near_inner")
    received, inner = lax.optimization_barrier((received, inner))
    packet = shaped(2 * pairs * deep + 4 * wide + 8 * half, lanes)
    end = shaped(4, half * lx, lanes)
    dense, low, high, *packets = call(
        functools.partial(xpack_kernel, len(received)),
        [shaped(lx * pairs, deep, 2 * points), end, end] + [packet] * rounds["gx"],
        (dense, body, *received),
        name="xpack",
    )
    packets, body = lax.optimization_barrier((packets, body))
    received = exchange(packets, "gx")
    (ends,) = call(
        ends_kernel,
        [shaped(lx, ly, lanes)],
        (offsets, low, high, inner),
        [pltpu.VMEM((10, half * lx, lanes), F32)],
        name="near_ends",
    )
    received, ends = lax.optimization_barrier((received, ends))
    (out,) = call(
        functools.partial(final_kernel, len(received)),
        [shaped(lx, ly, lanes)],
        (offsets, dense, ends, weights, down_inverse, surfaces, *received),
        [
            pltpu.VMEM((2, (lx + 4) * half * deep, (SPAN + 1) * points), BF16),
            pltpu.VMEM((2, lx * half, 8 + deep + 8, (SPAN + 1) * points), F32),
            pltpu.VMEM((2 * boxes, 2 * points), F32),
            pltpu.VMEM((2, 14 + lz, wide, lanes), F32),
            pltpu.VMEM((2, 10, half, lanes), F32),
        ],
        24,
        "final",
    )
    return out


def solution(mesh):
    in_specs = (P(None, "gx", "gy", "gz"), P("gx", "gy", "gz"), P(), P(), P())
    out_specs = P("gx", "gy", "gz")
    return jax.shard_map(
        per_device, mesh=mesh, in_specs=in_specs, out_specs=out_specs, check_vma=False
    )
```

```python
import functools
import math

import jax
import jax.numpy as jnp
import numpy as np
from jax import lax
from jax.experimental import pallas as pl
from jax.experimental.pallas import tpu as pltpu
from jax.sharding import PartitionSpec as P

BODIES = 32
RADIUS = 0.9
REACH = 3
SPAN = 2 * REACH + 1
F32 = jnp.float32
BF16 = jnp.bfloat16
NT = (((1,), (1,)), ((), ()))


def surface(points):
    number = np.arange(points).astype(np.float32)
    height = np.float32(1.0) - (np.float32(2.0) * number + np.float32(1.0)) / np.float32(points)
    across = np.sqrt(np.float32(1.0) - height * height)
    turned = number * np.float32(math.pi * (3.0 - math.sqrt(5.0)))
    columns = np.zeros((points, 128), np.float32)
    columns[:, 0] = RADIUS * across * np.cos(turned)
    columns[:, 1] = RADIUS * across * np.sin(turned)
    columns[:, 2] = RADIUS * height
    return columns


def numbering():
    table, count = {}, 0
    for ox in range(-REACH, REACH + 1):
        for oy in range(-REACH, REACH + 1):
            for oz in range(-REACH, REACH + 1):
                if max(abs(ox), abs(oy), abs(oz)) >= 2:
                    table[ox, oy, oz] = count
                    count += 1
    return table


def split(value):
    high = value.astype(BF16)
    return high, (value - high.astype(F32)).astype(BF16)


def surface_green(sphere, offs_ref, x, y):
    rows = [offs_ref[c, x, pl.ds(y, 1), :] - 0.5 for c in range(3)]
    square = None
    for c in range(3):
        delta = sphere[:, c : c + 1] - rows[c]
        square = delta * delta if square is None else square + delta * delta
    return lax.rsqrt(square)


def select(even, one, two):
    return jnp.where(even, one, two), jnp.where(even, two, one)


def put(refs, at, even, low, high):
    refs[0][at, :] = jnp.where(even, high, low)
    for ref in refs[1:]:
        ref[at, :] = jnp.where(even, low, high)


def get(refs, axis):
    index = lax.axis_index(axis)
    one = refs[0][...]
    above, below = select(index % 2 == 0, one, refs[1][...] if len(refs) > 1 else one)
    return jnp.where(index == lax.axis_size(axis) - 1, 0.0, above), jnp.where(index == 0, 0.0, below)


def upward_kernel(
    offs_hbm, q_hbm, sphere_hbm, uinv_hbm, dinv_hbm, offs_ref, q_ref, dinv_ref, g_ref, u_ref, *rest
):
    *packets, sphere_ref, uinv_ref, wide_ref, sems = rest
    copies = [
        pltpu.make_async_copy(source, target, sems.at[n])
        for n, (source, target) in enumerate(
            (
                (offs_hbm, offs_ref),
                (q_hbm, q_ref),
                (sphere_hbm, sphere_ref),
                (uinv_hbm, uinv_ref),
                (dinv_hbm, dinv_ref),
            )
        )
    ]
    for copy in copies:
        copy.start()
    _, lx, ly, lanes = offs_ref.shape
    lz = lanes // BODIES
    half = ly // 2
    points = uinv_ref.shape[0]
    even = lax.axis_index("gy") % 2 == 0
    offset = lax.broadcasted_iota(jnp.int32, (lanes, 2 * points), 1)
    offset = offset - lax.broadcasted_iota(jnp.int32, (lanes, 2 * points), 0) // BODIES
    wide_ref[...] = jnp.zeros_like(wide_ref)
    column = lax.broadcasted_iota(jnp.int32, (2 * points, 2 * points), 1)
    within = column % points
    wanted = column - within + jnp.where(within < points // 2, 2 * within, 2 * within - points + 1)
    shuffle = (lax.broadcasted_iota(jnp.int32, (2 * points, 2 * points), 0) == wanted).astype(BF16)
    for copy in copies[:3]:
        copy.wait()
    check = None
    sphere = sphere_ref[...]
    for c in range(4):
        for x in range(lx):
            low, high = [
                offs_ref[c, x, pl.ds(y, 1), :] if c < 3 else q_ref[x, pl.ds(y, 1), :] for y in (0, ly - 1)
            ]
            put(packets, pl.ds(lx * lz + c * lx + x, 1), even, low, high)
    for x in range(lx):
        for pair in range(half):
            parts = []
            for y in (2 * pair, 2 * pair + 1):
                kernel = surface_green(sphere, offs_ref, x, y)
                g_ref[x * ly + y] = kernel
                parts.append(kernel * q_ref[x, pl.ds(y, 1), :])
            part = (offset == (x * half + pair) * lz).astype(BF16)
            part = jnp.dot(
                jnp.concatenate(split(jnp.concatenate(parts, axis=0)), axis=1),
                jnp.concatenate([part, part], axis=0),
                preferred_element_type=F32,
            )
            check = part if check is None else check + part
    copies[3].wait()
    wide_ref[:points, :points] = uinv_ref[...]
    wide_ref[points:, points:] = uinv_ref[...]
    inverse = [jnp.dot(part, shuffle, preferred_element_type=F32).astype(BF16) for part in split(wide_ref[...])]
    high, low = split(check.T[: u_ref.shape[0]])
    density = jnp.dot(
        jnp.concatenate([high, high, low], axis=1),
        jnp.concatenate(inverse + inverse[:1], axis=0),
        preferred_element_type=F32,
    )
    u_ref[...] = density.astype(BF16).astype(F32)
    for x in range(lx):
        low = u_ref[pl.ds(x * half * lz, lz), :]
        high = u_ref[pl.ds((x * half + half - 1) * lz, lz), :]
        put(packets, pl.ds(x * lz, lz), even, low, high)
    copies[4].wait()


def relay(t_ref, copies, w_ref, rows_ref):
    count, width = t_ref.shape
    groups = width // 128
    stride = rows_ref.shape[0] // groups
    points = math.isqrt(width)
    half = points // 2
    order = numbering()
    for a in range(groups):
        if a % (groups // len(copies)) == 0:
            copies[a // (groups // len(copies))].wait()
        rows_ref[pl.ds(a * stride, count), :] = t_ref[:, a * 128 : (a + 1) * 128].astype(F32)
    left = lax.broadcasted_iota(jnp.int32, (groups, 128), 1) < points
    zero = jnp.zeros((groups, 128), F32)
    for ox in range(SPAN):
        for oy in range(SPAN):
            for k in range((SPAN + 1) // 2):
                loaded = []
                for oz in (2 * k, 2 * k + 1):
                    at = order.get((ox - REACH, oy - REACH, oz - REACH))
                    loaded.append(zero if at is None else rows_ref[pl.ds(at, groups, stride=stride), :])
                one, two = loaded
                even = jnp.where(left, one, pltpu.roll(two, points, 1))
                odd = jnp.where(left, pltpu.roll(one, points, 1), two)
                at = slice(k * 128, (k + 1) * 128)
                w_ref[ox, pl.ds(oy * points, half), at] = even.astype(BF16)
                w_ref[ox, pl.ds(oy * points + half, half), at] = odd.astype(BF16)


def zpack_kernel(count, offs_ref, q_ref, u_ref, *rest):
    received, (d_ref, r_ref, *packets) = rest[:count], rest[count:]
    _, lx, ly, lanes = offs_ref.shape
    lz = lanes // BODIES
    half = ly // 2
    wide = ly + 2
    above, below = get(received, "gy")
    even = lax.axis_index("gz") % 2 == 0
    for x in range(lx):
        at = x * (half + 2) * lz
        d_ref[pl.ds(at, lz), :] = below[x * lz : (x + 1) * lz]
        d_ref[pl.ds(at + lz, half * lz), :] = u_ref[pl.ds(x * half * lz, half * lz), :]
        d_ref[pl.ds(at + (half + 1) * lz, lz), :] = above[x * lz : (x + 1) * lz]
        for c in range(4):
            row = lx * lz + c * lx + x
            r_ref[c, pl.ds(x * wide, 1), :] = below[row : row + 1]
            r_ref[c, pl.ds(x * wide + 1, ly), :] = offs_ref[c, x] if c < 3 else q_ref[x]
            r_ref[c, pl.ds(x * wide + ly + 1, 1), :] = above[row : row + 1]
    for g in range(lx * (half + 2)):
        put(packets, pl.ds(g * 2, 2), even, d_ref[pl.ds(g * lz, 2), :], d_ref[pl.ds(g * lz + lz - 2, 2), :])
    spot = lax.broadcasted_iota(jnp.int32, (lx, lanes), 1) // BODIES
    base = lx * (half + 2) * 2
    for c in range(4):
        rows = [r_ref[c, pl.ds(j, lx, stride=wide), :] for j in range(wide)]
        for pack in range(half):
            low = high = None
            for j in range(4):
                row = rows[2 * pack + j]
                first = pltpu.roll(row, j * BODIES, 1) if j else row
                last = pltpu.roll(row, (j + 1) % 4 * BODIES, 1) if (j + 1) % 4 else row
                low = first if low is None else jnp.where(spot == j, first, low)
                high = last if high is None else jnp.where(spot == j, last, high)
            put(packets, pl.ds(base + (c * half + pack) * lx, lx), even, low, high)


def xpack_kernel(count, d_ref, r_ref, *rest):
    received, (e_ref, zl_ref, zh_ref, *packets) = rest[:count], rest[count:]
    groups = e_ref.shape[0]
    lx = zl_ref.shape[1] // 2
    pairs = groups // lx
    half = pairs - 2
    wide = 2 * half + 2
    lz = d_ref.shape[0] // groups
    above, below = get(received, "gz")
    even = lax.axis_index("gx") % 2 == 0
    for g in range(groups):
        e_ref[g, pl.ds(0, 2), :] = below[g * 2 : g * 2 + 2]
        e_ref[g, pl.ds(2, lz), :] = d_ref[pl.ds(g * lz, lz), :]
        e_ref[g, pl.ds(2 + lz, 2), :] = above[g * 2 : g * 2 + 2]
    base = groups * 2
    for c in range(4):
        zl_ref[c] = below[base + c * half * lx : base + (c + 1) * half * lx]
        zh_ref[c] = above[base + c * half * lx : base + (c + 1) * half * lx]
    deep = lz + 4
    for n in range(2 * pairs):
        put(packets, pl.ds(n * deep, deep), even, e_ref[n], e_ref[groups - 2 * pairs + n])
    base = 2 * pairs * deep
    for c in range(4):
        low, high = r_ref[c, pl.ds(0, wide), :], r_ref[c, pl.ds((lx - 1) * wide, wide), :]
        put(packets, pl.ds(base + c * wide, wide), even, low, high)
    base = base + 4 * wide
    for end, ref in enumerate((zl_ref, zh_ref)):
        for c in range(4):
            for pack in range(half):
                low, high = ref[c, pl.ds(pack * lx, 1), :], ref[c, pl.ds(pack * lx + lx - 1, 1), :]
                put(packets, pl.ds(base + (end * 4 + c) * half + pack, 1), even, low, high)


def turn(offs_ref, x):
    _, _, ly, lanes = offs_ref.shape
    lead = lax.broadcasted_iota(jnp.int32, (ly, lanes), 0).astype(F32)
    spots = (lax.broadcasted_iota(jnp.int32, (ly, lanes), 1) // BODIES).astype(F32)
    places = [offs_ref[0, x] + float(x), offs_ref[1, x] + lead, offs_ref[2, x] + spots]
    return jnp.concatenate(places + [places[0]], axis=0).T


def pick(turned, ly, y, z):
    return [turned[z * BODIES : (z + 1) * BODIES, c * ly + y : c * ly + y + 1] for c in range(3)]


def attract(total, target, source, weight, own=False):
    square = None
    for t, s in zip(target, source):
        delta = t - s
        square = delta * delta if square is None else square + delta * delta
    inverse = lax.rsqrt(square)
    if own:
        inverse = jnp.where(square > 0.0, inverse, 0.0)
    term = inverse * weight
    return term if total is None else total + term


def lane_sum(ones, parts):
    high, low = split(jnp.concatenate(parts, axis=0))
    out = lax.dot_general(ones, high, NT, preferred_element_type=F32)
    return (out + lax.dot_general(ones, low, NT, preferred_element_type=F32))[:1]


def spans(value, spot, lz):
    return [jnp.where((spot >= z - 1) & (spot <= z + 1), value, 0.0) for z in range(lz)]


def gather(out_ref, n, y, turned, lz, rows, start=0.0):
    _, ly, lanes = out_ref.shape
    ones = jnp.ones((8, lanes), BF16)
    parts = []
    for z in range(lz):
        target = pick(turned, ly, y, z)
        total = None
        for source, weight, own in rows(z):
            total = attract(total, target, source, weight, own)
        parts.append(jnp.zeros((BODIES, lanes), F32) if total is None else total)
    out_ref[n, pl.ds(y, 1), :] = start + lane_sum(ones, parts)


def row_source(ref, at, z, own=False):
    return [ref[c, at, :] for c in range(3)], ref[3 + z, at, :], own


def lay_pairs(ref, at, rows):
    lanes = ref.shape[2]
    side = lax.broadcasted_iota(jnp.int32, (rows, lanes), 1) < lanes // 2
    values = [ref[c] for c in range(3)] + [ref[at - 1]]
    after = [pltpu.roll(jnp.concatenate([value[1:], value[:1]], axis=0), lanes // 2, 1) for value in values]
    for end in range(2):
        keep = side if end == 0 else ~side
        for c in range(4):
            ref[at + end * 5 + c] = jnp.where(keep, values[c], after[c])
        ref[at + end * 5 + 4] = jnp.where(keep, values[3], 0.0)


def pair_sources(ref, base, z, lz, at, own):
    end = 0 if z == 0 else 1
    for n in range(0, len(at), 2):
        row = pl.ds(at[n], 1)
        source = [ref[base + end * 5 + c, row, :] for c in range(3)]
        yield source, ref[base + end * 5 + (3 if n + 1 < len(at) else 4), row, :], own in (at[n], at[n] + 1)


def edge_kernel(t_hbm, after_ref, offs_ref, q_ref, out_ref, w_ref, win_ref, t_ref, rows_ref, sems):
    chunks = sems.shape[0]
    cut = t_ref.shape[1] // chunks
    copies = [
        pltpu.make_async_copy(
            t_hbm.at[:, pl.ds(n * cut, cut)], t_ref.at[:, pl.ds(n * cut, cut)], sems.at[n]
        )
        for n in range(chunks)
    ]
    for copy in copies:
        copy.start()
    _, lx, ly, lanes = offs_ref.shape
    lz = lanes // BODIES
    spot = lax.broadcasted_iota(jnp.int32, (ly, lanes), 1) // BODIES
    lead = lax.broadcasted_iota(jnp.int32, (ly, lanes), 0)
    for x in range(lx):
        at = pl.ds(x * ly, ly)
        shift = [float(x), lead.astype(F32), spot.astype(F32)]
        for c in range(3):
            win_ref[c, at, :] = offs_ref[c, x] + shift[c]
        for z, value in enumerate(spans(q_ref[x], spot, lz)):
            win_ref[3 + z, at, :] = value
    for n, x in enumerate((0, lx - 1)):
        turned = turn(offs_ref, x)
        for y in range(ly):

            def rows(z):
                for xx in range(max(x - 1, 0), min(x + 2, lx)):
                    for yy in range(max(y - 1, 0), min(y + 2, ly)):
                        yield row_source(win_ref, pl.ds(xx * ly + yy, 1), z, xx == x and yy == y)

            gather(out_ref, n, y, turned, lz, rows)
    relay(t_ref, copies, w_ref, rows_ref)


def strips(r_ref, win_ref, wide, lz):
    _, rows, lanes = r_ref.shape
    place = lax.broadcasted_iota(jnp.int32, (rows, lanes), 0)
    spot = lax.broadcasted_iota(jnp.int32, (rows, lanes), 1) // BODIES
    base = [place // wide, place % wide - 1, spot]
    for c in range(3):
        win_ref[c] = r_ref[c] + base[c].astype(F32)
    for z, value in enumerate(spans(r_ref[3], spot, lz)):
        win_ref[3 + z] = value
    win_ref[3 + lz] = r_ref[3]
    lay_pairs(win_ref, 4 + lz, rows)


def inner_kernel(offs_ref, r_ref, near_ref, out_ref, win_ref):
    _, lx, ly, lanes = offs_ref.shape
    lz = lanes // BODIES
    wide = ly + 2
    strips(r_ref, win_ref, wide, lz)
    for x in range(lx):
        outer = x in (0, lx - 1)
        turned = turn(offs_ref, x)
        for y in range(ly):
            halo = [yy for yy in (y, y + 2) if yy in (0, ly + 1)]

            def rows(z):
                for xx in range(max(x - 1, 0), min(x + 2, lx)):
                    at = [xx * wide + yy for yy in (halo if outer else range(y, y + 3))]
                    if z in (0, lz - 1):
                        yield from pair_sources(win_ref, 4 + lz, z, lz, at, x * wide + y + 1)
                    else:
                        for row in at:
                            yield row_source(win_ref, pl.ds(row, 1), z, row == x * wide + y + 1)

            start = near_ref[0 if x == 0 else 1, pl.ds(y, 1), :] if outer else 0.0
            if outer and not halo:
                out_ref[x, pl.ds(y, 1), :] = start
            else:
                gather(out_ref, x, y, turned, lz, rows, start)


def ends_kernel(offs_ref, zl_ref, zh_ref, near_ref, out_ref, end_ref):
    _, lx, ly, lanes = offs_ref.shape
    lz = lanes // BODIES
    half = ly // 2
    end_windows(zl_ref, -1.0, end_ref, 0, lz, half)
    end_windows(zh_ref, float(lz), end_ref, 5, lz, half)
    for x in range(lx):
        turned = turn(offs_ref, x)
        for y in range(ly):

            def rows(z):
                nearby = range(max(x - 1, 0), min(x + 2, lx))
                for end in range(2):
                    if z == (0 if end == 0 else lz - 1):
                        for xx in nearby:
                            at = pl.ds(y // 2 * lx + xx, 1)
                            source = [end_ref[end * 5 + c, at, :] for c in range(3)]
                            yield source, end_ref[end * 5 + 3 + y % 2, at, :], False

            gather(out_ref, x, y, turned, lz, rows, near_ref[x, pl.ds(y, 1), :])


def end_windows(end_ref, base, win_ref, at, lz, half):
    rows = end_ref.shape[1]
    lanes = end_ref.shape[2]
    count = rows // half
    place = lax.broadcasted_iota(jnp.int32, (rows, lanes), 0)
    spot = lax.broadcasted_iota(jnp.int32, (rows, lanes), 1) // BODIES
    shift = [(place % count).astype(F32), (spot + 2 * (place // count) - 1).astype(F32), base]
    for c in range(3):
        win_ref[at + c] = end_ref[c] + shift[c]
    for s in range(2):
        win_ref[at + 3 + s] = jnp.where((spot >= s) & (spot < s + 3), end_ref[3], 0.0)


def final_kernel(count, offs_ref, e_ref, near_ref, w_ref, dinv_ref, g_ref, *rest):
    received, rest = rest[:count], rest[count:]
    out_ref, left_ref, acc_ref, sum_ref, side_ref, edge_ref = rest
    _, lx, ly, lanes = offs_ref.shape
    lz = lanes // BODIES
    points = dinv_ref.shape[0]
    half = ly // 2
    pairs = half + 2
    wide = ly + 2
    deep = lz + 4
    block = half * deep
    above, below = get(received, "gx")

    def plane(x, pair):
        if x < 2:
            return below[(x * pairs + pair) * deep : (x * pairs + pair + 1) * deep]
        if x < lx + 2:
            return e_ref[(x - 2) * pairs + pair]
        return above[((x - lx - 2) * pairs + pair) * deep : ((x - lx - 2) * pairs + pair + 1) * deep]

    side = lax.broadcasted_iota(jnp.int32, (deep, 128), 1) < points
    for x in range(lx + 4):
        planes = [plane(x, pair) for pair in range(pairs)]
        turned = [pltpu.roll(value, points, 1) for value in planes]
        at = pl.ds(x * block, block)
        for j in range(SPAN // 2 + 1):
            early, late = [], []
            for p in range(half):
                before = turned[p + j - 1] if j else 0.0
                after = turned[p + j] if j < SPAN // 2 else 0.0
                early.append(jnp.where(side, before, after))
                late.append(planes[p + j] if j < SPAN // 2 else jnp.zeros((deep, 128), F32))
            left_ref[0, at, j * 128 : (j + 1) * 128] = jnp.concatenate(early, axis=0).astype(BF16)
            left_ref[1, at, j * 128 : (j + 1) * 128] = jnp.concatenate(late, axis=0).astype(BF16)
    spot = lax.broadcasted_iota(jnp.int32, (wide, lanes), 1) // BODIES
    lead = lax.broadcasted_iota(jnp.int32, (wide, lanes), 0).astype(F32) - 1.0
    base = 2 * pairs * deep
    ends = base + 4 * wide
    for side, value in enumerate((below, above)):
        shift = [-1.0 if side == 0 else float(lx), lead, spot.astype(F32)]
        for c in range(3):
            side_ref[side, c] = value[base + c * wide : base + (c + 1) * wide] + shift[c]
        for z, part in enumerate(spans(value[base + 3 * wide : base + 4 * wide], spot, lz)):
            side_ref[side, 3 + z] = part
        side_ref[side, 3 + lz] = value[base + 3 * wide : base + 4 * wide]
        lay_pairs(side_ref.at[side], 4 + lz, wide)
    spot = lax.broadcasted_iota(jnp.int32, (half, lanes), 1) // BODIES
    place = lax.broadcasted_iota(jnp.int32, (half, lanes), 0)
    for side, value in enumerate((below, above)):
        for end in range(2):
            shift = [-1.0 if side == 0 else float(lx), (spot + 2 * place - 1).astype(F32), -1.0 if end == 0 else float(lz)]
            for c in range(3):
                at = ends + (end * 4 + c) * half
                edge_ref[side, end * 5 + c] = value[at : at + half] + shift[c]
            at = ends + (end * 4 + 3) * half
            for s in range(2):
                edge_ref[side, end * 5 + 3 + s] = jnp.where((spot >= s) & (spot < s + 3), value[at : at + half], 0.0)


    def side_unit(x, y, turned):
        side = 0 if x == 0 else 1

        def rows(z):
            if z in (0, lz - 1):
                yield from pair_sources(side_ref.at[side], 4 + lz, z, lz, [y, y + 1, y + 2], None)
            else:
                for dy in range(3):
                    at = pl.ds(y + dy, 1)
                    yield [side_ref[side, c, at, :] for c in range(3)], side_ref[side, 3 + z, at, :], False
            for end in range(2):
                if z == (0 if end == 0 else lz - 1):
                    at = pl.ds(y // 2, 1)
                    source = [edge_ref[side, end * 5 + c, at, :] for c in range(3)]
                    yield source, edge_ref[side, end * 5 + 3 + y % 2, at, :], False

        gather(out_ref, x, y, turned, lz, rows, near_ref[x, pl.ds(y, 1), :])

    def units():
        for x in (0, lx - 1):
            turned = turn(offs_ref, x)
            for y in range(ly):
                side_unit(x, y, turned)
                yield

    waiting = units()
    high, low = split(jnp.concatenate([dinv_ref[...].T] * 2, axis=1))
    turned_inverse = jnp.concatenate([high, low, high], axis=1)
    boxes = lx * half * lz
    shape = (2 * boxes, lx * half * lanes)
    expand = (
        lax.broadcasted_iota(jnp.int32, shape, 1) // BODIES == lax.broadcasted_iota(jnp.int32, shape, 0) % boxes
    ).astype(BF16)
    lane = lax.broadcasted_iota(jnp.int32, (lz, 128), 1)
    level = lax.broadcasted_iota(jnp.int32, (lz, 128), 0)
    totals = {}
    for ox in range(-REACH, REACH + 1):
        chosen = [b for b in range(lx) if not (ox == -REACH and b % 2 == 0) and not (ox == REACH and b % 2 == 1)]
        wanted = [(cy, b) for cy in range(2) for b in chosen]
        parts = [left_ref[cy, pl.ds((b + ox + 2) * block, block), : SPAN * points] for cy, b in wanted]
        got = jnp.dot(jnp.concatenate(parts, axis=0), w_ref[ox + REACH], preferred_element_type=F32)
        for n, key in enumerate(wanted):
            piece = got[n * block : (n + 1) * block]
            totals[key] = totals[key] + piece if key in totals else piece
        next(waiting, None)
    for cy in range(2):
        for b in range(lx):
            for p in range(half):
                acc_ref[cy, b * half + p, pl.ds(8, deep), :] = totals[cy, b][p * deep : (p + 1) * deep]
        for g in range(lx * half):
            folded = None
            for k in range((SPAN + 1) // 2):
                shown = []
                for oz in (2 * k - REACH, 2 * k + 1 - REACH):
                    if oz > REACH:
                        shown.append(jnp.zeros((lz, 128), F32))
                        continue
                    got = acc_ref[cy, g, pl.ds(8 + oz + 2, lz), k * 128 : (k + 1) * 128]
                    if oz == -REACH:
                        got = jnp.where(level % 2 == 1, got, 0.0)
                    if oz == REACH:
                        got = jnp.where(level % 2 == 0, got, 0.0)
                    shown.append(got)
                both = jnp.where(lane < points, shown[0], shown[1])
                folded = both if folded is None else folded + both
            sum_ref[pl.ds((cy * lx * half + g) * lz, lz), :] = folded
    for _ in waiting:
        pass
    high, low = split(sum_ref[...])
    dense = lax.dot_general(
        turned_inverse, jnp.concatenate([high, high, low], axis=1), NT, preferred_element_type=F32
    )
    parts = split(dense)
    parts = [
        jnp.concatenate([part[:, cy * boxes : (cy + 1) * boxes] for part in parts], axis=1) for cy in range(2)
    ]
    dense = jnp.dot(jnp.concatenate(parts, axis=0), expand, preferred_element_type=F32)
    for x in range(lx):
        for y in range(ly):
            g = x * half + y // 2
            part = dense[y % 2 * points : (y % 2 + 1) * points, g * lanes : (g + 1) * lanes]
            far = jnp.sum(g_ref[x * ly + y] * part, axis=0, keepdims=True)
            at = pl.ds(y, 1)
            start = out_ref[x, at, :] if x in (0, lx - 1) else near_ref[x, at, :]
            out_ref[x, at, :] = start + far


def rounds_of(axis):
    return [[(i, i + 1) for i in range(start, lax.axis_size(axis) - 1, 2)] for start in range(2)]


def rounds_in(axis):
    return max(1, sum(1 for pairs in rounds_of(axis) if pairs))


def exchange(packets, axis):
    count = lax.axis_size(axis)
    planes = lax.axis_size("gx")
    results = []
    for packet, pairs in zip(packets, rounds_of(axis)):
        swaps = [swap for i, j in pairs for swap in ((i, j), (j, i))]
        idle = sorted(set(range(count)) - {i for i, _ in swaps})
        if not idle or axis == "gx" or planes % 2:
            results.append(lax.ppermute(packet, axis, swaps))
            continue
        swaps = [(plane * count + i, plane * count + j) for plane in range(planes) for i, j in swaps]
        swaps += [(plane * count + i, (plane ^ 1) * count + i) for plane in range(planes) for i in idle]
        results.append(lax.ppermute(packet, ("gx", axis), swaps))
    return results


def call(kernel, outs, args, scratch=(), limit=8, name=None, spaces=None):
    spec = pl.BlockSpec(memory_space=pltpu.VMEM)
    return pl.pallas_call(
        kernel,
        out_shape=outs,
        in_specs=[pl.BlockSpec(memory_space=space) for space in spaces] if spaces else [spec] * len(args),
        out_specs=[spec] * len(outs),
        scratch_shapes=list(scratch),
        compiler_params=pltpu.CompilerParams(vmem_limit_bytes=limit << 20),
        name=name,
    )(*args)


def shaped(*shape):
    return jax.ShapeDtypeStruct(shape, F32)


def per_device(offsets, charges, up_inverse, translations, down_inverse):
    points = up_inverse.shape[0]
    _, lx, ly, lanes = offsets.shape
    lz = lanes // BODIES
    half = ly // 2
    pairs = half + 2
    wide = ly + 2
    deep = lz + 4
    rounds = {axis: rounds_in(axis) for axis in ("gx", "gy", "gz")}
    sphere = jnp.asarray(surface(points))
    boxes = lx * half * lz
    packet = shaped(lx * lz + 4 * lx, lanes)
    inputs = [
        pltpu.with_memory_space_constraint(value, pltpu.HBM)
        for value in (offsets, charges, sphere, up_inverse, down_inverse)
    ]
    offsets, charges, down_inverse, surfaces, density, *packets = call(
        upward_kernel,
        [shaped(*value.shape) for value in (offsets, charges, down_inverse)]
        + [shaped(lx * ly, points, lanes), shaped(boxes, 2 * points)]
        + [packet] * rounds["gy"],
        inputs,
        [
            pltpu.VMEM(sphere.shape, F32),
            pltpu.VMEM(up_inverse.shape, F32),
            pltpu.VMEM((2 * points, 2 * points), F32),
            pltpu.SemaphoreType.DMA((5,)),
        ],
        4,
        "upward",
        [pltpu.HBM] * 5,
    )
    received = exchange(packets, "gy")
    count, width = translations.shape
    stride = count // 2 * 2 + 1
    edge, weights = call(
        edge_kernel,
        [
            shaped(2, ly, lanes),
            jax.ShapeDtypeStruct((SPAN, SPAN * points, (SPAN + 1) * points), BF16),
        ],
        (pltpu.with_memory_space_constraint(translations, pltpu.HBM), density, offsets, charges),
        [
            pltpu.VMEM((3 + lz, lx * ly, lanes), F32),
            pltpu.VMEM(translations.shape, BF16),
            pltpu.VMEM((width // 128 * stride, 128), F32),
            pltpu.SemaphoreType.DMA((8,)),
        ],
        24,
        "near_edge",
        [pltpu.HBM, pl.ANY, pltpu.VMEM, pltpu.VMEM],
    )
    received, edge, weights = lax.optimization_barrier((received, edge, weights))
    packet = shaped(lx * pairs * 2 + 4 * half * lx, lanes)
    dense, body, *packets = call(
        functools.partial(zpack_kernel, len(received)),
        [shaped(lx * pairs * lz, 2 * points), shaped(4, lx * wide, lanes)] + [packet] * rounds["gz"],
        (offsets, charges, density, *received),
        name="zpack",
    )
    packets, body = lax.optimization_barrier((packets, body))
    received = exchange(packets, "gz")
    windows = [pltpu.VMEM((14 + lz, lx * wide, lanes), F32)]
    (inner,) = call(inner_kernel, [shaped(lx, ly, lanes)], (offsets, body, edge), windows, name="near_inner")
    received, inner = lax.optimization_barrier((received, inner))
    packet = shaped(2 * pairs * deep + 4 * wide + 8 * half, lanes)
    end = shaped(4, half * lx, lanes)
    dense, low, high, *packets = call(
        functools.partial(xpack_kernel, len(received)),
        [shaped(lx * pairs, deep, 2 * points), end, end] + [packet] * rounds["gx"],
        (dense, body, *received),
        name="xpack",
    )
    packets, body = lax.optimization_barrier((packets, body))
    received = exchange(packets, "gx")
    (ends,) = call(
        ends_kernel,
        [shaped(lx, ly, lanes)],
        (offsets, low, high, inner),
        [pltpu.VMEM((10, half * lx, lanes), F32)],
        name="near_ends",
    )
    received, ends = lax.optimization_barrier((received, ends))
    (out,) = call(
        functools.partial(final_kernel, len(received)),
        [shaped(lx, ly, lanes)],
        (offsets, dense, ends, weights, down_inverse, surfaces, *received),
        [
            pltpu.VMEM((2, (lx + 4) * half * deep, (SPAN + 1) * points), BF16),
            pltpu.VMEM((2, lx * half, 8 + deep + 8, (SPAN + 1) * points), F32),
            pltpu.VMEM((2 * boxes, 2 * points), F32),
            pltpu.VMEM((2, 14 + lz, wide, lanes), F32),
            pltpu.VMEM((2, 10, half, lanes), F32),
        ],
        24,
        "final",
    )
    return out


def solution(mesh):
    in_specs = (P(None, "gx", "gy", "gz"), P("gx", "gy", "gz"), P(), P(), P())
    out_specs = P("gx", "gy", "gz")
    return jax.shard_map(
        per_device, mesh=mesh, in_specs=in_specs, out_specs=out_specs, check_vma=False
    )
```
